512 devices in a mesh: rows: 128 (over z, y, core), sub: 4 (over x).
Axes of the slice: x: 4, y: 4, z: 16, core: 2. Of those that a mesh axis runs over, the one named last changes fastest.
Arguments:
- factor_a: float32 [131072, 256], P(('rows', 'sub')), may hold values from -6 to 6
- factor_b: float32 [131072, 256], P(('rows', 'sub')), may hold values from -0.0009765625 to 0.0009765625
- value_diffs: float32 [131072, 32], P(('rows', 'sub')), may hold values from -6 to 6
- residual_diffs: float32 [131072, 32], P(('rows', 'sub')), may hold values from -6 to 6
- residual: float32 [131072], P(('rows', 'sub')), may hold values from -6 to 6
Outputs:
- update: float32 [131072], P(('rows', 'sub'))
- new_a: float32 [131072, 256], P(('rows', 'sub'))
- new_b: float32 [131072, 256], P(('rows', 'sub'))
The draws below stay inside these ranges and needn't reach their ends.
All inputs are finite; a program needn't handle non-finite values.
Results may differ from the reference program's by a relative error of at most 0.0003.
Values sent between devices are 32-bit elements; how exact they have to be, the bound alone decides.
A program may use at most 64 MiB of HBM per device.

```python
import jax
import jax.numpy as jnp
from jax import lax

RANK = 256
COLS = 32
ROWS = 131072


def level_of(stream_key, shape, cuts, low, top_value):
    gain = 1.0
    for position, blocks in cuts:
        draws = jax.random.uniform(jax.random.fold_in(jax.random.fold_in(stream_key, 6), position), (blocks,), jnp.float32, low / len(cuts), top_value / len(cuts))
        gain = gain * jnp.repeat(jnp.exp(draws), shape[position] // blocks).reshape((-1,) + (1,) * (len(shape) - 1 - position))
    return gain


def gaussian(rng, shape, scale, limit, split=(), kind=jnp.bfloat16):
    drawn = scale * jax.random.normal(rng, shape, jnp.float32)
    if split:
        drawn = drawn * level_of(rng, shape, split, -0.22, 0.18)
    return jnp.clip(drawn, -limit, limit).astype(kind)


def setup_inputs(seed: int = 0) -> dict:
    seeds = jax.random.split(jax.random.key(seed), 6)
    factor_a = gaussian(seeds[0], (ROWS, RANK), 1.0, 6.0, ((0, 512),), jnp.float32)
    factor_b = gaussian(seeds[1], (ROWS, RANK), (ROWS * RANK) ** -0.5, 0.0009765625, ((0, 512),), jnp.float32)
    value_diffs = gaussian(seeds[2], (ROWS, COLS), 1.0, 6.0, ((0, 512),), jnp.float32)
    residual_diffs = gaussian(seeds[3], (ROWS, COLS), 1.0, 6.0, ((0, 512),), jnp.float32)
    residual = gaussian(seeds[4], (ROWS,), 1.0, 6.0, ((0, 512),), jnp.float32)
    return {"factor_a": factor_a, "factor_b": factor_b, "value_diffs": value_diffs, "residual_diffs": residual_diffs, "residual": residual}


def matmul(left, right):
    return jnp.dot(left.astype(jnp.float32), right.astype(jnp.float32), precision=lax.Precision.HIGHEST, preferred_element_type=jnp.float32)

def small_inverse(lower):
    extent = lower.shape[0]
    diag_inv = 1.0 / jnp.diagonal(lower)
    strict = jnp.tril(lower, -1) * diag_inv[:, None]
    ident = jnp.eye(extent, dtype=lower.dtype)
    result = ident - strict
    power = strict
    for level in range(3):
        power = matmul(power, power)
        result = matmul(result, ident + power)
    return result * diag_inv[None, :]

def lower_inverse(lower):
    extent = lower.shape[0]
    if extent <= 8:
        return small_inverse(lower)
    half = extent // 2
    upper_inv = lower_inverse(lower[:half, :half])
    tail_inv = lower_inverse(lower[half:, half:])
    corner = -matmul(tail_inv, matmul(lower[half:, :half], upper_inv))
    zeros = jnp.zeros((half, extent - half), lower.dtype)
    return jnp.concatenate([jnp.concatenate([upper_inv, zeros], axis=1), jnp.concatenate([corner, tail_inv], axis=1)], axis=0)

def tri_solve(matrix, rhs, lower):
    if lower:
        return matmul(lower_inverse(matrix), rhs)
    return matmul(lower_inverse(matrix.T).T, rhs)

def inverse_gram(gram_v):
    low_v = jnp.linalg.cholesky(gram_v)
    low_inv = lower_inverse(low_v)
    return matmul(low_inv.T, low_inv)

def truncate(gram_a, gram_b, width):
    low_a = jnp.linalg.cholesky(gram_a)
    low_b = jnp.linalg.cholesky(gram_b)
    core = matmul(low_a.T, low_b)
    start = matmul(core.T, core[:, :width])
    low_y = jnp.linalg.cholesky(matmul(start.T, start))
    basis = tri_solve(low_y, start.T, True).T
    return (matmul(low_b, basis), tri_solve(low_b.T, basis, False))

def reference(factor_a, factor_b, value_diffs, residual_diffs, residual):
    gram_v = matmul(residual_diffs.T, residual_diffs)
    proj = matmul(factor_b.T, residual_diffs)
    proj_r = matmul(factor_b.T, residual)
    gram_r = matmul(residual_diffs.T, residual)
    inv_v = inverse_gram(gram_v)
    coeffs = -matmul(inv_v, gram_r)
    fresh = value_diffs - matmul(factor_a, proj)
    scaled_v = matmul(residual_diffs, inv_v)
    update = -matmul(factor_a, proj_r) + matmul(fresh, coeffs)
    wide_a = jnp.concatenate([factor_a, fresh], axis=1)
    wide_b = jnp.concatenate([factor_b, scaled_v], axis=1)
    gram_a = matmul(wide_a.T, wide_a)
    gram_b = matmul(wide_b.T, wide_b)
    left_map, right_map = truncate(gram_a, gram_b, factor_a.shape[1])
    return (update, matmul(wide_a, left_map), matmul(wide_b, right_map))
```

```python
import functools

import jax
import jax.numpy as jnp
from jax import lax
from jax.experimental import pallas as pl
from jax.experimental.pallas import tpu as pltpu
from jax.sharding import PartitionSpec as P

MESH = pl.DeviceIdType.MESH
LANES = 128
PACK = 768
BLOCK = 32

NN = (((1,), (0,)), ((), ()))
NT = (((1,), (1,)), ((), ()))
TN = (((0,), (0,)), ((), ()))


def dot(left, right, dims=NN):
    return lax.dot_general(left, right, dims, precision=lax.Precision.HIGHEST, preferred_element_type=jnp.float32)


def pack_pair(gram, out_ref, base):
    row = lax.broadcasted_iota(jnp.int32, (LANES, LANES), 0)
    lane = lax.broadcasted_iota(jnp.int32, (LANES, LANES), 1)
    first, last = gram[:LANES, :LANES], gram[LANES:, LANES:]
    out_ref[base:base + LANES, :] = jnp.where(row >= lane, first, last)
    out_ref[base + LANES:base + 2 * LANES, :] = gram[LANES:, :LANES]
    return jnp.sum(jnp.where(row == lane, last, 0.0), axis=0, keepdims=True)


def unpack_pair(red_ref, base, diag):
    row = lax.broadcasted_iota(jnp.int32, (LANES, LANES), 0)
    lane = lax.broadcasted_iota(jnp.int32, (LANES, LANES), 1)
    both = red_ref[base:base + LANES, :]
    turned = both.T
    low = red_ref[base + LANES:base + 2 * LANES, :]
    first = jnp.where(row >= lane, both, turned)
    last = jnp.where(row < lane, both, jnp.where(row > lane, turned, diag))
    return jnp.concatenate(
        [jnp.concatenate([first, low.T], axis=1), jnp.concatenate([low, last], axis=1)], axis=0
    )


def reduce_kernel(sizes, a_ref, b_ref, v_ref, d_ref, r_ref, out_ref, local, pair, half, near, mine, far, total, full,
                  pair_sem, near_sem, far_sem, total_sem, back_sem, cross_sem,
                  pair_out, near_out, far_out, total_out, back_out, cross_out):
    nz, ny, nx = sizes
    peers = ny * nx
    rows = PACK // 2
    piece = rows // peers
    tiles = piece // 8
    place = lax.axis_index("rows")
    x = lax.axis_index("sub")
    core = lax.rem(place, 2)
    y = lax.rem(place // 2, ny)
    z = place // (2 * ny)
    me = y * nx + x
    near_ids = []
    for dy in range(ny):
        for dx in range(nx):
            if dy or dx:
                qy, qx = lax.rem(y + dy, ny), lax.rem(x + dx, nx)
                hops = min(dy, ny - dy) + min(dx, nx - dx)
                near_ids.append((hops, dy * nx + dx, qy * nx + qx, ((z * ny + qy) * 2 + core, qx)))
    near_ids = [item[2:] for item in sorted(near_ids, key=lambda item: (-item[0], item[1]))]
    far_ids = []
    for dz in sorted(range(1, nz), key=lambda d: -min(d, nz - d)):
        qz = lax.rem(z + dz, nz)
        far_ids.append((dz, qz, ((qz * ny + y) * 2 + core, x)))
    partner = (place + 1 - 2 * core, x)
    owners = [(t * nz) // tiles if nz >= tiles else t % nz for t in range(tiles)]

    barrier = pltpu.get_barrier_semaphore()
    for _, _, dev in far_ids:
        pl.semaphore_signal(barrier, inc=1, device_id=dev, device_id_type=MESH)
    for _, dev in near_ids:
        pl.semaphore_signal(barrier, inc=1, device_id=dev, device_id_type=MESH)
    pl.semaphore_signal(barrier, inc=1, device_id=partner, device_id_type=MESH)

    a, b = a_ref[...], b_ref[...]
    v, d = v_ref[...], d_ref[...]
    cols = v.shape[1]
    diag_a = pack_pair(dot(a, a, TN), local, 0)
    diag_b = pack_pair(dot(b, b, TN), local, 2 * LANES)
    va = dot(v, a, TN)
    left = jnp.concatenate([d.T, jnp.broadcast_to(r_ref[...], (8, d.shape[0]))], axis=0)
    db = dot(left, b)
    dd = dot(left, d)
    vv = dot(v, v, TN)
    local[512:512 + cols, :] = va[:, :LANES]
    local[512 + cols:576, :] = va[:, LANES:]
    local[576:616, :] = db[:, :LANES]
    local[616:656, :] = db[:, LANES:]
    local[656:696, :] = jnp.zeros((40, LANES), jnp.float32)
    local[656:656 + cols, 0:cols] = vv
    local[656:696, 64:64 + cols] = dd
    local[696:768, :] = jnp.zeros((72, LANES), jnp.float32)
    local[696:697, :] = diag_a
    local[697:698, :] = diag_b

    pl.semaphore_wait(barrier, len(far_ids) + len(near_ids) + 1)

    def send(src, dst, out_sem, in_sem, dev):
        copy = pltpu.make_async_remote_copy(
            src_ref=src, dst_ref=dst, send_sem=out_sem, recv_sem=in_sem, device_id=dev, device_id_type=MESH
        )
        copy.start()
        return copy

    def arrived(ref, sem):
        pltpu.make_async_copy(ref, ref, sem).wait()

    pending = []

    def ds(start, size):
        return pl.ds(pl.multiple_of(start, 8), size)

    pending.append(send(local.at[ds((1 - core) * rows, rows)], pair, pair_out, pair_sem, partner))
    arrived(pair, pair_sem)
    half[...] = local[ds(core * rows, rows), :] + pair[...]

    for k, (q, dev) in enumerate(near_ids):
        pending.append(send(half.at[ds(q * piece, piece)], near.at[me], near_out.at[k], near_sem.at[me], dev))
    value = half[ds(me * piece, piece), :]
    for q, _ in near_ids:
        arrived(near.at[q], near_sem.at[q])
        value = value + near[q]
    mine[...] = value

    for t, owner in enumerate(owners):
        tile = pl.ds(8 * t, 8)

        @pl.when(z != owner)
        def _():
            send(mine.at[tile], far.at[t, z], far_out.at[t], far_sem.at[t, z], ((owner * ny + y) * 2 + core, x))

    for t, owner in enumerate(owners):
        tile = pl.ds(8 * t, 8)

        @pl.when(z == owner)
        def _():
            value = mine[8 * t:8 * t + 8, :]
            for dz, qz, dev in far_ids:
                arrived(far.at[t, qz], far_sem.at[t, qz])
                value = value + far[t, qz]
            total[8 * t:8 * t + 8, :] = value
            for dz, qz, dev in far_ids:
                send(total.at[tile], total.at[tile], total_out.at[t, dz], total_sem.at[t], dev)

    for t, owner in enumerate(owners):
        tile = pl.ds(8 * t, 8)

        @pl.when(z != owner)
        def _():
            arrived(total.at[tile], total_sem.at[t])

    slot = core * peers
    for k, (q, dev) in enumerate(near_ids):
        pending.append(send(total, full.at[slot + me], back_out.at[k], back_sem.at[me], dev))
    pending.append(send(total, full.at[slot + me], cross_out.at[me], cross_sem.at[me], partner))
    full[slot + me] = total[...]
    for q, _ in reversed(near_ids):
        arrived(full.at[slot + q], back_sem.at[q])
        pending.append(send(full.at[slot + q], full.at[slot + q], cross_out.at[q], cross_sem.at[q], partner))
    other = (1 - core) * peers
    for q in range(peers):
        arrived(full.at[other + q], cross_sem.at[q])
    for q in range(2 * peers):
        out_ref[q * piece:(q + 1) * piece, :] = full[q]

    for copy in pending:
        copy.wait_send()
    for t, owner in enumerate(owners):
        tile = pl.ds(8 * t, 8)

        @pl.when(z != owner)
        def _():
            arrived(mine.at[tile], far_out.at[t])

        @pl.when(z == owner)
        def _():
            for dz, _, _ in far_ids:
                arrived(total.at[tile], total_out.at[t, dz])


def reduce_all(sizes, a, b, v, d, r):
    nz, ny, nx = sizes
    peers = ny * nx
    piece = PACK // 2 // peers
    tiles = piece // 8
    vmem = pl.BlockSpec(memory_space=pltpu.VMEM)
    dma = pltpu.SemaphoreType.DMA
    return pl.pallas_call(
        functools.partial(reduce_kernel, sizes),
        out_shape=jax.ShapeDtypeStruct((PACK, LANES), jnp.float32),
        in_specs=[vmem] * 5,
        out_specs=vmem,
        scratch_shapes=[
            pltpu.VMEM((PACK, LANES), jnp.float32),
            pltpu.VMEM((PACK // 2, LANES), jnp.float32),
            pltpu.VMEM((PACK // 2, LANES), jnp.float32),
            pltpu.VMEM((peers, piece, LANES), jnp.float32),
            pltpu.VMEM((piece, LANES), jnp.float32),
            pltpu.VMEM((tiles, nz, 8, LANES), jnp.float32),
            pltpu.VMEM((piece, LANES), jnp.float32),
            pltpu.VMEM((2 * peers, piece, LANES), jnp.float32),
            dma(()), dma((peers,)), dma((tiles, nz)), dma((tiles,)), dma((peers,)), dma((peers,)),
            dma(()), dma((peers,)), dma((tiles,)), dma((tiles, nz)), dma((peers,)), dma((peers,)),
        ],
        compiler_params=pltpu.CompilerParams(collective_id=0, has_side_effects=True, vmem_limit_bytes=32 << 20),
    )(a, b, v, d, r)


def eliminate(block):
    row = lax.broadcasted_iota(jnp.int32, (BLOCK, LANES), 0)
    for j in range(BLOCK):
        scale = lax.rsqrt(block[j:j + 1, j:j + 1])
        pivot = block[j:j + 1, :] * scale
        column = block[:, j:j + 1] * scale
        block = jnp.where(row > j, block - column * pivot, jnp.where(row == j, pivot, block))
    return pltpu.roll(block, LANES - BLOCK, 1)[:, :BLOCK]


def with_identity(block, offset):
    row = lax.broadcasted_iota(jnp.int32, (BLOCK, LANES), 0)
    lane = lax.broadcasted_iota(jnp.int32, (BLOCK, LANES), 1)
    if offset:
        block = pltpu.roll(block, LANES - offset, 1)
    return jnp.where(lane < BLOCK, block, jnp.where(lane == row + BLOCK, 1.0, 0.0))


def largest(values):
    return jnp.max(jnp.max(values, axis=1, keepdims=True), axis=0, keepdims=True)


def diagonal(matrix):
    row = lax.broadcasted_iota(jnp.int32, matrix.shape, 0)
    lane = lax.broadcasted_iota(jnp.int32, matrix.shape, 1)
    return jnp.where(row == lane, matrix, 0.0)


def chain_kernel(red_ref, a_ref, b_ref, v_ref, d_ref, up_ref, na_ref, nb_ref, aug):
    width = a_ref.shape[1]
    cols = v_ref.shape[1]
    small = red_ref[656:696, :]
    gram_v = pltpu.roll(small, 64, 1)
    lower_inv = eliminate(with_identity(gram_v[:cols, :], 0))
    inv_v = dot(lower_inv, lower_inv, TN)
    vv = small[:cols, :cols]
    gram_r = gram_v[cols:cols + 8, :cols]
    gram_a = unpack_pair(red_ref, 0, red_ref[696:697, :])
    gram_b = unpack_pair(red_ref, 256, red_ref[697:698, :])
    va = jnp.concatenate([red_ref[512:512 + cols, :], red_ref[512 + cols:576, :]], axis=1)
    db = jnp.concatenate([red_ref[576:616, :], red_ref[616:656, :]], axis=1)
    proj_t, proj_r = db[:cols, :], db[cols:cols + 8, :]
    scale_a = 1.0 / jnp.maximum(largest(diagonal(gram_a)), largest(diagonal(vv)))
    scale_b = 1.0 / largest(diagonal(gram_b))
    gram_a = gram_a * scale_a
    va = va * scale_a
    vv = vv * scale_a

    w = dot(inv_v, proj_t)
    s = (gram_b - dot(proj_t, w, TN)) * scale_b
    ws = w * scale_b
    k1 = dot(gram_a, s) + dot(va, ws, TN)
    k2 = dot(va, s) + dot(vv, ws)
    j1 = dot(s, k1)
    c = dot(inv_v, k2)
    cs = c * scale_b
    aug[:, :width] = dot(k1, j1, TN) + dot(k2, cs, TN)
    row = lax.broadcasted_iota(jnp.int32, (width, width), 0)
    lane = lax.broadcasted_iota(jnp.int32, (width, width), 1)
    aug[:, width:] = jnp.where(row == lane, 1.0, 0.0)

    a, b, v, d = a_ref[...], b_ref[...], v_ref[...], d_ref[...]
    coeffs = -dot(gram_r, inv_v)
    lead = -proj_r - dot(coeffs, proj_t)
    up = dot(lead, a, NT) + dot(coeffs, v, NT)
    up_ref[...] = up[:1, :]
    root = jnp.sqrt(scale_b)
    fa = (dot(a, j1) + dot(v, cs)) / root
    fb = (dot(b - dot(d, w), k1) + dot(d, c)) * root

    for k in range(width // BLOCK):
        lo, hi = k * BLOCK, (k + 1) * BLOCK
        tile = lo // LANES * LANES
        linv = eliminate(with_identity(aug[lo:hi, tile:tile + LANES], lo - tile))
        rows = dot(linv, aug[lo:hi, :])
        aug[lo:hi, :] = rows
        if hi < width:
            below = rows[:, :width].T[hi:, :]
            aug[hi:, :] = aug[hi:, :] - dot(below, rows)
    inv = aug[:, width:]
    na_ref[...] = dot(fa, inv, NT)
    nb_ref[...] = dot(fb, inv, NT)


def finish(red, a, b, v, d):
    vmem = pl.BlockSpec(memory_space=pltpu.VMEM)
    rows, width = a.shape
    return pl.pallas_call(
        chain_kernel,
        out_shape=(
            jax.ShapeDtypeStruct((1, rows), jnp.float32),
            jax.ShapeDtypeStruct((rows, width), jnp.float32),
            jax.ShapeDtypeStruct((rows, width), jnp.float32),
        ),
        in_specs=[vmem] * 5,
        out_specs=(vmem,) * 3,
        scratch_shapes=[pltpu.VMEM((width, 2 * width), jnp.float32)],
        compiler_params=pltpu.CompilerParams(vmem_limit_bytes=32 << 20),
    )(red, a, b, v, d)


def solution(mesh):
    nx = mesh.shape["sub"]
    sizes = (mesh.shape["rows"] // (2 * nx), nx, nx)

    def on_device(a, b, v, d, r):
        red = reduce_all(sizes, a, b, v, d, r.reshape(1, -1))
        up, new_a, new_b = finish(red, a, b, v, d)
        return up.reshape(-1), new_a, new_b

    spread = P(("rows", "sub"))
    wide = P(("rows", "sub"), None)
    return jax.shard_map(
        on_device, mesh=mesh, in_specs=(wide,) * 4 + (spread,), out_specs=(spread, wide, wide), check_vma=False
    )
```

```python
import functools

import jax
import jax.numpy as jnp
from jax import lax
from jax.experimental import pallas as pl
from jax.experimental.pallas import tpu as pltpu
from jax.sharding import PartitionSpec as P

MESH = pl.DeviceIdType.MESH
LANES = 128
PACK = 768
BLOCK = 32

NN = (((1,), (0,)), ((), ()))
NT = (((1,), (1,)), ((), ()))
TN = (((0,), (0,)), ((), ()))


def dot(left, right, dims=NN):
    return lax.dot_general(left, right, dims, precision=lax.Precision.HIGHEST, preferred_element_type=jnp.float32)


def pack_pair(gram, out_ref, base):
    row = lax.broadcasted_iota(jnp.int32, (LANES, LANES), 0)
    lane = lax.broadcasted_iota(jnp.int32, (LANES, LANES), 1)
    first, last = gram[:LANES, :LANES], gram[LANES:, LANES:]
    out_ref[base:base + LANES, :] = jnp.where(row >= lane, first, last)
    out_ref[base + LANES:base + 2 * LANES, :] = gram[LANES:, :LANES]
    return jnp.sum(jnp.where(row == lane, last, 0.0), axis=0, keepdims=True)


def unpack_pair(red_ref, base, diag):
    row = lax.broadcasted_iota(jnp.int32, (LANES, LANES), 0)
    lane = lax.broadcasted_iota(jnp.int32, (LANES, LANES), 1)
    both = red_ref[base:base + LANES, :]
    turned = both.T
    low = red_ref[base + LANES:base + 2 * LANES, :]
    first = jnp.where(row >= lane, both, turned)
    last = jnp.where(row < lane, both, jnp.where(row > lane, turned, diag))
    return jnp.concatenate(
        [jnp.concatenate([first, low.T], axis=1), jnp.concatenate([low, last], axis=1)], axis=0
    )


def reduce_kernel(sizes, a_ref, b_ref, v_ref, d_ref, r_ref, out_ref, local, pair, half, near, mine, far, total, full,
                  pair_sem, near_sem, far_sem, total_sem, back_sem, cross_sem,
                  pair_out, near_out, far_out, total_out, back_out, cross_out):
    nz, ny, nx = sizes
    peers = ny * nx
    rows = PACK // 2
    piece = rows // peers
    tiles = piece // 8
    place = lax.axis_index("rows")
    x = lax.axis_index("sub")
    core = lax.rem(place, 2)
    y = lax.rem(place // 2, ny)
    z = place // (2 * ny)
    me = y * nx + x
    near_ids = []
    for dy in range(ny):
        for dx in range(nx):
            if dy or dx:
                qy, qx = lax.rem(y + dy, ny), lax.rem(x + dx, nx)
                hops = min(dy, ny - dy) + min(dx, nx - dx)
                near_ids.append((hops, dy * nx + dx, qy * nx + qx, ((z * ny + qy) * 2 + core, qx)))
    near_ids = [item[2:] for item in sorted(near_ids, key=lambda item: (-item[0], item[1]))]
    far_ids = []
    for dz in sorted(range(1, nz), key=lambda d: -min(d, nz - d)):
        qz = lax.rem(z + dz, nz)
        far_ids.append((dz, qz, ((qz * ny + y) * 2 + core, x)))
    partner = (place + 1 - 2 * core, x)
    owners = [(t * nz) // tiles if nz >= tiles else t % nz for t in range(tiles)]

    barrier = pltpu.get_barrier_semaphore()
    for _, _, dev in far_ids:
        pl.semaphore_signal(barrier, inc=1, device_id=dev, device_id_type=MESH)
    for _, dev in near_ids:
        pl.semaphore_signal(barrier, inc=1, device_id=dev, device_id_type=MESH)
    pl.semaphore_signal(barrier, inc=1, device_id=partner, device_id_type=MESH)

    a, b = a_ref[...], b_ref[...]
    v, d = v_ref[...], d_ref[...]
    cols = v.shape[0]
    diag_a = pack_pair(dot(a, a, TN), local, 0)
    diag_b = pack_pair(dot(b, b, TN), local, 2 * LANES)
    va = dot(v, a)
    left = jnp.concatenate([d, jnp.broadcast_to(r_ref[...], (8, d.shape[1]))], axis=0)
    db = dot(left, b)
    dd = dot(left, d, NT)
    vv = dot(v, v, NT)
    local[512:512 + cols, :] = va[:, :LANES]
    local[512 + cols:576, :] = va[:, LANES:]
    local[576:616, :] = db[:, :LANES]
    local[616:656, :] = db[:, LANES:]
    local[656:696, :] = jnp.zeros((40, LANES), jnp.float32)
    local[656:656 + cols, 0:cols] = vv
    local[656:696, 64:64 + cols] = dd
    local[696:768, :] = jnp.zeros((72, LANES), jnp.float32)
    local[696:697, :] = diag_a
    local[697:698, :] = diag_b

    pl.semaphore_wait(barrier, len(far_ids) + len(near_ids) + 1)

    def send(src, dst, out_sem, in_sem, dev):
        copy = pltpu.make_async_remote_copy(
            src_ref=src, dst_ref=dst, send_sem=out_sem, recv_sem=in_sem, device_id=dev, device_id_type=MESH
        )
        copy.start()
        return copy

    def arrived(ref, sem):
        pltpu.make_async_copy(ref, ref, sem).wait()

    pending = []

    def ds(start, size):
        return pl.ds(pl.multiple_of(start, 8), size)

    pending.append(send(local.at[ds((1 - core) * rows, rows)], pair, pair_out, pair_sem, partner))
    arrived(pair, pair_sem)
    half[...] = local[ds(core * rows, rows), :] + pair[...]

    for k, (q, dev) in enumerate(near_ids):
        pending.append(send(half.at[ds(q * piece, piece)], near.at[me], near_out.at[k], near_sem.at[me], dev))
    value = half[ds(me * piece, piece), :]
    for q, _ in near_ids:
        arrived(near.at[q], near_sem.at[q])
        value = value + near[q]
    mine[...] = value

    for t, owner in enumerate(owners):
        tile = pl.ds(8 * t, 8)

        @pl.when(z != owner)
        def _():
            send(mine.at[tile], far.at[t, z], far_out.at[t], far_sem.at[t, z], ((owner * ny + y) * 2 + core, x))

    for t, owner in enumerate(owners):
        tile = pl.ds(8 * t, 8)

        @pl.when(z == owner)
        def _():
            value = mine[8 * t:8 * t + 8, :]
            for dz, qz, dev in far_ids:
                arrived(far.at[t, qz], far_sem.at[t, qz])
                value = value + far[t, qz]
            total[8 * t:8 * t + 8, :] = value
            for dz, qz, dev in far_ids:
                send(total.at[tile], total.at[tile], total_out.at[t, dz], total_sem.at[t], dev)

    for t, owner in enumerate(owners):
        tile = pl.ds(8 * t, 8)

        @pl.when(z != owner)
        def _():
            arrived(total.at[tile], total_sem.at[t])

    slot = core * peers
    for k, (q, dev) in enumerate(near_ids):
        pending.append(send(total, full.at[slot + me], back_out.at[k], back_sem.at[me], dev))
    pending.append(send(total, full.at[slot + me], cross_out.at[me], cross_sem.at[me], partner))
    full[slot + me] = total[...]
    for q, _ in reversed(near_ids):
        arrived(full.at[slot + q], back_sem.at[q])
        pending.append(send(full.at[slot + q], full.at[slot + q], cross_out.at[q], cross_sem.at[q], partner))
    other = (1 - core) * peers
    for q in range(peers):
        arrived(full.at[other + q], cross_sem.at[q])
    for q in range(2 * peers):
        out_ref[q * piece:(q + 1) * piece, :] = full[q]

    for copy in pending:
        copy.wait_send()
    for t, owner in enumerate(owners):
        tile = pl.ds(8 * t, 8)

        @pl.when(z != owner)
        def _():
            arrived(mine.at[tile], far_out.at[t])

        @pl.when(z == owner)
        def _():
            for dz, _, _ in far_ids:
                arrived(total.at[tile], total_out.at[t, dz])


def reduce_all(sizes, a, b, v, d, r):
    nz, ny, nx = sizes
    peers = ny * nx
    piece = PACK // 2 // peers
    tiles = piece // 8
    vmem = pl.BlockSpec(memory_space=pltpu.VMEM)
    dma = pltpu.SemaphoreType.DMA
    return pl.pallas_call(
        functools.partial(reduce_kernel, sizes),
        out_shape=jax.ShapeDtypeStruct((PACK, LANES), jnp.float32),
        in_specs=[vmem] * 5,
        out_specs=vmem,
        scratch_shapes=[
            pltpu.VMEM((PACK, LANES), jnp.float32),
            pltpu.VMEM((PACK // 2, LANES), jnp.float32),
            pltpu.VMEM((PACK // 2, LANES), jnp.float32),
            pltpu.VMEM((peers, piece, LANES), jnp.float32),
            pltpu.VMEM((piece, LANES), jnp.float32),
            pltpu.VMEM((tiles, nz, 8, LANES), jnp.float32),
            pltpu.VMEM((piece, LANES), jnp.float32),
            pltpu.VMEM((2 * peers, piece, LANES), jnp.float32),
            dma(()), dma((peers,)), dma((tiles, nz)), dma((tiles,)), dma((peers,)), dma((peers,)),
            dma(()), dma((peers,)), dma((tiles,)), dma((tiles, nz)), dma((peers,)), dma((peers,)),
        ],
        compiler_params=pltpu.CompilerParams(collective_id=0, has_side_effects=True, vmem_limit_bytes=32 << 20),
    )(a, b, v, d, r)


def inverse_factor(tile, lane_in, lane_out):
    groups = BLOCK // 8
    sub = lax.broadcasted_iota(jnp.int32, (8, LANES), 0)
    lane = lax.broadcasted_iota(jnp.int32, (8, LANES), 1)
    columns = [
        {
            i: jnp.broadcast_to(tile[8 * i:8 * i + 8, lane_in + j:lane_in + j + 1], (8, LANES))
            for i in range(j // 8, groups)
        }
        for j in range(BLOCK)
    ]
    out = [jnp.where(lane == sub + (8 * i + lane_out), 1.0, 0.0) for i in range(groups)]
    for j in range(BLOCK):
        g, r = j // 8, j % 8
        scale = lax.rsqrt(columns[j][g][r:r + 1, :])
        column = {i: columns[j][i] * scale for i in range(g, groups)}
        pivot = out[g][r:r + 1, :] * scale
        for b in range(j + 1, BLOCK):
            factor = column[b // 8][b % 8:b % 8 + 1, :]
            for i in range(b // 8, groups):
                columns[b][i] = columns[b][i] - column[i] * factor
        out[g] = jnp.where(sub > r, out[g] - column[g] * pivot, jnp.where(sub == r, pivot, out[g]))
        for i in range(g + 1, groups):
            out[i] = out[i] - column[i] * pivot
    return jnp.concatenate(out, axis=0)


def largest(values):
    return jnp.max(jnp.max(values, axis=1, keepdims=True), axis=0, keepdims=True)


def diagonal(matrix):
    row = lax.broadcasted_iota(jnp.int32, matrix.shape, 0)
    lane = lax.broadcasted_iota(jnp.int32, matrix.shape, 1)
    return jnp.where(row == lane, matrix, 0.0)


def framed(rows, before, after):
    parts = [rows]
    if before:
        parts = [jnp.zeros((before, rows.shape[1]), rows.dtype)] + parts
    if after:
        parts = parts + [jnp.zeros((after, rows.shape[1]), rows.dtype)]
    return jnp.concatenate(parts, axis=0) if len(parts) > 1 else rows


def chain_kernel(red_ref, a_ref, b_ref, v_ref, d_ref, up_ref, na_ref, nb_ref, z_ref, f_ref):
    rows, width = a_ref.shape
    cols = v_ref.shape[0]
    small = red_ref[656:696, :]
    lower_inv = inverse_factor(small[:cols, :], 64, 0)[:, :cols]
    inv_v = dot(lower_inv.T, lower_inv)
    vv = small[:cols, :cols]
    gram_r = small[cols:cols + 8, 64:64 + cols]
    gram_a = unpack_pair(red_ref, 0, red_ref[696:697, :])
    gram_b = unpack_pair(red_ref, 256, red_ref[697:698, :])
    va = jnp.concatenate([red_ref[512:512 + cols, :], red_ref[512 + cols:576, :]], axis=1)
    db = jnp.concatenate([red_ref[576:616, :], red_ref[616:656, :]], axis=1)
    proj_t, proj_r = db[:cols, :], db[cols:cols + 8, :]
    scale_a = 1.0 / jnp.maximum(largest(diagonal(gram_a)), largest(diagonal(vv)))
    scale_b = 1.0 / largest(diagonal(gram_b))
    gram_a = gram_a * scale_a
    va = va * scale_a
    vv = vv * scale_a
    av = va.T
    proj = proj_t.T

    w = dot(inv_v, proj_t)
    ws = w * scale_b
    wst = dot(proj, inv_v) * scale_b
    s = (gram_b - dot(proj, w)) * scale_b
    k1 = dot(gram_a, s) + dot(av, ws)
    k1t = dot(s, gram_a) + dot(wst, va)
    k2 = dot(va, s) + dot(vv, ws)
    k2t = dot(s, av) + dot(wst, vv)
    j1 = dot(s, k1)
    c = dot(inv_v, k2)
    cs = c * scale_b
    z_ref[...] = dot(k1t, j1) + dot(k2t, cs)

    a, b = a_ref[...], b_ref[...]
    v, d = v_ref[...], d_ref[...]
    coeffs = -dot(gram_r, inv_v)
    lead = -proj_r - dot(coeffs, proj_t)
    up = dot(lead, a, NT) + dot(coeffs, v)
    up_ref[...] = up[:1, :]
    root = jnp.sqrt(scale_b)
    f_ref[:rows, :] = (dot(a, j1) + dot(v.T, cs)) / root
    dn = d.T
    f_ref[rows:, :] = (dot(b - dot(dn, w), k1) + dot(dn, c)) * root

    for lo in range(0, width, BLOCK):
        hi = lo + BLOCK
        base = lo // LANES * LANES
        tile = slice(base, base + LANES)
        inv = inverse_factor(z_ref[lo:hi, tile], lo - base, lo - base)
        inv = framed(inv, lo - base, base + LANES - hi)
        if hi < width:
            panel = dot(z_ref[hi:, tile], inv, NT)
            for start in range(hi // LANES * LANES, width, LANES):
                first = max(hi, start)
                right = framed(panel[first - hi:start + LANES - hi, :], first - start, 0)
                z_ref[first:, start:start + LANES] = z_ref[first:, start:start + LANES] - dot(panel[first - hi:, :], right, NT)
        done = dot(f_ref[:, tile], inv, NT)
        if lo == base:
            na_ref[:, tile] = done[:rows, :]
            nb_ref[:, tile] = done[rows:, :]
        else:
            na_ref[:, tile] = na_ref[:, tile] + done[:rows, :]
            nb_ref[:, tile] = nb_ref[:, tile] + done[rows:, :]
        if hi < width:
            for start in range(hi // LANES * LANES, width, LANES):
                first = max(hi, start)
                right = framed(panel[first - hi:start + LANES - hi, :], first - start, 0)
                f_ref[:, start:start + LANES] = f_ref[:, start:start + LANES] - dot(done, right, NT)


def finish(red, a, b, v, d):
    vmem = pl.BlockSpec(memory_space=pltpu.VMEM)
    rows, width = a.shape
    return pl.pallas_call(
        chain_kernel,
        out_shape=(
            jax.ShapeDtypeStruct((1, rows), jnp.float32),
            jax.ShapeDtypeStruct((rows, width), jnp.float32),
            jax.ShapeDtypeStruct((rows, width), jnp.float32),
        ),
        in_specs=[vmem] * 5,
        out_specs=(vmem,) * 3,
        scratch_shapes=[pltpu.VMEM((width, width), jnp.float32), pltpu.VMEM((2 * rows, width), jnp.float32)],
        compiler_params=pltpu.CompilerParams(vmem_limit_bytes=32 << 20),
    )(red, a, b, v, d)


def solution(mesh):
    nx = mesh.shape["sub"]
    sizes = (mesh.shape["rows"] // (2 * nx), nx, nx)

    def on_device(a, b, v, d, r):
        red = reduce_all(sizes, a, b, v.T, d.T, r.reshape(1, -1))
        up, new_a, new_b = finish(red, a, b, v.T, d.T)
        return up.reshape(-1), new_a, new_b

    spread = P(("rows", "sub"))
    wide = P(("rows", "sub"), None)
    return jax.shard_map(
        on_device, mesh=mesh, in_specs=(wide,) * 4 + (spread,), out_specs=(spread, wide, wide), check_vma=False
    )
```

```python
import functools

import jax
import jax.numpy as jnp
from jax import lax
from jax.experimental import pallas as pl
from jax.experimental.pallas import tpu as pltpu
from jax.sharding import PartitionSpec as P

MESH = pl.DeviceIdType.MESH
LANES = 128
PACK = 768
BLOCK = 32

NN = (((1,), (0,)), ((), ()))
NT = (((1,), (1,)), ((), ()))
TN = (((0,), (0,)), ((), ()))


def halves(value):
    high = value.astype(jnp.bfloat16)
    return high, (value - high.astype(jnp.float32)).astype(jnp.bfloat16)


def dot(left, right, dims=NN):
    left = left if isinstance(left, tuple) else halves(left)
    right = right if isinstance(right, tuple) else halves(right)

    def one(l, r):
        return lax.dot_general(l, r, dims, preferred_element_type=jnp.float32)

    return one(left[0], right[0]) + (one(left[0], right[1]) + one(left[1], right[0]))


def gram_pair(value, out_ref, base):
    turned = value.T
    whole, first = halves(value), halves(turned[:LANES, :])
    return pack_pair(
        dot(first, tuple(part[:, :LANES] for part in whole)), dot(turned[LANES:, :], whole), out_ref, base
    )


def pack_pair(first, below, out_ref, base):
    row = lax.broadcasted_iota(jnp.int32, (LANES, LANES), 0)
    lane = lax.broadcasted_iota(jnp.int32, (LANES, LANES), 1)
    last = below[:, LANES:]
    out_ref[base:base + LANES, :] = jnp.where(row >= lane, first, last)
    out_ref[base + LANES:base + 2 * LANES, :] = below[:, :LANES]
    return jnp.sum(jnp.where(row == lane, last, 0.0), axis=0, keepdims=True)


def unpack_pair(red_ref, base, diag):
    row = lax.broadcasted_iota(jnp.int32, (LANES, LANES), 0)
    lane = lax.broadcasted_iota(jnp.int32, (LANES, LANES), 1)
    both = red_ref[base:base + LANES, :]
    turned = both.T
    low = red_ref[base + LANES:base + 2 * LANES, :]
    first = jnp.where(row >= lane, both, turned)
    last = jnp.where(row < lane, both, jnp.where(row > lane, turned, diag))
    return jnp.concatenate(
        [jnp.concatenate([first, low.T], axis=1), jnp.concatenate([low, last], axis=1)], axis=0
    )


def fetch(sources, targets, sems):
    copies = [pltpu.make_async_copy(src, dst, sems.at[k]) for k, (src, dst) in enumerate(zip(sources, targets))]
    for copy in copies:
        copy.start()
    return copies


def reduce_kernel(sizes, a_hbm, b_hbm, v_hbm, d_hbm, r_hbm, out_ref, a_ref, b_ref, v_ref, d_ref, r_ref, load_sem, local, pair, half, near, mine, far, total, full,
                  pair_sem, near_sem, far_sem, total_sem, back_sem, cross_sem,
                  pair_out, near_out, far_out, total_out, back_out, cross_out):
    nz, ny, nx = sizes
    peers = ny * nx
    rows = PACK // 2
    piece = rows // peers
    tiles = piece // 8
    place = lax.axis_index("rows")
    x = lax.axis_index("sub")
    core = lax.rem(place, 2)
    y = lax.rem(place // 2, ny)
    z = place // (2 * ny)
    me = y * nx + x
    near_ids = []
    for dy in range(ny):
        for dx in range(nx):
            if dy or dx:
                qy, qx = lax.rem(y + dy, ny), lax.rem(x + dx, nx)
                hops = min(dy, ny - dy) + min(dx, nx - dx)
                near_ids.append((hops, dy * nx + dx, qy * nx + qx, ((z * ny + qy) * 2 + core, qx)))
    near_ids = [item[2:] for item in sorted(near_ids, key=lambda item: (-item[0], item[1]))]
    far_ids = []
    for dz in sorted(range(1, nz), key=lambda d: -min(d, nz - d)):
        qz = lax.rem(z + dz, nz)
        far_ids.append((dz, qz, ((qz * ny + y) * 2 + core, x)))
    partner = (place + 1 - 2 * core, x)
    owners = [(t * nz) // tiles if nz >= tiles else t % nz for t in range(tiles)]

    loads = fetch((b_hbm, d_hbm, r_hbm, a_hbm, v_hbm), (b_ref, d_ref, r_ref, a_ref, v_ref), load_sem)
    barrier = pltpu.get_barrier_semaphore()
    for _, _, dev in far_ids:
        pl.semaphore_signal(barrier, inc=1, device_id=dev, device_id_type=MESH)
    for _, dev in near_ids:
        pl.semaphore_signal(barrier, inc=1, device_id=dev, device_id_type=MESH)
    pl.semaphore_signal(barrier, inc=1, device_id=partner, device_id_type=MESH)

    cols = v_ref.shape[0]
    for copy in loads[:3]:
        copy.wait()
    diag_b = gram_pair(b_ref[...], local, 2 * LANES)
    d = d_ref[...]
    left = halves(jnp.concatenate([d, jnp.broadcast_to(r_ref[...], (8, d.shape[1]))], axis=0))
    db = dot(left, b_ref[...])
    dd = dot(left, d, NT)
    for copy in loads[3:]:
        copy.wait()
    diag_a = gram_pair(a_ref[...], local, 0)
    v = halves(v_ref[...])
    va = dot(v, a_ref[...])
    vv = dot(v, v, NT)
    local[512:512 + cols, :] = va[:, :LANES]
    local[512 + cols:576, :] = va[:, LANES:]
    local[576:616, :] = db[:, :LANES]
    local[616:656, :] = db[:, LANES:]
    local[656:696, :] = jnp.zeros((40, LANES), jnp.float32)
    local[656:656 + cols, 0:cols] = vv
    local[656:696, 64:64 + cols] = dd
    local[696:768, :] = jnp.zeros((72, LANES), jnp.float32)
    local[696:697, :] = diag_a
    local[697:698, :] = diag_b

    pl.semaphore_wait(barrier, len(far_ids) + len(near_ids) + 1)

    def send(src, dst, out_sem, in_sem, dev):
        copy = pltpu.make_async_remote_copy(
            src_ref=src, dst_ref=dst, send_sem=out_sem, recv_sem=in_sem, device_id=dev, device_id_type=MESH
        )
        copy.start()
        return copy

    def arrived(ref, sem):
        pltpu.make_async_copy(ref, ref, sem).wait()

    pending = []

    def ds(start, size):
        return pl.ds(pl.multiple_of(start, 8), size)

    pending.append(send(local.at[ds((1 - core) * rows, rows)], pair, pair_out, pair_sem, partner))
    arrived(pair, pair_sem)
    half[...] = local[ds(core * rows, rows), :] + pair[...]

    for k, (q, dev) in enumerate(near_ids):
        pending.append(send(half.at[ds(q * piece, piece)], near.at[me], near_out.at[k], near_sem.at[me], dev))
    value = half[ds(me * piece, piece), :]
    for q, _ in near_ids:
        arrived(near.at[q], near_sem.at[q])
        value = value + near[q]
    mine[...] = value

    for t, owner in enumerate(owners):
        tile = pl.ds(8 * t, 8)

        @pl.when(z != owner)
        def _():
            send(mine.at[tile], far.at[t, z], far_out.at[t], far_sem.at[t, z], ((owner * ny + y) * 2 + core, x))

    for t, owner in enumerate(owners):
        tile = pl.ds(8 * t, 8)

        @pl.when(z == owner)
        def _():
            value = mine[8 * t:8 * t + 8, :]
            for dz, qz, dev in far_ids:
                arrived(far.at[t, qz], far_sem.at[t, qz])
                value = value + far[t, qz]
            total[8 * t:8 * t + 8, :] = value
            for dz, qz, dev in far_ids:
                send(total.at[tile], total.at[tile], total_out.at[t, dz], total_sem.at[t], dev)

    for t, owner in enumerate(owners):
        tile = pl.ds(8 * t, 8)

        @pl.when(z != owner)
        def _():
            arrived(total.at[tile], total_sem.at[t])

    slot = core * peers
    for k, (q, dev) in enumerate(near_ids):
        pending.append(send(total, full.at[slot + me], back_out.at[k], back_sem.at[me], dev))
    pending.append(send(total, full.at[slot + me], cross_out.at[me], cross_sem.at[me], partner))
    full[slot + me] = total[...]
    for q, _ in reversed(near_ids):
        arrived(full.at[slot + q], back_sem.at[q])
        pending.append(send(full.at[slot + q], full.at[slot + q], cross_out.at[q], cross_sem.at[q], partner))
    other = (1 - core) * peers
    for q in range(peers):
        arrived(full.at[other + q], cross_sem.at[q])
    for q in range(2 * peers):
        out_ref[q * piece:(q + 1) * piece, :] = full[q]

    for copy in pending:
        copy.wait_send()
    for t, owner in enumerate(owners):
        tile = pl.ds(8 * t, 8)

        @pl.when(z != owner)
        def _():
            arrived(mine.at[tile], far_out.at[t])

        @pl.when(z == owner)
        def _():
            for dz, _, _ in far_ids:
                arrived(total.at[tile], total_out.at[t, dz])


def reduce_all(sizes, a, b, v, d, r):
    nz, ny, nx = sizes
    peers = ny * nx
    piece = PACK // 2 // peers
    tiles = piece // 8
    vmem = pl.BlockSpec(memory_space=pltpu.VMEM)
    dma = pltpu.SemaphoreType.DMA
    return pl.pallas_call(
        functools.partial(reduce_kernel, sizes),
        out_shape=jax.ShapeDtypeStruct((PACK, LANES), jnp.float32),
        in_specs=[pl.BlockSpec(memory_space=pltpu.HBM)] * 5,
        out_specs=vmem,
        scratch_shapes=[
            *(pltpu.VMEM(value.shape, jnp.float32) for value in (a, b, v, d, r)),
            dma((5,)),
            pltpu.VMEM((PACK, LANES), jnp.float32),
            pltpu.VMEM((PACK // 2, LANES), jnp.float32),
            pltpu.VMEM((PACK // 2, LANES), jnp.float32),
            pltpu.VMEM((peers, piece, LANES), jnp.float32),
            pltpu.VMEM((piece, LANES), jnp.float32),
            pltpu.VMEM((tiles, nz, 8, LANES), jnp.float32),
            pltpu.VMEM((piece, LANES), jnp.float32),
            pltpu.VMEM((2 * peers, piece, LANES), jnp.float32),
            dma(()), dma((peers,)), dma((tiles, nz)), dma((tiles,)), dma((peers,)), dma((peers,)),
            dma(()), dma((peers,)), dma((tiles,)), dma((tiles, nz)), dma((peers,)), dma((peers,)),
        ],
        compiler_params=pltpu.CompilerParams(collective_id=0, has_side_effects=True, vmem_limit_bytes=32 << 20),
    )(a, b, v, d, r)


def inverse_factor(tile, lane_in, lane_out):
    groups = BLOCK // 8
    sub = lax.broadcasted_iota(jnp.int32, (8, LANES), 0)
    lane = lax.broadcasted_iota(jnp.int32, (8, LANES), 1)
    columns = [
        {
            i: jnp.broadcast_to(tile[8 * i:8 * i + 8, lane_in + j:lane_in + j + 1], (8, LANES))
            for i in range(j // 8, groups)
        }
        for j in range(BLOCK)
    ]
    out = [jnp.where(lane == sub + (8 * i + lane_out), 1.0, 0.0) for i in range(groups)]
    for j in range(BLOCK):
        g, r = j // 8, j % 8
        scale = lax.rsqrt(columns[j][g][r:r + 1, :])
        column = {i: columns[j][i] * scale for i in range(g, groups)}
        pivot = out[g][r:r + 1, :] * scale
        for b in range(j + 1, BLOCK):
            factor = column[b // 8][b % 8:b % 8 + 1, :]
            for i in range(b // 8, groups):
                columns[b][i] = columns[b][i] - column[i] * factor
        out[g] = jnp.where(sub > r, out[g] - column[g] * pivot, jnp.where(sub == r, pivot, out[g]))
        for i in range(g + 1, groups):
            out[i] = out[i] - column[i] * pivot
    return jnp.concatenate(out, axis=0)


def largest(values):
    return jnp.max(jnp.max(values, axis=1, keepdims=True), axis=0, keepdims=True)


def diagonal(matrix):
    row = lax.broadcasted_iota(jnp.int32, matrix.shape, 0)
    lane = lax.broadcasted_iota(jnp.int32, matrix.shape, 1)
    return jnp.where(row == lane, matrix, 0.0)


def framed(rows, before, after):
    parts = [rows]
    if before:
        parts = [jnp.zeros((before, rows.shape[1]), rows.dtype)] + parts
    if after:
        parts = parts + [jnp.zeros((after, rows.shape[1]), rows.dtype)]
    return jnp.concatenate(parts, axis=0) if len(parts) > 1 else rows


def chain_kernel(red_ref, a_hbm, b_hbm, v_hbm, d_hbm, up_ref, na_ref, nb_ref, a_ref, b_ref, v_ref, d_ref, load_sem, z_ref, f_ref):
    loads = fetch((a_hbm, b_hbm, v_hbm, d_hbm), (a_ref, b_ref, v_ref, d_ref), load_sem)
    rows, width = a_ref.shape
    cols = v_ref.shape[0]
    small = red_ref[656:696, :]
    lower_inv = inverse_factor(small[:cols, :], 64, 0)[:, :cols]
    inv_v = dot(lower_inv.T, lower_inv)
    vv = small[:cols, :cols]
    gram_r = small[cols:cols + 8, 64:64 + cols]
    gram_a = unpack_pair(red_ref, 0, red_ref[696:697, :])
    gram_b = unpack_pair(red_ref, 256, red_ref[697:698, :])
    va = jnp.concatenate([red_ref[512:512 + cols, :], red_ref[512 + cols:576, :]], axis=1)
    db = jnp.concatenate([red_ref[576:616, :], red_ref[616:656, :]], axis=1)
    proj_t, proj_r = db[:cols, :], db[cols:cols + 8, :]
    scale_a = 1.0 / jnp.maximum(largest(diagonal(gram_a)), largest(diagonal(vv)))
    scale_b = 1.0 / largest(diagonal(gram_b))
    gram_a = gram_a * scale_a
    va = va * scale_a
    vv = vv * scale_a
    av = va.T
    proj = proj_t.T

    inv_v = halves(inv_v)
    w = dot(inv_v, proj_t)
    proj = halves(proj)
    wt = dot(proj, inv_v)
    ws = halves(w * scale_b)
    wst = halves(wt * scale_b)
    s = halves((gram_b - dot(proj, w)) * scale_b)
    gram_a, va, vv, av = halves(gram_a), halves(va), halves(vv), halves(av)
    k1 = halves(dot(gram_a, s) + dot(av, ws))
    k1t = dot(s, gram_a) + dot(wst, va)
    k2 = dot(va, s) + dot(vv, ws)
    k2t = dot(s, av) + dot(wst, vv)
    j1 = halves(dot(s, k1))
    c = dot(inv_v, k2)
    cs = halves(c * scale_b)
    z_ref[...] = dot(k1t, j1) + dot(k2t, cs)

    for copy in loads:
        copy.wait()
    v, d = v_ref[...], d_ref[...]
    coeffs = -dot(gram_r, inv_v)
    lead = -proj_r - dot(coeffs, proj_t)
    a = halves(a_ref[...])
    up = dot(lead, a, NT) + dot(coeffs, v)
    up_ref[...] = up[:1, :]
    root = jnp.sqrt(scale_b)
    f_ref[:rows, :] = (dot(a, j1) + dot(v.T, cs)) / root
    dn = halves(d.T)
    f_ref[rows:, :] = (dot(b_ref[...] - dot(dn, w), k1) + dot(dn, c)) * root

    for lo in range(0, width, BLOCK):
        hi = lo + BLOCK
        base = lo // LANES * LANES
        tile = slice(base, base + LANES)
        inv = inverse_factor(z_ref[lo:hi, tile], lo - base, lo - base)
        inv = halves(framed(inv, lo - base, base + LANES - hi))
        if hi < width:
            panel = halves(dot(z_ref[hi:, tile], inv, NT))
            for start in range(hi // LANES * LANES, width, LANES):
                first = max(hi, start)
                left = tuple(part[first - hi:, :] for part in panel)
                right = tuple(framed(part[first - hi:start + LANES - hi, :], first - start, 0) for part in panel)
                z_ref[first:, start:start + LANES] = z_ref[first:, start:start + LANES] - dot(left, right, NT)
        done = dot(f_ref[:, tile], inv, NT)
        if lo == base:
            na_ref[:, tile] = done[:rows, :]
            nb_ref[:, tile] = done[rows:, :]
        else:
            na_ref[:, tile] = na_ref[:, tile] + done[:rows, :]
            nb_ref[:, tile] = nb_ref[:, tile] + done[rows:, :]
        if hi < width:
            done = halves(done)
            for start in range(hi // LANES * LANES, width, LANES):
                first = max(hi, start)
                right = tuple(framed(part[first - hi:start + LANES - hi, :], first - start, 0) for part in panel)
                f_ref[:, start:start + LANES] = f_ref[:, start:start + LANES] - dot(done, right, NT)


def finish(red, a, b, v, d):
    vmem = pl.BlockSpec(memory_space=pltpu.VMEM)
    rows, width = a.shape
    return pl.pallas_call(
        chain_kernel,
        out_shape=(
            jax.ShapeDtypeStruct((1, rows), jnp.float32),
            jax.ShapeDtypeStruct((rows, width), jnp.float32),
            jax.ShapeDtypeStruct((rows, width), jnp.float32),
        ),
        in_specs=[vmem] + [pl.BlockSpec(memory_space=pltpu.HBM)] * 4,
        out_specs=(vmem,) * 3,
        scratch_shapes=[
            *(pltpu.VMEM(value.shape, jnp.float32) for value in (a, b, v, d)),
            pltpu.SemaphoreType.DMA((4,)),
            pltpu.VMEM((width, width), jnp.float32), pltpu.VMEM((2 * rows, width), jnp.float32)],
        compiler_params=pltpu.CompilerParams(vmem_limit_bytes=32 << 20),
    )(red, a, b, v, d)


def solution(mesh):
    nx = mesh.shape["sub"]
    sizes = (mesh.shape["rows"] // (2 * nx), nx, nx)

    def on_device(a, b, v, d, r):
        hbm = lambda value: pltpu.with_memory_space_constraint(value, pltpu.HBM)
        a, b, vt, dt, rt = hbm(a), hbm(b), hbm(v.T), hbm(d.T), hbm(r.reshape(1, -1))
        red = reduce_all(sizes, a, b, vt, dt, rt)
        up, new_a, new_b = finish(red, a, b, vt, dt)
        return up.reshape(-1), new_a, new_b

    spread = P(("rows", "sub"))
    wide = P(("rows", "sub"), None)
    return jax.shard_map(
        on_device, mesh=mesh, in_specs=(wide,) * 4 + (spread,), out_specs=(spread, wide, wide), check_vma=False
    )
```

```python
import functools

import jax
import jax.numpy as jnp
from jax import lax
from jax.experimental import pallas as pl
from jax.experimental.pallas import tpu as pltpu
from jax.sharding import PartitionSpec as P

MESH = pl.DeviceIdType.MESH
LANES = 128
PACK = 704
BLOCK = 32

NN = (((1,), (0,)), ((), ()))
NT = (((1,), (1,)), ((), ()))
TN = (((0,), (0,)), ((), ()))


def halves(value):
    high = value.astype(jnp.bfloat16)
    return high, (value - high.astype(jnp.float32)).astype(jnp.bfloat16)


def dot(left, right, dims=NN):
    left = left if isinstance(left, tuple) else halves(left)
    right = right if isinstance(right, tuple) else halves(right)

    def one(l, r):
        return lax.dot_general(l, r, dims, preferred_element_type=jnp.float32)

    return one(left[0], right[0]) + (one(left[0], right[1]) + one(left[1], right[0]))


def gram_pair(value, out_ref, base):
    turned = value.T
    whole, first = halves(value), halves(turned[:LANES, :])
    return pack_pair(
        dot(first, tuple(part[:, :LANES] for part in whole)), dot(turned[LANES:, :], whole), out_ref, base
    )


def pack_pair(first, below, out_ref, base):
    row = lax.broadcasted_iota(jnp.int32, (LANES, LANES), 0)
    lane = lax.broadcasted_iota(jnp.int32, (LANES, LANES), 1)
    last = below[:, LANES:]
    out_ref[base:base + LANES, :] = jnp.where(row >= lane, first, last)
    out_ref[base + LANES:base + 2 * LANES, :] = below[:, :LANES]
    return jnp.sum(jnp.where(row == lane, last, 0.0), axis=0, keepdims=True)


def unpack_pair(red_ref, base, diag):
    row = lax.broadcasted_iota(jnp.int32, (LANES, LANES), 0)
    lane = lax.broadcasted_iota(jnp.int32, (LANES, LANES), 1)
    both = red_ref[base:base + LANES, :]
    turned = both.T
    low = red_ref[base + LANES:base + 2 * LANES, :]
    first = jnp.where(row >= lane, both, turned)
    last = jnp.where(row < lane, both, jnp.where(row > lane, turned, diag))
    return jnp.concatenate(
        [jnp.concatenate([first, low.T], axis=1), jnp.concatenate([low, last], axis=1)], axis=0
    )


def fetch(sources, targets, sems):
    copies = [pltpu.make_async_copy(src, dst, sems.at[k]) for k, (src, dst) in enumerate(zip(sources, targets))]
    for copy in copies:
        copy.start()
    return copies


def reduce_kernel(sizes, a_hbm, b_hbm, v_hbm, d_hbm, r_hbm, out_ref, a_ref, b_ref, v_ref, d_ref, r_ref, load_sem,
                  local, pair, half, near, more, mine, far, total, full,
                  pair_sem, near_sem, more_sem, far_sem, back_sem, rest_sem, cross_sem,
                  pair_out, near_out, more_out, far_out, back_out, rest_out, cross_out):
    nz, ny, nx = sizes
    rows = PACK // 2
    plane = ny * nx
    cell = 2 * plane
    steps = nz // 2
    place = lax.axis_index("rows")
    x = lax.axis_index("sub")
    core = lax.rem(place, 2)
    y = lax.rem(place // 2, ny)
    z = place // (2 * ny)
    side, step = lax.rem(z, 2), z // 2
    me = side * plane + y * nx + x
    near_ids = []
    for dz in range(2):
        for dy in range(ny):
            for dx in range(nx):
                if dz or dy or dx:
                    qz, qy, qx = lax.rem(side + dz, 2), lax.rem(y + dy, ny), lax.rem(x + dx, nx)
                    hops = dz + min(dy, ny - dy) + min(dx, nx - dx)
                    dev = (((2 * step + qz) * ny + qy) * 2 + core, qx)
                    near_ids.append((hops, len(near_ids), qz * plane + qy * nx + qx, dev))
    near_ids = [item[2:] for item in sorted(near_ids, key=lambda item: (-item[0], item[1]))]
    far_ids = []
    for dz in sorted(range(1, steps), key=lambda d: -min(d, steps - d)):
        qz = lax.rem(step + dz, steps)
        far_ids.append((qz, ((2 * (2 * ny) * qz + 2 * ny * side) + 2 * y + core, x)))
    partner = (place + 1 - 2 * core, x)
    doubles = [(0, qy, qx) for qy in range(ny) for qx in range(nx) if (qx + qy) % 2 == 0]
    doubles += [(1, qy, qx) for qy in range(ny) for qx in range(nx) if (qx + qy) % 4 == 1]
    even = side == 0
    double = (even & (lax.rem(x + y, 2) == 0)) | ((side == 1) & (lax.rem(x + y, 4) == 1))
    mine_second = jnp.where(even, y * (nx // 2) + x // 2, plane // 2 + y)

    loads = fetch((b_hbm, d_hbm, r_hbm, a_hbm, v_hbm), (b_ref, d_ref, r_ref, a_ref, v_ref), load_sem)
    barrier = pltpu.get_barrier_semaphore()
    for _, dev in far_ids:
        pl.semaphore_signal(barrier, inc=1, device_id=dev, device_id_type=MESH)
    for _, dev in near_ids:
        pl.semaphore_signal(barrier, inc=1, device_id=dev, device_id_type=MESH)
    pl.semaphore_signal(barrier, inc=1, device_id=partner, device_id_type=MESH)

    cols = v_ref.shape[0]
    for copy in loads[:3]:
        copy.wait()
    diag_b = gram_pair(b_ref[...], local, 2 * LANES)
    d = d_ref[...]
    left = halves(jnp.concatenate([d, jnp.broadcast_to(r_ref[...], (8, d.shape[1]))], axis=0))
    db = dot(left, b_ref[...])
    dd = dot(left, d, NT)
    for copy in loads[3:]:
        copy.wait()
    diag_a = gram_pair(a_ref[...], local, 0)
    v = halves(v_ref[...])
    va = dot(v, a_ref[...])
    vv = dot(v, v, NT)
    local[512:512 + cols, :] = va[:, :LANES]
    local[512 + cols:576, :] = va[:, LANES:]
    local[576:616, :] = db[:, :LANES]
    local[616:656, :] = db[:, LANES:]
    local[656:696, :] = jnp.zeros((40, LANES), jnp.float32)
    local[656:656 + cols, 0:cols] = vv
    local[656:696, 64:64 + cols] = dd
    local[696:704, :] = jnp.zeros((8, LANES), jnp.float32)
    local[696:697, :] = diag_a
    local[697:698, :] = diag_b

    pl.semaphore_wait(barrier, len(far_ids) + len(near_ids) + 1)

    def send(src, dst, out_sem, in_sem, dev):
        copy = pltpu.make_async_remote_copy(
            src_ref=src, dst_ref=dst, send_sem=out_sem, recv_sem=in_sem, device_id=dev, device_id_type=MESH
        )
        copy.start()
        return copy

    def arrived(ref, sem):
        pltpu.make_async_copy(ref, ref, sem).wait()

    pending = []

    def at(start, size=8):
        return pl.ds(pl.multiple_of(start, 8), size)

    def each_double(action):
        for k, (qz, qy, qx) in enumerate(doubles):

            @pl.when(me != qz * plane + qy * nx + qx)
            def _():
                action(k, (((2 * step + qz) * ny + qy) * 2 + core, qx))

    pending.append(send(local.at[at((1 - core) * rows, rows)], pair, pair_out, pair_sem, partner))
    arrived(pair, pair_sem)
    half[...] = local[at(core * rows, rows), :] + pair[...]

    for k, (q, dev) in enumerate(near_ids):
        pending.append(send(half.at[at(8 * q)], near.at[me], near_out.at[k], near_sem.at[me], dev))
    each_double(lambda k, dev: send(half.at[pl.ds(8 * (cell + k), 8)], more.at[me], more_out.at[k], more_sem.at[me], dev))
    value = half[at(8 * me), :]
    for q, _ in reversed(near_ids):
        arrived(near.at[q], near_sem.at[q])
        value = value + near[q]
    mine[0:8, :] = value

    @pl.when(jnp.logical_not(double))
    def _():
        for k, (q, dev) in enumerate(far_ids):
            send(mine.at[0:8], far.at[step, 0:8], far_out.at[k], far_sem.at[step], dev)
        far[step, 0:8] = mine[0:8, :]
        for q, _ in reversed(far_ids):
            arrived(far.at[q, 0:8], far_sem.at[q])
        value = far[0, 0:8]
        for k in range(1, steps):
            value = value + far[k, 0:8]
        total[0:8, :] = value

    @pl.when(double)
    def _():
        value = half[at(8 * (cell + mine_second)), :]
        for q, _ in reversed(near_ids):
            arrived(more.at[q], more_sem.at[q])
            value = value + more[q]
        mine[8:16, :] = value
        for k, (q, dev) in enumerate(far_ids):
            send(mine, far.at[step], far_out.at[k], far_sem.at[step], dev)
        far[step] = mine[...]
        for q, _ in reversed(far_ids):
            arrived(far.at[q], far_sem.at[q])
        value = far[0]
        for k in range(1, steps):
            value = value + far[k]
        total[...] = value

    base = core * rows
    for k, (q, dev) in enumerate(near_ids):
        pending.append(send(total.at[0:8], full.at[at(base + 8 * me)], back_out.at[k], back_sem.at[me], dev))
    pending.append(send(total.at[0:8], full.at[at(base + 8 * me)], cross_out.at[me], cross_sem.at[me], partner))
    full[at(base + 8 * me), :] = total[0:8, :]

    @pl.when(double)
    def _():
        spot = base + 8 * (cell + mine_second)
        for k, (q, dev) in enumerate(near_ids):
            send(total.at[8:16], full.at[at(spot)], rest_out.at[k], rest_sem.at[mine_second], dev)
        full[at(spot), :] = total[8:16, :]

    for q, _ in reversed(near_ids):
        tile = full.at[at(base + 8 * q)]
        arrived(tile, back_sem.at[q])
        pending.append(send(tile, tile, cross_out.at[q], cross_sem.at[q], partner))

    def rest_arrived(k, dev):
        arrived(full.at[at(base + 8 * (cell + k))], rest_sem.at[k])

    each_double(rest_arrived)
    tail = full.at[at(base + 8 * cell, rows - 8 * cell)]
    pending.append(send(tail, tail, cross_out.at[cell], cross_sem.at[cell], partner))
    other = (1 - core) * rows
    for q in range(cell):
        arrived(full.at[at(other + 8 * q)], cross_sem.at[q])
    arrived(full.at[at(other + 8 * cell, rows - 8 * cell)], cross_sem.at[cell])
    out_ref[...] = full[...]

    for copy in pending:
        copy.wait_send()
    each_double(lambda k, dev: arrived(half.at[pl.ds(8 * (cell + k), 8)], more_out.at[k]))

    @pl.when(jnp.logical_not(double))
    def _():
        for k in range(len(far_ids)):
            arrived(mine.at[0:8], far_out.at[k])

    @pl.when(double)
    def _():
        for k in range(len(far_ids)):
            arrived(mine, far_out.at[k])
        for k in range(len(near_ids)):
            arrived(total.at[8:16], rest_out.at[k])


def reduce_all(sizes, a, b, v, d, r):
    nz, ny, nx = sizes
    cell, steps = 2 * ny * nx, nz // 2
    rows = PACK // 2
    twice = rows // 8 - cell
    vmem = pl.BlockSpec(memory_space=pltpu.VMEM)
    dma = pltpu.SemaphoreType.DMA
    return pl.pallas_call(
        functools.partial(reduce_kernel, sizes),
        out_shape=jax.ShapeDtypeStruct((PACK, LANES), jnp.float32),
        in_specs=[pl.BlockSpec(memory_space=pltpu.HBM)] * 5,
        out_specs=vmem,
        scratch_shapes=[
            *(pltpu.VMEM(value.shape, jnp.float32) for value in (a, b, v, d, r)),
            dma((5,)),
            pltpu.VMEM((PACK, LANES), jnp.float32),
            pltpu.VMEM((rows, LANES), jnp.float32),
            pltpu.VMEM((rows, LANES), jnp.float32),
            pltpu.VMEM((cell, 8, LANES), jnp.float32),
            pltpu.VMEM((cell, 8, LANES), jnp.float32),
            pltpu.VMEM((16, LANES), jnp.float32),
            pltpu.VMEM((steps, 16, LANES), jnp.float32),
            pltpu.VMEM((16, LANES), jnp.float32),
            pltpu.VMEM((PACK, LANES), jnp.float32),
            dma(()), dma((cell,)), dma((cell,)), dma((steps,)), dma((cell,)), dma((twice,)), dma((cell + 1,)),
            dma(()), dma((cell,)), dma((twice,)), dma((steps,)), dma((cell,)), dma((cell,)), dma((cell + 1,)),
        ],
        compiler_params=pltpu.CompilerParams(collective_id=0, has_side_effects=True, vmem_limit_bytes=32 << 20),
    )(a, b, v, d, r)


def inverse_factor(tile, lane_in, lane_out):
    groups = BLOCK // 8
    sub = lax.broadcasted_iota(jnp.int32, (8, LANES), 0)
    lane = lax.broadcasted_iota(jnp.int32, (8, LANES), 1)
    columns = [
        {
            i: jnp.broadcast_to(tile[8 * i:8 * i + 8, lane_in + j:lane_in + j + 1], (8, LANES))
            for i in range(j // 8, groups)
        }
        for j in range(BLOCK)
    ]
    out = [jnp.where(lane == sub + (8 * i + lane_out), 1.0, 0.0) for i in range(groups)]
    for j in range(BLOCK):
        g, r = j // 8, j % 8
        scale = lax.rsqrt(columns[j][g][r:r + 1, :])
        column = {i: columns[j][i] * scale for i in range(g, groups)}
        pivot = out[g][r:r + 1, :] * scale
        for b in range(j + 1, BLOCK):
            factor = column[b // 8][b % 8:b % 8 + 1, :]
            for i in range(b // 8, groups):
                columns[b][i] = columns[b][i] - column[i] * factor
        out[g] = jnp.where(sub > r, out[g] - column[g] * pivot, jnp.where(sub == r, pivot, out[g]))
        for i in range(g + 1, groups):
            out[i] = out[i] - column[i] * pivot
    return jnp.concatenate(out, axis=0)


def largest(values):
    return jnp.max(jnp.max(values, axis=1, keepdims=True), axis=0, keepdims=True)


def diagonal(matrix):
    row = lax.broadcasted_iota(jnp.int32, matrix.shape, 0)
    lane = lax.broadcasted_iota(jnp.int32, matrix.shape, 1)
    return jnp.where(row == lane, matrix, 0.0)


def framed(rows, before, after):
    parts = [rows]
    if before:
        parts = [jnp.zeros((before, rows.shape[1]), rows.dtype)] + parts
    if after:
        parts = parts + [jnp.zeros((after, rows.shape[1]), rows.dtype)]
    return jnp.concatenate(parts, axis=0) if len(parts) > 1 else rows


def chain_kernel(red_ref, a_hbm, b_hbm, v_hbm, d_hbm, up_ref, na_ref, nb_ref, a_ref, b_ref, v_ref, d_ref, load_sem, z_ref, f_ref):
    loads = fetch((a_hbm, b_hbm, v_hbm, d_hbm), (a_ref, b_ref, v_ref, d_ref), load_sem)
    rows, width = a_ref.shape
    cols = v_ref.shape[0]
    small = red_ref[656:696, :]
    lower_inv = inverse_factor(small[:cols, :], 64, 0)[:, :cols]
    inv_v = dot(lower_inv.T, lower_inv)
    vv = small[:cols, :cols]
    gram_r = small[cols:cols + 8, 64:64 + cols]
    gram_a = unpack_pair(red_ref, 0, red_ref[696:697, :])
    gram_b = unpack_pair(red_ref, 256, red_ref[697:698, :])
    va = jnp.concatenate([red_ref[512:512 + cols, :], red_ref[512 + cols:576, :]], axis=1)
    db = jnp.concatenate([red_ref[576:616, :], red_ref[616:656, :]], axis=1)
    proj_t, proj_r = db[:cols, :], db[cols:cols + 8, :]
    scale_a = 1.0 / jnp.maximum(largest(diagonal(gram_a)), largest(diagonal(vv)))
    scale_b = 1.0 / largest(diagonal(gram_b))
    gram_a = gram_a * scale_a
    va = va * scale_a
    vv = vv * scale_a
    av = va.T
    proj = proj_t.T

    inv_v = halves(inv_v)
    w = dot(inv_v, proj_t)
    proj = halves(proj)
    wt = dot(proj, inv_v)
    ws = halves(w * scale_b)
    wst = halves(wt * scale_b)
    s = halves((gram_b - dot(proj, w)) * scale_b)
    gram_a, va, vv, av = halves(gram_a), halves(va), halves(vv), halves(av)
    k1 = halves(dot(gram_a, s) + dot(av, ws))
    k1t = dot(s, gram_a) + dot(wst, va)
    k2 = dot(va, s) + dot(vv, ws)
    k2t = dot(s, av) + dot(wst, vv)
    j1 = halves(dot(s, k1))
    c = dot(inv_v, k2)
    cs = halves(c * scale_b)
    z_ref[...] = dot(k1t, j1) + dot(k2t, cs)

    for copy in loads:
        copy.wait()
    v, d = v_ref[...], d_ref[...]
    coeffs = -dot(gram_r, inv_v)
    lead = -proj_r - dot(coeffs, proj_t)
    a = halves(a_ref[...])
    up = dot(lead, a, NT) + dot(coeffs, v)
    up_ref[...] = up[:1, :]
    root = jnp.sqrt(scale_b)
    f_ref[:rows, :] = (dot(a, j1) + dot(v.T, cs)) / root
    dn = halves(d.T)
    f_ref[rows:, :] = (dot(b_ref[...] - dot(dn, w), k1) + dot(dn, c)) * root

    for lo in range(0, width, BLOCK):
        hi = lo + BLOCK
        base = lo // LANES * LANES
        tile = slice(base, base + LANES)
        inv = inverse_factor(z_ref[lo:hi, tile], lo - base, lo - base)
        inv = halves(framed(inv, lo - base, base + LANES - hi))
        if hi < width:
            panel = halves(dot(z_ref[hi:, tile], inv, NT))
            for start in range(hi // LANES * LANES, width, LANES):
                first = max(hi, start)
                left = tuple(part[first - hi:, :] for part in panel)
                right = tuple(framed(part[first - hi:start + LANES - hi, :], first - start, 0) for part in panel)
                z_ref[first:, start:start + LANES] = z_ref[first:, start:start + LANES] - dot(left, right, NT)
        done = dot(f_ref[:, tile], inv, NT)
        if lo == base:
            na_ref[:, tile] = done[:rows, :]
            nb_ref[:, tile] = done[rows:, :]
        else:
            na_ref[:, tile] = na_ref[:, tile] + done[:rows, :]
            nb_ref[:, tile] = nb_ref[:, tile] + done[rows:, :]
        if hi < width:
            done = halves(done)
            for start in range(hi // LANES * LANES, width, LANES):
                first = max(hi, start)
                right = tuple(framed(part[first - hi:start + LANES - hi, :], first - start, 0) for part in panel)
                f_ref[:, start:start + LANES] = f_ref[:, start:start + LANES] - dot(done, right, NT)


def finish(red, a, b, v, d):
    vmem = pl.BlockSpec(memory_space=pltpu.VMEM)
    rows, width = a.shape
    return pl.pallas_call(
        chain_kernel,
        out_shape=(
            jax.ShapeDtypeStruct((1, rows), jnp.float32),
            jax.ShapeDtypeStruct((rows, width), jnp.float32),
            jax.ShapeDtypeStruct((rows, width), jnp.float32),
        ),
        in_specs=[vmem] + [pl.BlockSpec(memory_space=pltpu.HBM)] * 4,
        out_specs=(vmem,) * 3,
        scratch_shapes=[
            *(pltpu.VMEM(value.shape, jnp.float32) for value in (a, b, v, d)),
            pltpu.SemaphoreType.DMA((4,)),
            pltpu.VMEM((width, width), jnp.float32), pltpu.VMEM((2 * rows, width), jnp.float32)],
        compiler_params=pltpu.CompilerParams(vmem_limit_bytes=32 << 20),
    )(red, a, b, v, d)


def solution(mesh):
    nx = mesh.shape["sub"]
    sizes = (mesh.shape["rows"] // (2 * nx), nx, nx)

    def on_device(a, b, v, d, r):
        hbm = lambda value: pltpu.with_memory_space_constraint(value, pltpu.HBM)
        a, b, vt, dt, rt = hbm(a), hbm(b), hbm(v.T), hbm(d.T), hbm(r.reshape(1, -1))
        red = reduce_all(sizes, a, b, vt, dt, rt)
        up, new_a, new_b = finish(red, a, b, vt, dt)
        return up.reshape(-1), new_a, new_b

    spread = P(("rows", "sub"))
    wide = P(("rows", "sub"), None)
    return jax.shard_map(
        on_device, mesh=mesh, in_specs=(wide,) * 4 + (spread,), out_specs=(spread, wide, wide), check_vma=False
    )
```

```python
import functools

import jax
import jax.numpy as jnp
from jax import lax
from jax.experimental import pallas as pl
from jax.experimental.pallas import tpu as pltpu
from jax.sharding import PartitionSpec as P

MESH = pl.DeviceIdType.MESH
LANES = 128
PACK = 704
BLOCK = 32

NN = (((1,), (0,)), ((), ()))
NT = (((1,), (1,)), ((), ()))
TN = (((0,), (0,)), ((), ()))


def halves(value):
    high = value.astype(jnp.bfloat16)
    return high, (value - high.astype(jnp.float32)).astype(jnp.bfloat16)


def dot(left, right, dims=NN):
    left = left if isinstance(left, tuple) else halves(left)
    right = right if isinstance(right, tuple) else halves(right)

    def one(l, r):
        return lax.dot_general(l, r, dims, preferred_element_type=jnp.float32)

    return one(left[0], right[0]) + (one(left[0], right[1]) + one(left[1], right[0]))


def gram_pair(value, out_ref, base):
    turned = value.T
    whole, first = halves(value), halves(turned[:LANES, :])
    return pack_pair(
        dot(first, tuple(part[:, :LANES] for part in whole)), dot(turned[LANES:, :], whole), out_ref, base
    )


def pack_pair(first, below, out_ref, base):
    row = lax.broadcasted_iota(jnp.int32, (LANES, LANES), 0)
    lane = lax.broadcasted_iota(jnp.int32, (LANES, LANES), 1)
    last = below[:, LANES:]
    out_ref[base:base + LANES, :] = jnp.where(row >= lane, first, last)
    out_ref[base + LANES:base + 2 * LANES, :] = below[:, :LANES]
    return jnp.sum(jnp.where(row == lane, last, 0.0), axis=0, keepdims=True)


def unpack_pair(red_ref, base, diag):
    row = lax.broadcasted_iota(jnp.int32, (LANES, LANES), 0)
    lane = lax.broadcasted_iota(jnp.int32, (LANES, LANES), 1)
    both = red_ref[base:base + LANES, :]
    turned = both.T
    low = red_ref[base + LANES:base + 2 * LANES, :]
    first = jnp.where(row >= lane, both, turned)
    last = jnp.where(row < lane, both, jnp.where(row > lane, turned, diag))
    return jnp.concatenate(
        [jnp.concatenate([first, low.T], axis=1), jnp.concatenate([low, last], axis=1)], axis=0
    )


def fetch(sources, targets, sems):
    copies = [pltpu.make_async_copy(src, dst, sems.at[k]) for k, (src, dst) in enumerate(zip(sources, targets))]
    for copy in copies:
        copy.start()
    return copies


def reduce_kernel(sizes, a_hbm, b_hbm, v_hbm, d_hbm, r_hbm, out_ref, a_ref, b_ref, v_ref, d_ref, r_ref, load_sem,
                  local, pair, half, near, more, mine, far, total, full,
                  pair_sem, near_sem, more_sem, far_sem, back_sem, rest_sem, cross_sem,
                  pair_out, near_out, more_out, far_out, back_out, rest_out, cross_out):
    nz, ny, nx = sizes
    rows = PACK // 2
    plane = ny * nx
    cell = 2 * plane
    steps = nz // 2
    place = lax.axis_index("rows")
    x = lax.axis_index("sub")
    core = lax.rem(place, 2)
    y = lax.rem(place // 2, ny)
    z = place // (2 * ny)
    side, step = lax.rem(z, 2), z // 2
    me = side * plane + y * nx + x
    near_ids = []
    for dz in range(2):
        for dy in range(ny):
            for dx in range(nx):
                if dz or dy or dx:
                    qz, qy, qx = lax.rem(side + dz, 2), lax.rem(y + dy, ny), lax.rem(x + dx, nx)
                    hops = dz + min(dy, ny - dy) + min(dx, nx - dx)
                    dev = (((2 * step + qz) * ny + qy) * 2 + core, qx)
                    near_ids.append((hops, len(near_ids), qz * plane + qy * nx + qx, dev))
    near_ids = [item[2:] for item in sorted(near_ids, key=lambda item: (-item[0], item[1]))]
    far_ids = []
    for dz in sorted(range(1, steps), key=lambda d: -min(d, steps - d)):
        qz = lax.rem(step + dz, steps)
        far_ids.append((qz, ((2 * (2 * ny) * qz + 2 * ny * side) + 2 * y + core, x)))
    partner = (place + 1 - 2 * core, x)
    doubles = [(0, qy, qx) for qy in range(ny) for qx in range(nx) if (qx + qy) % 2 == 0]
    doubles += [(1, qy, qx) for qy in range(ny) for qx in range(nx) if (qx + qy) % 4 == 1]
    even = side == 0
    double = (even & (lax.rem(x + y, 2) == 0)) | ((side == 1) & (lax.rem(x + y, 4) == 1))
    mine_second = jnp.where(even, y * (nx // 2) + x // 2, plane // 2 + y)

    loads = fetch((b_hbm, d_hbm, r_hbm, a_hbm, v_hbm), (b_ref, d_ref, r_ref, a_ref, v_ref), load_sem)
    barrier = pltpu.get_barrier_semaphore()
    for _, dev in far_ids:
        pl.semaphore_signal(barrier, inc=1, device_id=dev, device_id_type=MESH)
    for _, dev in near_ids:
        pl.semaphore_signal(barrier, inc=1, device_id=dev, device_id_type=MESH)
    pl.semaphore_signal(barrier, inc=1, device_id=partner, device_id_type=MESH)

    cols = v_ref.shape[0]
    for copy in loads[:3]:
        copy.wait()
    diag_b = gram_pair(b_ref[...], local, 2 * LANES)
    d = d_ref[...]
    left = halves(jnp.concatenate([d, jnp.broadcast_to(r_ref[...], (8, d.shape[1]))], axis=0))
    db = dot(left, b_ref[...])
    dd = dot(left, d, NT)
    for copy in loads[3:]:
        copy.wait()
    diag_a = gram_pair(a_ref[...], local, 0)
    v = halves(v_ref[...])
    va = dot(v, a_ref[...])
    vv = dot(v, v, NT)
    local[512:512 + cols, :] = va[:, :LANES]
    local[512 + cols:576, :] = va[:, LANES:]
    local[576:616, :] = db[:, :LANES]
    local[616:656, :] = db[:, LANES:]
    local[656:696, :] = jnp.zeros((40, LANES), jnp.float32)
    local[656:656 + cols, 0:cols] = vv
    local[656:696, 64:64 + cols] = dd
    local[696:704, :] = jnp.zeros((8, LANES), jnp.float32)
    local[696:697, :] = diag_a
    local[697:698, :] = diag_b

    pl.semaphore_wait(barrier, len(far_ids) + len(near_ids) + 1)

    def send(src, dst, out_sem, in_sem, dev):
        copy = pltpu.make_async_remote_copy(
            src_ref=src, dst_ref=dst, send_sem=out_sem, recv_sem=in_sem, device_id=dev, device_id_type=MESH
        )
        copy.start()
        return copy

    def arrived(ref, sem):
        pltpu.make_async_copy(ref, ref, sem).wait()

    pending = []

    def at(start, size=8):
        return pl.ds(pl.multiple_of(start, 8), size)

    def each_double(action):
        for k, (qz, qy, qx) in enumerate(doubles):

            @pl.when(me != qz * plane + qy * nx + qx)
            def _():
                action(k, (((2 * step + qz) * ny + qy) * 2 + core, qx))

    pending.append(send(local.at[at((1 - core) * rows, rows)], pair, pair_out, pair_sem, partner))
    arrived(pair, pair_sem)
    half[...] = local[at(core * rows, rows), :] + pair[...]

    for k, (q, dev) in enumerate(near_ids):
        pending.append(send(half.at[at(8 * q)], near.at[me], near_out.at[k], near_sem.at[me], dev))
    each_double(lambda k, dev: send(half.at[pl.ds(8 * (cell + k), 8)], more.at[me], more_out.at[k], more_sem.at[me], dev))
    value = half[at(8 * me), :]
    for q, _ in reversed(near_ids):
        arrived(near.at[q], near_sem.at[q])
        value = value + near[q]
    mine[0:8, :] = value

    @pl.when(jnp.logical_not(double))
    def _():
        for k, (q, dev) in enumerate(far_ids):
            send(mine.at[0:8], far.at[step, 0:8], far_out.at[k], far_sem.at[step], dev)
        far[step, 0:8] = mine[0:8, :]
        for q, _ in reversed(far_ids):
            arrived(far.at[q, 0:8], far_sem.at[q])
        value = far[0, 0:8]
        for k in range(1, steps):
            value = value + far[k, 0:8]
        total[0:8, :] = value

    @pl.when(double)
    def _():
        value = half[at(8 * (cell + mine_second)), :]
        for q, _ in reversed(near_ids):
            arrived(more.at[q], more_sem.at[q])
            value = value + more[q]
        mine[8:16, :] = value
        for k, (q, dev) in enumerate(far_ids):
            send(mine, far.at[step], far_out.at[k], far_sem.at[step], dev)
        far[step] = mine[...]
        for q, _ in reversed(far_ids):
            arrived(far.at[q], far_sem.at[q])
        value = far[0]
        for k in range(1, steps):
            value = value + far[k]
        total[...] = value

    base = core * rows
    for k, (q, dev) in enumerate(near_ids):
        pending.append(send(total.at[0:8], full.at[at(base + 8 * me)], back_out.at[k], back_sem.at[me], dev))
    pending.append(send(total.at[0:8], full.at[at(base + 8 * me)], cross_out.at[me], cross_sem.at[me], partner))
    full[at(base + 8 * me), :] = total[0:8, :]

    @pl.when(double)
    def _():
        spot = base + 8 * (cell + mine_second)
        for k, (q, dev) in enumerate(near_ids):
            send(total.at[8:16], full.at[at(spot)], rest_out.at[k], rest_sem.at[mine_second], dev)
        full[at(spot), :] = total[8:16, :]

    for q, _ in reversed(near_ids):
        tile = full.at[at(base + 8 * q)]
        arrived(tile, back_sem.at[q])
        pending.append(send(tile, tile, cross_out.at[q], cross_sem.at[q], partner))

    def rest_arrived(k, dev):
        arrived(full.at[at(base + 8 * (cell + k))], rest_sem.at[k])

    each_double(rest_arrived)
    tail = full.at[at(base + 8 * cell, rows - 8 * cell)]
    pending.append(send(tail, tail, cross_out.at[cell], cross_sem.at[cell], partner))
    other = (1 - core) * rows
    for q in range(cell):
        arrived(full.at[at(other + 8 * q)], cross_sem.at[q])
    arrived(full.at[at(other + 8 * cell, rows - 8 * cell)], cross_sem.at[cell])
    out_ref[...] = full[...]

    for copy in pending:
        copy.wait_send()
    each_double(lambda k, dev: arrived(half.at[pl.ds(8 * (cell + k), 8)], more_out.at[k]))

    @pl.when(jnp.logical_not(double))
    def _():
        for k in range(len(far_ids)):
            arrived(mine.at[0:8], far_out.at[k])

    @pl.when(double)
    def _():
        for k in range(len(far_ids)):
            arrived(mine, far_out.at[k])
        for k in range(len(near_ids)):
            arrived(total.at[8:16], rest_out.at[k])


def reduce_all(sizes, a, b, v, d, r):
    nz, ny, nx = sizes
    cell, steps = 2 * ny * nx, nz // 2
    rows = PACK // 2
    twice = rows // 8 - cell
    vmem = pl.BlockSpec(memory_space=pltpu.VMEM)
    dma = pltpu.SemaphoreType.DMA
    return pl.pallas_call(
        functools.partial(reduce_kernel, sizes),
        out_shape=jax.ShapeDtypeStruct((PACK, LANES), jnp.float32),
        in_specs=[pl.BlockSpec(memory_space=pltpu.HBM)] * 5,
        out_specs=vmem,
        scratch_shapes=[
            *(pltpu.VMEM(value.shape, jnp.float32) for value in (a, b, v, d, r)),
            dma((5,)),
            pltpu.VMEM((PACK, LANES), jnp.float32),
            pltpu.VMEM((rows, LANES), jnp.float32),
            pltpu.VMEM((rows, LANES), jnp.float32),
            pltpu.VMEM((cell, 8, LANES), jnp.float32),
            pltpu.VMEM((cell, 8, LANES), jnp.float32),
            pltpu.VMEM((16, LANES), jnp.float32),
            pltpu.VMEM((steps, 16, LANES), jnp.float32),
            pltpu.VMEM((16, LANES), jnp.float32),
            pltpu.VMEM((PACK, LANES), jnp.float32),
            dma(()), dma((cell,)), dma((cell,)), dma((steps,)), dma((cell,)), dma((twice,)), dma((cell + 1,)),
            dma(()), dma((cell,)), dma((twice,)), dma((steps,)), dma((cell,)), dma((cell,)), dma((cell + 1,)),
        ],
        compiler_params=pltpu.CompilerParams(collective_id=0, has_side_effects=True, vmem_limit_bytes=32 << 20),
    )(a, b, v, d, r)


def eliminate(tile, offset, carried):
    groups = BLOCK // 8
    sub = lax.broadcasted_iota(jnp.int32, (8, LANES), 0)
    columns = [
        {
            i: jnp.broadcast_to(tile[8 * i:8 * i + 8, offset + j:offset + j + 1], (8, LANES))
            for i in range(j // 8, groups)
        }
        for j in range(BLOCK)
    ]
    carried = [[part[8 * i:8 * i + 8, :] for i in range(groups)] for part in carried]
    for j in range(BLOCK):
        g, r = j // 8, j % 8
        scale = lax.rsqrt(columns[j][g][r:r + 1, :])
        column = {i: columns[j][i] * scale for i in range(g, groups)}
        for b in range(j + 1, BLOCK):
            factor = column[b // 8][b % 8:b % 8 + 1, :]
            for i in range(b // 8, groups):
                columns[b][i] = columns[b][i] - column[i] * factor
        below = jnp.where(sub > r, column[g], 0.0)
        for out in carried:
            pivot = out[g][r:r + 1, :] * scale
            out[g] = jnp.where(sub == r, pivot, out[g] - below * pivot)
            for i in range(g + 1, groups):
                out[i] = out[i] - column[i] * pivot
    return [jnp.concatenate(out, axis=0) for out in carried]


def identity_at(offset):
    row = lax.broadcasted_iota(jnp.int32, (BLOCK, LANES), 0)
    lane = lax.broadcasted_iota(jnp.int32, (BLOCK, LANES), 1)
    return jnp.where(lane == row + offset, 1.0, 0.0)


def largest(values):
    return jnp.max(jnp.max(values, axis=1, keepdims=True), axis=0, keepdims=True)


def diagonal(matrix):
    row = lax.broadcasted_iota(jnp.int32, matrix.shape, 0)
    lane = lax.broadcasted_iota(jnp.int32, matrix.shape, 1)
    return jnp.where(row == lane, matrix, 0.0)


def chain_kernel(red_ref, a_hbm, b_hbm, v_hbm, d_hbm, up_ref, na_ref, nb_ref, a_ref, b_ref, v_ref, d_ref, load_sem, z_ref, y_ref, x_ref):
    loads = fetch((a_hbm, b_hbm, v_hbm, d_hbm), (a_ref, b_ref, v_ref, d_ref), load_sem)
    rows, width = a_ref.shape
    cols = v_ref.shape[0]
    small = red_ref[656:696, :]
    va = jnp.concatenate([red_ref[512:512 + cols, :], red_ref[512 + cols:576, :]], axis=1)
    db = jnp.concatenate([red_ref[576:616, :], red_ref[616:656, :]], axis=1)
    proj_t, proj_r = db[:cols, :], db[cols:cols + 8, :]
    solved = eliminate(small[:cols, :], 64, [identity_at(0), proj_t[:, :LANES], proj_t[:, LANES:]])
    low = solved[0][:, :cols]
    low_t, low = halves(low.T), halves(low)
    half = jnp.concatenate(solved[1:], axis=1)
    half_t, half = halves(half.T), halves(half)
    vv = small[:cols, :cols]
    gram_r = small[cols:cols + 8, 64:64 + cols]
    gram_a = unpack_pair(red_ref, 0, red_ref[696:697, :])
    gram_b = unpack_pair(red_ref, 256, red_ref[697:698, :])
    scale_a = 1.0 / jnp.maximum(largest(diagonal(gram_a)), largest(diagonal(vv)))
    scale_b = 1.0 / largest(diagonal(gram_b))
    gram_a = halves(gram_a * scale_a)
    va = va * scale_a
    vv = halves(vv * scale_a)
    av, va = halves(va.T), halves(va)

    s = halves((gram_b - dot(half_t, half)) * scale_b)
    w = dot(low_t, half)
    ws = halves(w * scale_b)
    wst = halves(dot(half_t, low) * scale_b)
    inv_v = halves(dot(low_t, low))
    k1 = halves(dot(gram_a, s) + dot(av, ws))
    k1t = halves(dot(s, gram_a) + dot(wst, va))
    k2 = dot(va, s) + dot(vv, ws)
    k2t = halves(dot(s, av) + dot(wst, vv))
    j1 = halves(dot(s, k1))
    c = dot(inv_v, k2)
    cs = halves(c * scale_b)

    def rows_of(pair, start, stop):
        return tuple(part[start:stop, :] for part in pair)

    def lanes_of(pair, start):
        return tuple(part[:, start:start + LANES] for part in pair)

    z_ref[:LANES, :] = dot(rows_of(k1t, 0, LANES), j1) + dot(rows_of(k2t, 0, LANES), cs)
    z_ref[LANES:, LANES:] = dot(rows_of(k1t, LANES, width), lanes_of(j1, LANES)) + dot(
        rows_of(k2t, LANES, width), lanes_of(cs, LANES)
    )
    row = lax.broadcasted_iota(jnp.int32, (width, width), 0)
    column = lax.broadcasted_iota(jnp.int32, (width, width), 1)
    y_ref[...] = jnp.where(row == column, 1.0, 0.0)
    lane = lax.broadcasted_iota(jnp.int32, (BLOCK, LANES), 1)
    root = jnp.sqrt(scale_b)
    fronts = []

    for lo in range(0, width, BLOCK):
        hi = lo + BLOCK
        base = lo // LANES * LANES
        own = slice(base, base + LANES)
        offset = lo - base
        block = z_ref[lo:hi, own]
        inside = (lane >= offset) & (lane < offset + BLOCK)
        carried = [jnp.where(inside, identity_at(offset), block)]
        carried += [z_ref[lo:hi, start:start + LANES] for start in range(base + LANES, width, LANES)]
        carried = eliminate(block, offset, carried)
        inv = halves(jnp.where(inside, carried[0], 0.0))
        right = {start: halves(part) for start, part in zip(range(base, width, LANES), carried) if start + LANES > hi}
        left = {start: halves(part.T) for start, part in zip(range(base, width, LANES), carried) if start + LANES > hi}
        if hi < width:
            first = hi // LANES * LANES
            near = rows_of(left[first], hi - first, hi - first + BLOCK)
            for start in right:
                tile = slice(start, start + LANES)
                z_ref[hi:hi + BLOCK, tile] = z_ref[hi:hi + BLOCK, tile] - dot(near, right[start])
        solved = dot(inv, y_ref[own, :base + LANES])
        x_ref[lo:hi, :base + LANES] = solved
        if base + LANES < width:
            x_ref[lo:hi, base + LANES:] = jnp.zeros((BLOCK, width - base - LANES), jnp.float32)
        solved = halves(solved)
        for start in right:
            top = max(hi, start)
            part = rows_of(left[start], top - start, LANES)
            y_ref[top:start + LANES, :base + LANES] = y_ref[top:start + LANES, :base + LANES] - dot(part, solved)
            top = max(hi + BLOCK, start)
            if top < start + LANES:
                part = rows_of(left[start], top - start, LANES)
                for other in right:
                    if other >= start:
                        tile = slice(other, other + LANES)
                        z_ref[top:start + LANES, tile] = z_ref[top:start + LANES, tile] - dot(part, right[other])

        if lo == 0:
            for copy in loads:
                copy.wait()
            coeffs = -dot(gram_r, inv_v)
            lead = -proj_r - dot(coeffs, proj_t)
            a = halves(a_ref[...])
            up = dot(lead, a, NT) + dot(coeffs, v_ref[...])
            up_ref[...] = up[:1, :]
            fronts.append(halves((dot(a, j1) + dot(v_ref[...].T, cs)) / root))
        if lo == BLOCK:
            d = halves(d_ref[...].T)
            fronts.append(halves((dot(b_ref[...] - dot(d, w), k1) + dot(d, c)) * root))
        if hi % LANES == 0:
            back = halves(x_ref[own, :])
            na_ref[:, own] = dot(fronts[0], back, NT)
            nb_ref[:, own] = dot(fronts[1], back, NT)


def finish(red, a, b, v, d):
    vmem = pl.BlockSpec(memory_space=pltpu.VMEM)
    rows, width = a.shape
    return pl.pallas_call(
        chain_kernel,
        out_shape=(
            jax.ShapeDtypeStruct((1, rows), jnp.float32),
            jax.ShapeDtypeStruct((rows, width), jnp.float32),
            jax.ShapeDtypeStruct((rows, width), jnp.float32),
        ),
        in_specs=[vmem] + [pl.BlockSpec(memory_space=pltpu.HBM)] * 4,
        out_specs=(vmem,) * 3,
        scratch_shapes=[
            *(pltpu.VMEM(value.shape, jnp.float32) for value in (a, b, v, d)),
            pltpu.SemaphoreType.DMA((4,)),
            pltpu.VMEM((width, width), jnp.float32), pltpu.VMEM((width, width), jnp.float32),
            pltpu.VMEM((width, width), jnp.float32)],
        compiler_params=pltpu.CompilerParams(vmem_limit_bytes=32 << 20),
    )(red, a, b, v, d)


def solution(mesh):
    nx = mesh.shape["sub"]
    sizes = (mesh.shape["rows"] // (2 * nx), nx, nx)

    def on_device(a, b, v, d, r):
        hbm = lambda value: pltpu.with_memory_space_constraint(value, pltpu.HBM)
        a, b, vt, dt, rt = hbm(a), hbm(b), hbm(v.T), hbm(d.T), hbm(r.reshape(1, -1))
        red = reduce_all(sizes, a, b, vt, dt, rt)
        up, new_a, new_b = finish(red, a, b, vt, dt)
        return up.reshape(-1), new_a, new_b

    spread = P(("rows", "sub"))
    wide = P(("rows", "sub"), None)
    return jax.shard_map(
        on_device, mesh=mesh, in_specs=(wide,) * 4 + (spread,), out_specs=(spread, wide, wide), check_vma=False
    )
```

```python
import functools

import jax
import jax.numpy as jnp
from jax import lax
from jax.experimental import pallas as pl
from jax.experimental.pallas import tpu as pltpu
from jax.sharding import PartitionSpec as P

MESH = pl.DeviceIdType.MESH
LANES = 128
PACK = 704
BLOCK = 32

NN = (((1,), (0,)), ((), ()))
NT = (((1,), (1,)), ((), ()))
TN = (((0,), (0,)), ((), ()))


def halves(value):
    high = value.astype(jnp.bfloat16)
    return high, (value - high.astype(jnp.float32)).astype(jnp.bfloat16)


def dot(left, right, dims=NN):
    left = left if isinstance(left, tuple) else halves(left)
    right = right if isinstance(right, tuple) else halves(right)

    def one(l, r):
        return lax.dot_general(l, r, dims, preferred_element_type=jnp.float32)

    return one(left[0], right[0]) + (one(left[0], right[1]) + one(left[1], right[0]))


def gram_pair(value, out_ref, base):
    turned = value.T
    whole, first = halves(value), halves(turned[:LANES, :])
    return pack_pair(
        dot(first, tuple(part[:, :LANES] for part in whole)), dot(turned[LANES:, :], whole), out_ref, base
    )


def pack_pair(first, below, out_ref, base):
    row = lax.broadcasted_iota(jnp.int32, (LANES, LANES), 0)
    lane = lax.broadcasted_iota(jnp.int32, (LANES, LANES), 1)
    last = below[:, LANES:]
    out_ref[base:base + LANES, :] = jnp.where(row >= lane, first, last)
    out_ref[base + LANES:base + 2 * LANES, :] = below[:, :LANES]
    return jnp.sum(jnp.where(row == lane, last, 0.0), axis=0, keepdims=True)


def unpack_pair(red_ref, base, diag):
    row = lax.broadcasted_iota(jnp.int32, (LANES, LANES), 0)
    lane = lax.broadcasted_iota(jnp.int32, (LANES, LANES), 1)
    both = red_ref[base:base + LANES, :]
    turned = both.T
    low = red_ref[base + LANES:base + 2 * LANES, :]
    first = jnp.where(row >= lane, both, turned)
    last = jnp.where(row < lane, both, jnp.where(row > lane, turned, diag))
    return jnp.concatenate(
        [jnp.concatenate([first, low.T], axis=1), jnp.concatenate([low, last], axis=1)], axis=0
    )


def fetch(sources, targets, sems):
    copies = [pltpu.make_async_copy(src, dst, sems.at[k]) for k, (src, dst) in enumerate(zip(sources, targets))]
    for copy in copies:
        copy.start()
    return copies


def reduce_kernel(sizes, a_hbm, b_hbm, v_hbm, d_hbm, r_hbm, out_ref, a_ref, b_ref, v_ref, d_ref, r_ref, load_sem,
                  local, pair, half, near, more, mine, far, total, full,
                  pair_sem, near_sem, more_sem, far_sem, back_sem, rest_sem, cross_sem,
                  pair_out, near_out, more_out, far_out, back_out, rest_out, cross_out):
    nz, ny, nx = sizes
    rows = PACK // 2
    plane = ny * nx
    cell = 2 * plane
    steps = nz // 2
    place = lax.axis_index("rows")
    x = lax.axis_index("sub")
    core = lax.rem(place, 2)
    y = lax.rem(place // 2, ny)
    z = place // (2 * ny)
    side, step = lax.rem(z, 2), z // 2
    me = side * plane + y * nx + x
    near_ids = []
    for dz in range(2):
        for dy in range(ny):
            for dx in range(nx):
                if dz or dy or dx:
                    qz, qy, qx = lax.rem(side + dz, 2), lax.rem(y + dy, ny), lax.rem(x + dx, nx)
                    hops = dz + min(dy, ny - dy) + min(dx, nx - dx)
                    dev = (((2 * step + qz) * ny + qy) * 2 + core, qx)
                    near_ids.append((hops, len(near_ids), qz * plane + qy * nx + qx, dev))
    near_ids = sorted(near_ids, key=lambda item: (-item[0], item[1]))
    rings = [[(q, dev) for hops, _, q, dev in near_ids if hops == ring] for ring in range(1, near_ids[0][0] + 1)]
    near_ids = [(hops - 1, q, dev) for hops, _, q, dev in near_ids]
    far_ids = []
    for dz in sorted(range(1, steps), key=lambda d: -min(d, steps - d)):
        qz = lax.rem(step + dz, steps)
        far_ids.append((qz, ((2 * (2 * ny) * qz + 2 * ny * side) + 2 * y + core, x)))
    partner = (place + 1 - 2 * core, x)
    doubles = [(0, qy, qx) for qy in range(ny) for qx in range(nx) if (qx + qy) % 2 == 0]
    doubles += [(1, qy, qx) for qy in range(ny) for qx in range(nx) if (qx + qy) % 4 == 1]
    even = side == 0
    double = (even & (lax.rem(x + y, 2) == 0)) | ((side == 1) & (lax.rem(x + y, 4) == 1))
    mine_second = jnp.where(even, y * (nx // 2) + x // 2, plane // 2 + y)

    loads = fetch((b_hbm, d_hbm, r_hbm, a_hbm, v_hbm), (b_ref, d_ref, r_ref, a_ref, v_ref), load_sem)
    barrier = pltpu.get_barrier_semaphore()
    for _, dev in far_ids:
        pl.semaphore_signal(barrier, inc=1, device_id=dev, device_id_type=MESH)
    for _, _, dev in near_ids:
        pl.semaphore_signal(barrier, inc=1, device_id=dev, device_id_type=MESH)
    pl.semaphore_signal(barrier, inc=1, device_id=partner, device_id_type=MESH)

    cols = v_ref.shape[0]
    for copy in loads[:3]:
        copy.wait()
    diag_b = gram_pair(b_ref[...], local, 2 * LANES)
    d = d_ref[...]
    left = halves(jnp.concatenate([d, jnp.broadcast_to(r_ref[...], (8, d.shape[1]))], axis=0))
    db = dot(left, b_ref[...])
    dd = dot(left, d, NT)
    for copy in loads[3:]:
        copy.wait()
    diag_a = gram_pair(a_ref[...], local, 0)
    v = halves(v_ref[...])
    va = dot(v, a_ref[...])
    vv = dot(v, v, NT)
    local[512:512 + cols, :] = va[:, :LANES]
    local[512 + cols:576, :] = va[:, LANES:]
    local[576:616, :] = db[:, :LANES]
    local[616:656, :] = db[:, LANES:]
    local[656:696, :] = jnp.zeros((40, LANES), jnp.float32)
    local[656:656 + cols, 0:cols] = vv
    local[656:696, 64:64 + cols] = dd
    local[696:704, :] = jnp.zeros((8, LANES), jnp.float32)
    local[696:697, :] = diag_a
    local[697:698, :] = diag_b

    pl.semaphore_wait(barrier, len(far_ids) + len(near_ids) + 1)

    def send(src, dst, out_sem, in_sem, dev):
        pltpu.make_async_remote_copy(
            src_ref=src, dst_ref=dst, send_sem=out_sem, recv_sem=in_sem, device_id=dev, device_id_type=MESH
        ).start()

    def arrived(ref, sem):
        pltpu.make_async_copy(ref, ref, sem).wait()

    def at(start, size=8):
        return pl.ds(pl.multiple_of(start, 8), size)

    def wait_tiles(count, sem):
        arrived(full.at[pl.ds(0, 8 * count)], sem)

    def each_double(action):
        for k, (qz, qy, qx) in enumerate(doubles):

            @pl.when(me != qz * plane + qy * nx + qx)
            def _():
                action(k, (((2 * step + qz) * ny + qy) * 2 + core, qx))

    others, lines = cell - 1, steps - 1
    single = jnp.logical_not(double)

    send(local.at[at((1 - core) * rows, rows)], pair, pair_out, pair_sem, partner)
    arrived(pair, pair_sem)
    half[...] = local[at(core * rows, rows), :] + pair[...]

    for _, q, dev in near_ids:
        send(half.at[at(8 * q)], near.at[me], near_out, near_sem, dev)
    each_double(lambda k, dev: send(half.at[pl.ds(8 * (cell + k), 8)], more.at[me], more_out, more_sem, dev))
    arrived(pair, pair_out)
    near[me] = half[at(8 * me), :]
    wait_tiles(others, near_sem)
    mine[0:8, :] = jnp.sum(near[...], axis=0)

    @pl.when(single)
    def _():
        for q, dev in far_ids:
            send(mine.at[0:8], far.at[step, 0:8], far_out, far_sem, dev)
        far[step, 0:8] = mine[0:8, :]
        wait_tiles(others, near_out)
        wait_tiles(len(doubles), more_out)
        wait_tiles(lines, far_sem)
        total[0:8, :] = jnp.sum(far[:, 0:8, :], axis=0)

    @pl.when(double)
    def _():
        more[me] = half[at(8 * (cell + mine_second)), :]
        wait_tiles(others, more_sem)
        mine[8:16, :] = jnp.sum(more[...], axis=0)
        for q, dev in far_ids:
            send(mine, far.at[step], far_out, far_sem, dev)
        far[step] = mine[...]
        wait_tiles(others, near_out)
        wait_tiles(len(doubles) - 1, more_out)
        wait_tiles(2 * lines, far_sem)
        total[...] = jnp.sum(far[...], axis=0)

    base = core * rows
    for ring, q, dev in near_ids:
        send(total.at[0:8], full.at[at(base + 8 * me)], back_out, back_sem.at[ring], dev)
    send(total.at[0:8], full.at[at(base + 8 * me)], cross_out, cross_sem, partner)
    full[at(base + 8 * me), :] = total[0:8, :]

    @pl.when(double)
    def _():
        spot = base + 8 * (cell + mine_second)
        for _, q, dev in near_ids:
            send(total.at[8:16], full.at[at(spot)], rest_out, rest_sem, dev)
        send(total.at[8:16], full.at[at(spot)], cross_out, cross_sem, partner)
        full[at(spot), :] = total[8:16, :]
        wait_tiles(2 * lines, far_out)

    @pl.when(single)
    def _():
        wait_tiles(lines, far_out)

    for ring, members in enumerate(rings):
        wait_tiles(len(members), back_sem.at[ring])
        for q, dev in members:
            tile = full.at[at(base + 8 * q)]
            send(tile, tile, cross_out, cross_sem, partner)

    @pl.when(single)
    def _():
        wait_tiles(len(doubles), rest_sem)

    @pl.when(double)
    def _():
        wait_tiles(len(doubles) - 1, rest_sem)

    def forward(k, dev):
        tile = full.at[at(base + 8 * (cell + k))]
        send(tile, tile, cross_out, cross_sem, partner)

    each_double(forward)
    wait_tiles(others, back_out)

    @pl.when(double)
    def _():
        wait_tiles(others, rest_out)

    arrived(full.at[at((1 - core) * rows, rows)], cross_sem)
    arrived(full.at[at(base, rows)], cross_out)
    out_ref[...] = full[...]


def reduce_all(sizes, a, b, v, d, r):
    nz, ny, nx = sizes
    cell, steps = 2 * ny * nx, nz // 2
    rows = PACK // 2
    twice = rows // 8 - cell
    vmem = pl.BlockSpec(memory_space=pltpu.VMEM)
    dma = pltpu.SemaphoreType.DMA
    return pl.pallas_call(
        functools.partial(reduce_kernel, sizes),
        out_shape=jax.ShapeDtypeStruct((PACK, LANES), jnp.float32),
        in_specs=[pl.BlockSpec(memory_space=pltpu.HBM)] * 5,
        out_specs=vmem,
        scratch_shapes=[
            *(pltpu.VMEM(value.shape, jnp.float32) for value in (a, b, v, d, r)),
            dma((5,)),
            pltpu.VMEM((PACK, LANES), jnp.float32),
            pltpu.VMEM((rows, LANES), jnp.float32),
            pltpu.VMEM((rows, LANES), jnp.float32),
            pltpu.VMEM((cell, 8, LANES), jnp.float32),
            pltpu.VMEM((cell, 8, LANES), jnp.float32),
            pltpu.VMEM((16, LANES), jnp.float32),
            pltpu.VMEM((steps, 16, LANES), jnp.float32),
            pltpu.VMEM((16, LANES), jnp.float32),
            pltpu.VMEM((PACK, LANES), jnp.float32),
            dma(()), dma(()), dma(()), dma(()), dma((8,)), dma(()), dma(()),
            *(dma(()) for _ in range(7)),
        ],
        compiler_params=pltpu.CompilerParams(collective_id=0, has_side_effects=True, vmem_limit_bytes=32 << 20),
    )(a, b, v, d, r)


def eliminate(tile, offset, carried):
    groups = BLOCK // 8
    sub = lax.broadcasted_iota(jnp.int32, (8, LANES), 0)
    columns = [
        {
            i: jnp.broadcast_to(tile[8 * i:8 * i + 8, offset + j:offset + j + 1], (8, LANES))
            for i in range(j // 8, groups)
        }
        for j in range(BLOCK)
    ]
    carried = [[part[8 * i:8 * i + 8, :] for i in range(groups)] for part in carried]
    for j in range(BLOCK):
        g, r = j // 8, j % 8
        scale = lax.rsqrt(columns[j][g][r:r + 1, :])
        column = {i: columns[j][i] * scale for i in range(g, groups)}
        for b in range(j + 1, BLOCK):
            factor = column[b // 8][b % 8:b % 8 + 1, :]
            for i in range(b // 8, groups):
                columns[b][i] = columns[b][i] - column[i] * factor
        below = jnp.where(sub > r, column[g], 0.0)
        for out in carried:
            pivot = out[g][r:r + 1, :] * scale
            out[g] = jnp.where(sub == r, pivot, out[g] - below * pivot)
            for i in range(g + 1, groups):
                out[i] = out[i] - column[i] * pivot
    return [jnp.concatenate(out, axis=0) for out in carried]


def identity_at(offset):
    row = lax.broadcasted_iota(jnp.int32, (BLOCK, LANES), 0)
    lane = lax.broadcasted_iota(jnp.int32, (BLOCK, LANES), 1)
    return jnp.where(lane == row + offset, 1.0, 0.0)


def largest(values):
    return jnp.max(jnp.max(values, axis=1, keepdims=True), axis=0, keepdims=True)


def diagonal(matrix):
    row = lax.broadcasted_iota(jnp.int32, matrix.shape, 0)
    lane = lax.broadcasted_iota(jnp.int32, matrix.shape, 1)
    return jnp.where(row == lane, matrix, 0.0)


def chain_kernel(red_ref, a_hbm, b_hbm, v_hbm, d_hbm, up_ref, na_ref, nb_ref, a_ref, b_ref, v_ref, d_ref, load_sem, z_ref, y_ref, x_ref):
    loads = fetch((a_hbm, b_hbm, v_hbm, d_hbm), (a_ref, b_ref, v_ref, d_ref), load_sem)
    rows, width = a_ref.shape
    cols = v_ref.shape[0]
    small = red_ref[656:696, :]
    va = jnp.concatenate([red_ref[512:512 + cols, :], red_ref[512 + cols:576, :]], axis=1)
    db = jnp.concatenate([red_ref[576:616, :], red_ref[616:656, :]], axis=1)
    proj_t, proj_r = db[:cols, :], db[cols:cols + 8, :]
    solved = eliminate(small[:cols, :], 64, [identity_at(0), proj_t[:, :LANES], proj_t[:, LANES:]])
    low = solved[0][:, :cols]
    low_t, low = halves(low.T), halves(low)
    half = jnp.concatenate(solved[1:], axis=1)
    half_t, half = halves(half.T), halves(half)
    vv = small[:cols, :cols]
    gram_r = small[cols:cols + 8, 64:64 + cols]
    gram_a = unpack_pair(red_ref, 0, red_ref[696:697, :])
    gram_b = unpack_pair(red_ref, 256, red_ref[697:698, :])
    scale_a = 1.0 / jnp.maximum(largest(diagonal(gram_a)), largest(diagonal(vv)))
    scale_b = 1.0 / largest(diagonal(gram_b))
    gram_a = halves(gram_a * scale_a)
    va = va * scale_a
    vv = halves(vv * scale_a)
    av, va = halves(va.T), halves(va)

    s = halves((gram_b - dot(half_t, half)) * scale_b)
    w = dot(low_t, half)
    ws = halves(w * scale_b)
    wst = halves(dot(half_t, low) * scale_b)
    inv_v = halves(dot(low_t, low))
    k1 = dot(gram_a, s) + dot(av, ws)
    k1t, k1 = halves(k1.T), halves(k1)
    k2 = dot(va, s) + dot(vv, ws)
    k2t = halves(dot(s, av) + dot(wst, vv))
    j1 = halves(dot(s, k1))
    c = dot(inv_v, k2)
    cs = halves(c * scale_b)

    def rows_of(pair, start, stop):
        return tuple(part[start:stop, :] for part in pair)

    def lanes_of(pair, start):
        return tuple(part[:, start:start + LANES] for part in pair)

    z_ref[:LANES, :] = dot(rows_of(k1t, 0, LANES), j1) + dot(rows_of(k2t, 0, LANES), cs)
    z_ref[LANES:, LANES:] = dot(rows_of(k1t, LANES, width), lanes_of(j1, LANES)) + dot(
        rows_of(k2t, LANES, width), lanes_of(cs, LANES)
    )
    row = lax.broadcasted_iota(jnp.int32, (width, width), 0)
    column = lax.broadcasted_iota(jnp.int32, (width, width), 1)
    y_ref[...] = jnp.where(row == column, 1.0, 0.0)
    lane = lax.broadcasted_iota(jnp.int32, (BLOCK, LANES), 1)
    root = jnp.sqrt(scale_b)
    fronts = []

    for lo in range(0, width, BLOCK):
        hi = lo + BLOCK
        base = lo // LANES * LANES
        own = slice(base, base + LANES)
        offset = lo - base
        block = z_ref[lo:hi, own]
        inside = (lane >= offset) & (lane < offset + BLOCK)
        carried = [jnp.where(inside, identity_at(offset), block)]
        carried += [z_ref[lo:hi, start:start + LANES] for start in range(base + LANES, width, LANES)]
        carried = eliminate(block, offset, carried)
        inv = halves(jnp.where(inside, carried[0], 0.0))
        right = {start: halves(part) for start, part in zip(range(base, width, LANES), carried) if start + LANES > hi}
        left = {start: halves(part.T) for start, part in zip(range(base, width, LANES), carried) if start + LANES > hi}
        if hi < width:
            first = hi // LANES * LANES
            near = rows_of(left[first], hi - first, hi - first + BLOCK)
            for start in right:
                tile = slice(start, start + LANES)
                z_ref[hi:hi + BLOCK, tile] = z_ref[hi:hi + BLOCK, tile] - dot(near, right[start])
        solved = dot(inv, y_ref[own, :base + LANES])
        x_ref[lo:hi, :base + LANES] = solved
        if base + LANES < width:
            x_ref[lo:hi, base + LANES:] = jnp.zeros((BLOCK, width - base - LANES), jnp.float32)
        solved = halves(solved)
        for start in right:
            top = max(hi, start)
            part = rows_of(left[start], top - start, LANES)
            y_ref[top:start + LANES, :base + LANES] = y_ref[top:start + LANES, :base + LANES] - dot(part, solved)
            top = max(hi + BLOCK, start)
            if top < start + LANES:
                part = rows_of(left[start], top - start, LANES)
                for other in right:
                    if other >= start:
                        tile = slice(other, other + LANES)
                        z_ref[top:start + LANES, tile] = z_ref[top:start + LANES, tile] - dot(part, right[other])

        if lo == 0:
            for copy in loads:
                copy.wait()
            coeffs = -dot(gram_r, inv_v)
            lead = -proj_r - dot(coeffs, proj_t)
            a = halves(a_ref[...])
            up = dot(lead, a, NT) + dot(coeffs, v_ref[...])
            up_ref[...] = up[:1, :]
            fronts.append(halves((dot(a, j1) + dot(v_ref[...].T, cs)) / root))
        if lo == BLOCK:
            d = halves(d_ref[...].T)
            fronts.append(halves((dot(b_ref[...] - dot(d, w), k1) + dot(d, c)) * root))
        if hi % LANES == 0:
            back = halves(x_ref[own, :])
            na_ref[:, own] = dot(fronts[0], back, NT)
            nb_ref[:, own] = dot(fronts[1], back, NT)


def finish(red, a, b, v, d):
    vmem = pl.BlockSpec(memory_space=pltpu.VMEM)
    rows, width = a.shape
    return pl.pallas_call(
        chain_kernel,
        out_shape=(
            jax.ShapeDtypeStruct((1, rows), jnp.float32),
            jax.ShapeDtypeStruct((rows, width), jnp.float32),
            jax.ShapeDtypeStruct((rows, width), jnp.float32),
        ),
        in_specs=[vmem] + [pl.BlockSpec(memory_space=pltpu.HBM)] * 4,
        out_specs=(vmem,) * 3,
        scratch_shapes=[
            *(pltpu.VMEM(value.shape, jnp.float32) for value in (a, b, v, d)),
            pltpu.SemaphoreType.DMA((4,)),
            pltpu.VMEM((width, width), jnp.float32), pltpu.VMEM((width, width), jnp.float32),
            pltpu.VMEM((width, width), jnp.float32)],
        compiler_params=pltpu.CompilerParams(vmem_limit_bytes=32 << 20),
    )(red, a, b, v, d)


def solution(mesh):
    nx = mesh.shape["sub"]
    sizes = (mesh.shape["rows"] // (2 * nx), nx, nx)

    def on_device(a, b, v, d, r):
        hbm = lambda value: pltpu.with_memory_space_constraint(value, pltpu.HBM)
        a, b, vt, dt, rt = hbm(a), hbm(b), hbm(v.T), hbm(d.T), hbm(r.reshape(1, -1))
        red = reduce_all(sizes, a, b, vt, dt, rt)
        up, new_a, new_b = finish(red, a, b, vt, dt)
        return up.reshape(-1), new_a, new_b

    spread = P(("rows", "sub"))
    wide = P(("rows", "sub"), None)
    return jax.shard_map(
        on_device, mesh=mesh, in_specs=(wide,) * 4 + (spread,), out_specs=(spread, wide, wide), check_vma=False
    )
```

```python
import functools

import jax
import jax.numpy as jnp
from jax import lax
from jax.experimental import pallas as pl
from jax.experimental.pallas import tpu as pltpu
from jax.sharding import PartitionSpec as P

MESH = pl.DeviceIdType.MESH
LANES = 128
PACK = 704
BLOCK = 32
NEXT = 4

NN = (((1,), (0,)), ((), ()))
NT = (((1,), (1,)), ((), ()))
TN = (((0,), (0,)), ((), ()))


def halves(value):
    high = value.astype(jnp.bfloat16)
    return high, (value - high.astype(jnp.float32)).astype(jnp.bfloat16)


def dot(left, right, dims=NN):
    left = left if isinstance(left, tuple) else halves(left)
    right = right if isinstance(right, tuple) else halves(right)

    def one(l, r):
        return lax.dot_general(l, r, dims, preferred_element_type=jnp.float32)

    return one(left[0], right[0]) + (one(left[0], right[1]) + one(left[1], right[0]))


def gram_pair(value, out_ref, base):
    turned = value.T
    whole, first = halves(value), halves(turned[:LANES, :])
    return pack_pair(
        dot(first, tuple(part[:, :LANES] for part in whole)), dot(turned[LANES:, :], whole), out_ref, base
    )


def pack_pair(first, below, out_ref, base):
    row = lax.broadcasted_iota(jnp.int32, (LANES, LANES), 0)
    lane = lax.broadcasted_iota(jnp.int32, (LANES, LANES), 1)
    last = below[:, LANES:]
    out_ref[base:base + LANES, :] = jnp.where(row >= lane, first, last)
    out_ref[base + LANES:base + 2 * LANES, :] = below[:, :LANES]
    return jnp.sum(jnp.where(row == lane, last, 0.0), axis=0, keepdims=True)


def unpack_pair(red_ref, base, diag):
    row = lax.broadcasted_iota(jnp.int32, (LANES, LANES), 0)
    lane = lax.broadcasted_iota(jnp.int32, (LANES, LANES), 1)
    both = red_ref[base:base + LANES, :]
    turned = both.T
    low = red_ref[base + LANES:base + 2 * LANES, :]
    first = jnp.where(row >= lane, both, turned)
    last = jnp.where(row < lane, both, jnp.where(row > lane, turned, diag))
    return jnp.concatenate(
        [jnp.concatenate([first, low.T], axis=1), jnp.concatenate([low, last], axis=1)], axis=0
    )


def fetch(sources, targets, sems):
    copies = [pltpu.make_async_copy(src, dst, sems.at[k]) for k, (src, dst) in enumerate(zip(sources, targets))]
    for copy in copies:
        copy.start()
    return copies


def reduce_kernel(sizes, a_hbm, b_hbm, v_hbm, d_hbm, r_hbm, out_ref, a_ref, b_ref, v_ref, d_ref, r_ref, load_sem,
                  local, pair, half, near, more, mine, far, total, full,
                  pair_sem, near_sem, more_sem, far_sem, back_sem, rest_sem, cross_sem,
                  pair_out, near_out, more_out, far_out, back_out, rest_out, cross_out):
    nz, ny, nx = sizes
    rows = PACK // 2
    plane = ny * nx
    cell = 2 * plane
    steps = nz // 2
    place = lax.axis_index("rows")
    x = lax.axis_index("sub")
    core = lax.rem(place, 2)
    y = lax.rem(place // 2, ny)
    z = place // (2 * ny)
    side, step = lax.rem(z, 2), z // 2
    me = side * plane + y * nx + x
    near_ids = []
    for dz in range(2):
        for dy in range(ny):
            for dx in range(nx):
                if dz or dy or dx:
                    qz, qy, qx = lax.rem(side + dz, 2), lax.rem(y + dy, ny), lax.rem(x + dx, nx)
                    hops = dz + min(dy, ny - dy) + min(dx, nx - dx)
                    dev = (((2 * step + qz) * ny + qy) * 2 + core, qx)
                    near_ids.append((hops, len(near_ids), qz * plane + qy * nx + qx, dev))
    near_ids = sorted(near_ids, key=lambda item: (-item[0], item[1]))
    rings = [[(q, dev) for hops, _, q, dev in near_ids if hops == ring] for ring in range(1, near_ids[0][0] + 1)]
    near_ids = [(hops - 1, q, dev) for hops, _, q, dev in near_ids]
    far_ids = []
    for dz in sorted(range(1, steps), key=lambda d: -min(d, steps - d)):
        qz = lax.rem(step + dz, steps)
        far_ids.append((qz, ((2 * (2 * ny) * qz + 2 * ny * side) + 2 * y + core, x)))
    partner = (place + 1 - 2 * core, x)
    doubles = [(0, qy, qx) for qy in range(ny) for qx in range(nx) if (qx + qy) % 2 == 0]
    doubles += [(1, qy, qx) for qy in range(ny) for qx in range(nx) if (qx + qy) % 4 == 1]
    even = side == 0
    double = (even & (lax.rem(x + y, 2) == 0)) | ((side == 1) & (lax.rem(x + y, 4) == 1))
    mine_second = jnp.where(even, y * (nx // 2) + x // 2, plane // 2 + y)

    loads = fetch((b_hbm, d_hbm, r_hbm, a_hbm, v_hbm), (b_ref, d_ref, r_ref, a_ref, v_ref), load_sem)
    barrier = pltpu.get_barrier_semaphore()
    for _, dev in far_ids:
        pl.semaphore_signal(barrier, inc=1, device_id=dev, device_id_type=MESH)
    for _, _, dev in near_ids:
        pl.semaphore_signal(barrier, inc=1, device_id=dev, device_id_type=MESH)
    pl.semaphore_signal(barrier, inc=1, device_id=partner, device_id_type=MESH)

    cols = v_ref.shape[0]
    for copy in loads[:3]:
        copy.wait()
    diag_b = gram_pair(b_ref[...], local, 2 * LANES)
    d = d_ref[...]
    left = halves(jnp.concatenate([d, jnp.broadcast_to(r_ref[...], (8, d.shape[1]))], axis=0))
    db = dot(left, b_ref[...])
    dd = dot(left, d, NT)
    for copy in loads[3:]:
        copy.wait()
    diag_a = gram_pair(a_ref[...], local, 0)
    v = halves(v_ref[...])
    va = dot(v, a_ref[...])
    vv = dot(v, v, NT)
    local[512:512 + cols, :] = va[:, :LANES]
    local[512 + cols:576, :] = va[:, LANES:]
    local[576:616, :] = db[:, :LANES]
    local[616:656, :] = db[:, LANES:]
    local[656:696, :] = jnp.zeros((40, LANES), jnp.float32)
    local[656:656 + cols, 0:cols] = vv
    local[656:696, 64:64 + cols] = dd
    local[696:704, :] = jnp.zeros((8, LANES), jnp.float32)
    local[696:697, :] = diag_a
    local[697:698, :] = diag_b

    pl.semaphore_wait(barrier, len(far_ids) + len(near_ids) + 1)

    def send(src, dst, out_sem, in_sem, dev):
        pltpu.make_async_remote_copy(
            src_ref=src, dst_ref=dst, send_sem=out_sem, recv_sem=in_sem, device_id=dev, device_id_type=MESH
        ).start()

    def arrived(ref, sem):
        pltpu.make_async_copy(ref, ref, sem).wait()

    def at(start, size=8):
        return pl.ds(pl.multiple_of(start, 8), size)

    def wait_tiles(count, sem):
        arrived(full.at[pl.ds(0, 8 * count)], sem)

    def each_double(action):
        for k, (qz, qy, qx) in enumerate(doubles):

            @pl.when(me != qz * plane + qy * nx + qx)
            def _():
                action(k, (((2 * step + qz) * ny + qy) * 2 + core, qx))

    others, lines = cell - 1, steps - 1
    single = jnp.logical_not(double)

    send(local.at[at((1 - core) * rows, rows)], pair, pair_out, pair_sem, partner)
    arrived(pair, pair_sem)
    half[...] = local[at(core * rows, rows), :] + pair[...]

    for _, q, dev in near_ids:
        send(half.at[at(8 * q)], near.at[me], near_out, near_sem, dev)
    each_double(lambda k, dev: send(half.at[pl.ds(8 * (cell + k), 8)], more.at[me], more_out, more_sem, dev))
    arrived(pair, pair_out)
    near[me] = half[at(8 * me), :]
    wait_tiles(others, near_sem)
    mine[0:8, :] = jnp.sum(near[...], axis=0)

    @pl.when(single)
    def _():
        for q, dev in far_ids:
            send(mine.at[0:8], far.at[step, 0:8], far_out, far_sem, dev)
        far[step, 0:8] = mine[0:8, :]
        wait_tiles(others, near_out)
        wait_tiles(len(doubles), more_out)
        wait_tiles(lines, far_sem)
        total[0:8, :] = jnp.sum(far[:, 0:8, :], axis=0)

    @pl.when(double)
    def _():
        more[me] = half[at(8 * (cell + mine_second)), :]
        wait_tiles(others, more_sem)
        mine[8:16, :] = jnp.sum(more[...], axis=0)
        for q, dev in far_ids:
            send(mine, far.at[step], far_out, far_sem, dev)
        far[step] = mine[...]
        wait_tiles(others, near_out)
        wait_tiles(len(doubles) - 1, more_out)
        wait_tiles(2 * lines, far_sem)
        total[...] = jnp.sum(far[...], axis=0)

    base = core * rows
    for ring, q, dev in near_ids:
        send(total.at[0:8], full.at[at(base + 8 * me)], back_out, back_sem.at[ring], dev)
    send(total.at[0:8], full.at[at(base + 8 * me)], cross_out, cross_sem, partner)
    full[at(base + 8 * me), :] = total[0:8, :]

    @pl.when(double)
    def _():
        spot = base + 8 * (cell + mine_second)
        for _, q, dev in near_ids:
            send(total.at[8:16], full.at[at(spot)], rest_out, rest_sem, dev)
        send(total.at[8:16], full.at[at(spot)], cross_out, cross_sem, partner)
        full[at(spot), :] = total[8:16, :]
        wait_tiles(2 * lines, far_out)

    @pl.when(single)
    def _():
        wait_tiles(lines, far_out)

    for ring, members in enumerate(rings):
        wait_tiles(len(members), back_sem.at[ring])
        for q, dev in members:
            tile = full.at[at(base + 8 * q)]
            send(tile, tile, cross_out, cross_sem, partner)

    @pl.when(single)
    def _():
        wait_tiles(len(doubles), rest_sem)

    @pl.when(double)
    def _():
        wait_tiles(len(doubles) - 1, rest_sem)

    def forward(k, dev):
        tile = full.at[at(base + 8 * (cell + k))]
        send(tile, tile, cross_out, cross_sem, partner)

    each_double(forward)
    wait_tiles(others, back_out)

    @pl.when(double)
    def _():
        wait_tiles(others, rest_out)

    arrived(full.at[at((1 - core) * rows, rows)], cross_sem)
    arrived(full.at[at(base, rows)], cross_out)
    out_ref[...] = full[...]


def reduce_all(sizes, a, b, v, d, r):
    nz, ny, nx = sizes
    cell, steps = 2 * ny * nx, nz // 2
    rows = PACK // 2
    twice = rows // 8 - cell
    vmem = pl.BlockSpec(memory_space=pltpu.VMEM)
    dma = pltpu.SemaphoreType.DMA
    return pl.pallas_call(
        functools.partial(reduce_kernel, sizes),
        out_shape=jax.ShapeDtypeStruct((PACK, LANES), jnp.float32),
        in_specs=[pl.BlockSpec(memory_space=pltpu.HBM)] * 5,
        out_specs=vmem,
        scratch_shapes=[
            *(pltpu.VMEM(value.shape, jnp.float32) for value in (a, b, v, d, r)),
            dma((5,)),
            pltpu.VMEM((PACK, LANES), jnp.float32),
            pltpu.VMEM((rows, LANES), jnp.float32),
            pltpu.VMEM((rows, LANES), jnp.float32),
            pltpu.VMEM((cell, 8, LANES), jnp.float32),
            pltpu.VMEM((cell, 8, LANES), jnp.float32),
            pltpu.VMEM((16, LANES), jnp.float32),
            pltpu.VMEM((steps, 16, LANES), jnp.float32),
            pltpu.VMEM((16, LANES), jnp.float32),
            pltpu.VMEM((PACK, LANES), jnp.float32),
            dma(()), dma(()), dma(()), dma(()), dma((8,)), dma(()), dma(()),
            *(dma(()) for _ in range(7)),
        ],
        compiler_params=pltpu.CompilerParams(collective_id=0, has_side_effects=True, vmem_limit_bytes=32 << 20),
    )(a, b, v, d, r)


def eliminate(tile, offset, carried, spread):
    groups = BLOCK // 8
    sub = lax.broadcasted_iota(jnp.int32, (8, LANES), 0)
    columns = [
        {
            i: jnp.broadcast_to(tile[8 * i:8 * i + 8, offset + j:offset + j + 1], (8, LANES))
            for i in range(j // 8, groups)
        }
        for j in range(BLOCK)
    ]
    carried = [[part[8 * i:8 * i + 8, :] for i in range(groups)] for part in carried]
    for j in range(BLOCK):
        g, r = j // 8, j % 8
        scale = lax.rsqrt(columns[j][g][r:r + 1, :])
        column = {i: columns[j][i] * scale for i in range(g, groups)}
        for i in range(g, groups):
            spread[j, 8 * i:8 * i + 8, :] = column[i]
        for b in range(j + 1, BLOCK):
            if b < j + NEXT:
                factor = column[b // 8][b % 8:b % 8 + 1, :]
            else:
                factor = spread[j, b:b + 1, :]
            for i in range(b // 8, groups):
                columns[b][i] = columns[b][i] - column[i] * factor
        below = jnp.where(sub > r, column[g], 0.0)
        for out in carried:
            pivot = out[g][r:r + 1, :] * scale
            out[g] = jnp.where(sub == r, pivot, out[g] - below * pivot)
            for i in range(g + 1, groups):
                out[i] = out[i] - column[i] * pivot
    return [jnp.concatenate(out, axis=0) for out in carried]


def identity_at(offset):
    row = lax.broadcasted_iota(jnp.int32, (BLOCK, LANES), 0)
    lane = lax.broadcasted_iota(jnp.int32, (BLOCK, LANES), 1)
    return jnp.where(lane == row + offset, 1.0, 0.0)


def largest(values):
    return jnp.max(jnp.max(values, axis=1, keepdims=True), axis=0, keepdims=True)


def diagonal(matrix):
    row = lax.broadcasted_iota(jnp.int32, matrix.shape, 0)
    lane = lax.broadcasted_iota(jnp.int32, matrix.shape, 1)
    return jnp.where(row == lane, matrix, 0.0)


def chain_kernel(red_ref, a_hbm, b_hbm, v_hbm, d_hbm, up_ref, na_ref, nb_ref, a_ref, b_ref, v_ref, d_ref, load_sem, z_ref, y_ref, x_ref, spread):
    loads = fetch((a_hbm, b_hbm, v_hbm, d_hbm), (a_ref, b_ref, v_ref, d_ref), load_sem)
    rows, width = a_ref.shape
    cols = v_ref.shape[0]
    small = red_ref[656:696, :]
    va = jnp.concatenate([red_ref[512:512 + cols, :], red_ref[512 + cols:576, :]], axis=1)
    db = jnp.concatenate([red_ref[576:616, :], red_ref[616:656, :]], axis=1)
    proj_t, proj_r = db[:cols, :], db[cols:cols + 8, :]
    solved = eliminate(small[:cols, :], 64, [identity_at(0), proj_t[:, :LANES], proj_t[:, LANES:]], spread)
    low = solved[0][:, :cols]
    low_t, low = halves(low.T), halves(low)
    half = jnp.concatenate(solved[1:], axis=1)
    half_t, half = halves(half.T), halves(half)
    vv = small[:cols, :cols]
    gram_r = small[cols:cols + 8, 64:64 + cols]
    gram_a = unpack_pair(red_ref, 0, red_ref[696:697, :])
    gram_b = unpack_pair(red_ref, 256, red_ref[697:698, :])
    scale_a = 1.0 / jnp.maximum(largest(diagonal(gram_a)), largest(diagonal(vv)))
    scale_b = 1.0 / largest(diagonal(gram_b))
    gram_a = halves(gram_a * scale_a)
    va = va * scale_a
    vv = halves(vv * scale_a)
    av, va = halves(va.T), halves(va)

    s = halves((gram_b - dot(half_t, half)) * scale_b)
    w = dot(low_t, half)
    ws = halves(w * scale_b)
    wst = halves(dot(half_t, low) * scale_b)
    inv_v = halves(dot(low_t, low))
    k1 = dot(gram_a, s) + dot(av, ws)
    k1t, k1 = halves(k1.T), halves(k1)
    k2 = dot(va, s) + dot(vv, ws)
    k2t = halves(dot(s, av) + dot(wst, vv))
    j1 = halves(dot(s, k1))
    c = dot(inv_v, k2)
    cs = halves(c * scale_b)

    def rows_of(pair, start, stop):
        return tuple(part[start:stop, :] for part in pair)

    def lanes_of(pair, start):
        return tuple(part[:, start:start + LANES] for part in pair)

    z_ref[:LANES, :] = dot(rows_of(k1t, 0, LANES), j1) + dot(rows_of(k2t, 0, LANES), cs)
    z_ref[LANES:, LANES:] = dot(rows_of(k1t, LANES, width), lanes_of(j1, LANES)) + dot(
        rows_of(k2t, LANES, width), lanes_of(cs, LANES)
    )
    row = lax.broadcasted_iota(jnp.int32, (width, width), 0)
    column = lax.broadcasted_iota(jnp.int32, (width, width), 1)
    y_ref[...] = jnp.where(row == column, 1.0, 0.0)
    lane = lax.broadcasted_iota(jnp.int32, (BLOCK, LANES), 1)
    root = jnp.sqrt(scale_b)
    fronts = []

    for lo in range(0, width, BLOCK):
        hi = lo + BLOCK
        base = lo // LANES * LANES
        own = slice(base, base + LANES)
        offset = lo - base
        block = z_ref[lo:hi, own]
        inside = (lane >= offset) & (lane < offset + BLOCK)
        carried = [jnp.where(inside, identity_at(offset), block)]
        rest = [z_ref[lo:hi, start:start + LANES] for start in range(base + LANES, width, LANES)]
        if hi % LANES == 0:
            carried += rest
        carried = eliminate(block, offset, carried, spread)
        inv = halves(jnp.where(inside, carried[0], 0.0))
        if hi % LANES:
            narrow = halves(pltpu.roll(jnp.where(inside, carried[0], 0.0), (LANES - offset) % LANES, 1)[:, :BLOCK])
            carried += [dot(narrow, part) for part in rest]
        right = {start: halves(part) for start, part in zip(range(base, width, LANES), carried) if start + LANES > hi}
        left = {start: halves(part.T) for start, part in zip(range(base, width, LANES), carried) if start + LANES > hi}
        if hi < width:
            first = hi // LANES * LANES
            near = rows_of(left[first], hi - first, hi - first + BLOCK)
            for start in right:
                tile = slice(start, start + LANES)
                z_ref[hi:hi + BLOCK, tile] = z_ref[hi:hi + BLOCK, tile] - dot(near, right[start])
        solved = dot(inv, y_ref[own, :base + LANES])
        x_ref[lo:hi, :base + LANES] = solved
        if base + LANES < width:
            x_ref[lo:hi, base + LANES:] = jnp.zeros((BLOCK, width - base - LANES), jnp.float32)
        solved = halves(solved)
        for start in right:
            top = max(hi, start)
            part = rows_of(left[start], top - start, LANES)
            y_ref[top:start + LANES, :base + LANES] = y_ref[top:start + LANES, :base + LANES] - dot(part, solved)
            top = max(hi + BLOCK, start)
            if top < start + LANES:
                part = rows_of(left[start], top - start, LANES)
                for other in right:
                    if other >= start:
                        tile = slice(other, other + LANES)
                        z_ref[top:start + LANES, tile] = z_ref[top:start + LANES, tile] - dot(part, right[other])

        if lo == 0:
            for copy in loads:
                copy.wait()
            coeffs = -dot(gram_r, inv_v)
            lead = -proj_r - dot(coeffs, proj_t)
            a = halves(a_ref[...])
            up = dot(lead, a, NT) + dot(coeffs, v_ref[...])
            up_ref[...] = up[:1, :]
            fronts.append(halves((dot(a, j1) + dot(v_ref[...].T, cs)) / root))
        if lo == BLOCK:
            d = halves(d_ref[...].T)
            fronts.append(halves((dot(b_ref[...] - dot(d, w), k1) + dot(d, c)) * root))
        if hi % LANES == 0:
            back = halves(x_ref[own, :])
            na_ref[:, own] = dot(fronts[0], back, NT)
            nb_ref[:, own] = dot(fronts[1], back, NT)


def finish(red, a, b, v, d):
    vmem = pl.BlockSpec(memory_space=pltpu.VMEM)
    rows, width = a.shape
    return pl.pallas_call(
        chain_kernel,
        out_shape=(
            jax.ShapeDtypeStruct((1, rows), jnp.float32),
            jax.ShapeDtypeStruct((rows, width), jnp.float32),
            jax.ShapeDtypeStruct((rows, width), jnp.float32),
        ),
        in_specs=[vmem] + [pl.BlockSpec(memory_space=pltpu.HBM)] * 4,
        out_specs=(vmem,) * 3,
        scratch_shapes=[
            *(pltpu.VMEM(value.shape, jnp.float32) for value in (a, b, v, d)),
            pltpu.SemaphoreType.DMA((4,)),
            pltpu.VMEM((width, width), jnp.float32), pltpu.VMEM((width, width), jnp.float32),
            pltpu.VMEM((width, width), jnp.float32), pltpu.VMEM((BLOCK, BLOCK, LANES), jnp.float32)],
        compiler_params=pltpu.CompilerParams(vmem_limit_bytes=32 << 20),
    )(red, a, b, v, d)


def solution(mesh):
    nx = mesh.shape["sub"]
    sizes = (mesh.shape["rows"] // (2 * nx), nx, nx)

    def on_device(a, b, v, d, r):
        hbm = lambda value: pltpu.with_memory_space_constraint(value, pltpu.HBM)
        a, b, vt, dt, rt = hbm(a), hbm(b), hbm(v.T), hbm(d.T), hbm(r.reshape(1, -1))
        red = reduce_all(sizes, a, b, vt, dt, rt)
        up, new_a, new_b = finish(red, a, b, vt, dt)
        return up.reshape(-1), new_a, new_b

    spread = P(("rows", "sub"))
    wide = P(("rows", "sub"), None)
    return jax.shard_map(
        on_device, mesh=mesh, in_specs=(wide,) * 4 + (spread,), out_specs=(spread, wide, wide), check_vma=False
    )
```

```python
import functools

import jax
import jax.numpy as jnp
from jax import lax
from jax.experimental import pallas as pl
from jax.experimental.pallas import tpu as pltpu
from jax.sharding import PartitionSpec as P

MESH = pl.DeviceIdType.MESH
LANES = 128
PACK = 704
BLOCK = 32
NEXT = 4

NN = (((1,), (0,)), ((), ()))
NT = (((1,), (1,)), ((), ()))
TN = (((0,), (0,)), ((), ()))


def halves(value):
    high = value.astype(jnp.bfloat16)
    return high, (value - high.astype(jnp.float32)).astype(jnp.bfloat16)


def dot(left, right, dims=NN):
    left = left if isinstance(left, tuple) else halves(left)
    right = right if isinstance(right, tuple) else halves(right)

    def one(l, r):
        return lax.dot_general(l, r, dims, preferred_element_type=jnp.float32)

    return one(left[0], right[0]) + (one(left[0], right[1]) + one(left[1], right[0]))


def gram_pair(value, out_ref, base):
    turned = value.T
    whole, first = halves(value), halves(turned[:LANES, :])
    return pack_pair(
        dot(first, tuple(part[:, :LANES] for part in whole)), dot(turned[LANES:, :], whole), out_ref, base
    )


def pack_pair(first, below, out_ref, base):
    row = lax.broadcasted_iota(jnp.int32, (LANES, LANES), 0)
    lane = lax.broadcasted_iota(jnp.int32, (LANES, LANES), 1)
    last = below[:, LANES:]
    out_ref[base:base + LANES, :] = jnp.where(row >= lane, first, last)
    out_ref[base + LANES:base + 2 * LANES, :] = below[:, :LANES]
    return jnp.sum(jnp.where(row == lane, last, 0.0), axis=0, keepdims=True)


def unpack_pair(red_ref, base, diag):
    row = lax.broadcasted_iota(jnp.int32, (LANES, LANES), 0)
    lane = lax.broadcasted_iota(jnp.int32, (LANES, LANES), 1)
    both = red_ref[base:base + LANES, :]
    turned = both.T
    low = red_ref[base + LANES:base + 2 * LANES, :]
    first = jnp.where(row >= lane, both, turned)
    last = jnp.where(row < lane, both, jnp.where(row > lane, turned, diag))
    return jnp.concatenate(
        [jnp.concatenate([first, low.T], axis=1), jnp.concatenate([low, last], axis=1)], axis=0
    )


def fetch(sources, targets, sems):
    copies = [pltpu.make_async_copy(src, dst, sems.at[k]) for k, (src, dst) in enumerate(zip(sources, targets))]
    for copy in copies:
        copy.start()
    return copies


def reduce_kernel(sizes, a_hbm, b_hbm, v_hbm, d_hbm, r_hbm, out_ref, a_ref, b_ref, v_ref, d_ref, r_ref, load_sem,
                  local, pair, half, near, more, mine, far, total, full,
                  pair_sem, near_sem, more_sem, far_sem, back_sem, rest_sem, cross_sem,
                  pair_out, near_out, more_out, far_out, back_out, rest_out, cross_out):
    nz, ny, nx = sizes
    rows = PACK // 2
    plane = ny * nx
    cell = 2 * plane
    steps = nz // 2
    place = lax.axis_index("rows")
    x = lax.axis_index("sub")
    core = lax.rem(place, 2)
    y = lax.rem(place // 2, ny)
    z = place // (2 * ny)
    side, step = lax.rem(z, 2), z // 2
    me = side * plane + y * nx + x
    near_ids = []
    for dz in range(2):
        for dy in range(ny):
            for dx in range(nx):
                if dz or dy or dx:
                    qz, qy, qx = lax.rem(side + dz, 2), lax.rem(y + dy, ny), lax.rem(x + dx, nx)
                    hops = dz + min(dy, ny - dy) + min(dx, nx - dx)
                    dev = (((2 * step + qz) * ny + qy) * 2 + core, qx)
                    near_ids.append((hops, len(near_ids), qz * plane + qy * nx + qx, dev))
    near_ids = sorted(near_ids, key=lambda item: (-item[0], item[1]))
    rings = [[(q, dev) for hops, _, q, dev in near_ids if hops == ring] for ring in range(1, near_ids[0][0] + 1)]
    near_ids = [(hops - 1, q, dev) for hops, _, q, dev in near_ids]
    far_ids = []
    for dz in sorted(range(1, steps), key=lambda d: -min(d, steps - d)):
        qz = lax.rem(step + dz, steps)
        far_ids.append((qz, ((2 * (2 * ny) * qz + 2 * ny * side) + 2 * y + core, x)))
    partner = (place + 1 - 2 * core, x)
    doubles = [(0, qy, qx) for qy in range(ny) for qx in range(nx) if (qx + qy) % 2 == 0]
    doubles += [(1, qy, qx) for qy in range(ny) for qx in range(nx) if (qx + qy) % 4 == 1]
    even = side == 0
    double = (even & (lax.rem(x + y, 2) == 0)) | ((side == 1) & (lax.rem(x + y, 4) == 1))
    mine_second = jnp.where(even, y * (nx // 2) + x // 2, plane // 2 + y)

    loads = fetch((b_hbm, d_hbm, r_hbm, a_hbm, v_hbm), (b_ref, d_ref, r_ref, a_ref, v_ref), load_sem)
    barrier = pltpu.get_barrier_semaphore()
    for _, dev in far_ids:
        pl.semaphore_signal(barrier, inc=1, device_id=dev, device_id_type=MESH)
    for _, _, dev in near_ids:
        pl.semaphore_signal(barrier, inc=1, device_id=dev, device_id_type=MESH)
    pl.semaphore_signal(barrier, inc=1, device_id=partner, device_id_type=MESH)

    cols = v_ref.shape[0]

    def half_a():
        for k in (3, 4):
            loads[k].wait()
        diag = gram_pair(a_ref[...], local, 0)
        v, d = halves(v_ref[...]), halves(d_ref[...])
        va = dot(v, a_ref[...])
        local[256:256 + cols, :] = va[:, :LANES]
        local[256 + cols:320, :] = va[:, LANES:]
        local[320:352, :] = jnp.zeros((32, LANES), jnp.float32)
        local[320:320 + cols, 0:cols] = dot(v, v, NT)
        local[320:320 + cols, 64:64 + cols] = dot(d, d, NT)
        for k in range(4):
            local[320 + k:321 + k, 32:64] = diag[:, 32 * k:32 * k + 32]

    def half_b():
        for k in (0, 2):
            loads[k].wait()
        diag = gram_pair(b_ref[...], local, rows)
        d = d_ref[...]
        last = jnp.broadcast_to(r_ref[...], (8, d.shape[1]))
        db = dot(jnp.concatenate([d, last], axis=0), b_ref[...])
        local[608:648, :] = db[:, :LANES]
        local[648:688, :] = db[:, LANES:]
        local[688:704, :] = jnp.zeros((16, LANES), jnp.float32)
        local[688:689, :] = diag
        local[696:704, 0:cols] = dot(last, d, NT)

    def send(src, dst, out_sem, in_sem, dev):
        pltpu.make_async_remote_copy(
            src_ref=src, dst_ref=dst, send_sem=out_sem, recv_sem=in_sem, device_id=dev, device_id_type=MESH
        ).start()

    def arrived(ref, sem):
        pltpu.make_async_copy(ref, ref, sem).wait()

    def at(start, size=8):
        return pl.ds(pl.multiple_of(start, 8), size)

    def wait_tiles(count, sem):
        arrived(full.at[pl.ds(0, 8 * count)], sem)

    def each_double(action):
        for k, (qz, qy, qx) in enumerate(doubles):

            @pl.when(me != qz * plane + qy * nx + qx)
            def _():
                action(k, (((2 * step + qz) * ny + qy) * 2 + core, qx))

    others, lines = cell - 1, steps - 1
    single = jnp.logical_not(double)

    @pl.when(core == 0)
    def _():
        loads[1].wait()
        half_b()
        pl.semaphore_wait(barrier, len(far_ids) + len(near_ids) + 1)
        send(local.at[rows:PACK], pair, pair_out, pair_sem, partner)
        half_a()

    @pl.when(core == 1)
    def _():
        loads[1].wait()
        half_a()
        pl.semaphore_wait(barrier, len(far_ids) + len(near_ids) + 1)
        send(local.at[0:rows], pair, pair_out, pair_sem, partner)
        half_b()

    arrived(pair, pair_sem)
    half[...] = local[at(core * rows, rows), :] + pair[...]

    for _, q, dev in near_ids:
        send(half.at[at(8 * q)], near.at[me], near_out, near_sem, dev)
    each_double(lambda k, dev: send(half.at[pl.ds(8 * (cell + k), 8)], more.at[me], more_out, more_sem, dev))
    arrived(pair, pair_out)
    near[me] = half[at(8 * me), :]
    wait_tiles(others, near_sem)
    mine[0:8, :] = jnp.sum(near[...], axis=0)

    @pl.when(single)
    def _():
        for q, dev in far_ids:
            send(mine.at[0:8], far.at[step, 0:8], far_out, far_sem, dev)
        far[step, 0:8] = mine[0:8, :]
        wait_tiles(others, near_out)
        wait_tiles(len(doubles), more_out)
        wait_tiles(lines, far_sem)
        total[0:8, :] = jnp.sum(far[:, 0:8, :], axis=0)

    @pl.when(double)
    def _():
        more[me] = half[at(8 * (cell + mine_second)), :]
        wait_tiles(others, more_sem)
        mine[8:16, :] = jnp.sum(more[...], axis=0)
        for q, dev in far_ids:
            send(mine, far.at[step], far_out, far_sem, dev)
        far[step] = mine[...]
        wait_tiles(others, near_out)
        wait_tiles(len(doubles) - 1, more_out)
        wait_tiles(2 * lines, far_sem)
        total[...] = jnp.sum(far[...], axis=0)

    base = core * rows
    for ring, q, dev in near_ids:
        send(total.at[0:8], full.at[at(base + 8 * me)], back_out, back_sem.at[ring], dev)
    send(total.at[0:8], full.at[at(base + 8 * me)], cross_out, cross_sem, partner)
    full[at(base + 8 * me), :] = total[0:8, :]

    @pl.when(double)
    def _():
        spot = base + 8 * (cell + mine_second)
        for _, q, dev in near_ids:
            send(total.at[8:16], full.at[at(spot)], rest_out, rest_sem, dev)
        send(total.at[8:16], full.at[at(spot)], cross_out, cross_sem, partner)
        full[at(spot), :] = total[8:16, :]
        wait_tiles(2 * lines, far_out)

    @pl.when(single)
    def _():
        wait_tiles(lines, far_out)

    for ring, members in enumerate(rings):
        wait_tiles(len(members), back_sem.at[ring])
        for q, dev in members:
            tile = full.at[at(base + 8 * q)]
            send(tile, tile, cross_out, cross_sem, partner)

    @pl.when(single)
    def _():
        wait_tiles(len(doubles), rest_sem)

    @pl.when(double)
    def _():
        wait_tiles(len(doubles) - 1, rest_sem)

    def forward(k, dev):
        tile = full.at[at(base + 8 * (cell + k))]
        send(tile, tile, cross_out, cross_sem, partner)

    each_double(forward)
    wait_tiles(others, back_out)

    @pl.when(double)
    def _():
        wait_tiles(others, rest_out)

    arrived(full.at[at((1 - core) * rows, rows)], cross_sem)
    arrived(full.at[at(base, rows)], cross_out)
    out_ref[...] = full[...]


def reduce_all(sizes, a, b, v, d, r):
    nz, ny, nx = sizes
    cell, steps = 2 * ny * nx, nz // 2
    rows = PACK // 2
    twice = rows // 8 - cell
    vmem = pl.BlockSpec(memory_space=pltpu.VMEM)
    dma = pltpu.SemaphoreType.DMA
    return pl.pallas_call(
        functools.partial(reduce_kernel, sizes),
        out_shape=jax.ShapeDtypeStruct((PACK, LANES), jnp.float32),
        in_specs=[pl.BlockSpec(memory_space=pltpu.HBM)] * 5,
        out_specs=vmem,
        scratch_shapes=[
            *(pltpu.VMEM(value.shape, jnp.float32) for value in (a, b, v, d, r)),
            dma((5,)),
            pltpu.VMEM((PACK, LANES), jnp.float32),
            pltpu.VMEM((rows, LANES), jnp.float32),
            pltpu.VMEM((rows, LANES), jnp.float32),
            pltpu.VMEM((cell, 8, LANES), jnp.float32),
            pltpu.VMEM((cell, 8, LANES), jnp.float32),
            pltpu.VMEM((16, LANES), jnp.float32),
            pltpu.VMEM((steps, 16, LANES), jnp.float32),
            pltpu.VMEM((16, LANES), jnp.float32),
            pltpu.VMEM((PACK, LANES), jnp.float32),
            dma(()), dma(()), dma(()), dma(()), dma((8,)), dma(()), dma(()),
            *(dma(()) for _ in range(7)),
        ],
        compiler_params=pltpu.CompilerParams(collective_id=0, has_side_effects=True, vmem_limit_bytes=32 << 20),
    )(a, b, v, d, r)


def eliminate(tile, offset, carried, spread):
    groups = BLOCK // 8
    sub = lax.broadcasted_iota(jnp.int32, (8, LANES), 0)
    columns = [
        {
            i: jnp.broadcast_to(tile[8 * i:8 * i + 8, offset + j:offset + j + 1], (8, LANES))
            for i in range(j // 8, groups)
        }
        for j in range(BLOCK)
    ]
    carried = [[part[8 * i:8 * i + 8, :] for i in range(groups)] for part in carried]
    for j in range(BLOCK):
        g, r = j // 8, j % 8
        scale = lax.rsqrt(columns[j][g][r:r + 1, :])
        column = {i: columns[j][i] * scale for i in range(g, groups)}
        for i in range(g, groups):
            spread[j, 8 * i:8 * i + 8, :] = column[i]
        for b in range(j + 1, BLOCK):
            if b < j + NEXT:
                factor = column[b // 8][b % 8:b % 8 + 1, :]
            else:
                factor = spread[j, b:b + 1, :]
            for i in range(b // 8, groups):
                columns[b][i] = columns[b][i] - column[i] * factor
        below = jnp.where(sub > r, column[g], 0.0)
        for out in carried:
            pivot = out[g][r:r + 1, :] * scale
            out[g] = jnp.where(sub == r, pivot, out[g] - below * pivot)
            for i in range(g + 1, groups):
                out[i] = out[i] - column[i] * pivot
    return [jnp.concatenate(out, axis=0) for out in carried]


def identity_at(offset):
    row = lax.broadcasted_iota(jnp.int32, (BLOCK, LANES), 0)
    lane = lax.broadcasted_iota(jnp.int32, (BLOCK, LANES), 1)
    return jnp.where(lane == row + offset, 1.0, 0.0)


def largest(values):
    return jnp.max(jnp.max(values, axis=1, keepdims=True), axis=0, keepdims=True)


def diagonal(matrix):
    row = lax.broadcasted_iota(jnp.int32, matrix.shape, 0)
    lane = lax.broadcasted_iota(jnp.int32, matrix.shape, 1)
    return jnp.where(row == lane, matrix, 0.0)


def chain_kernel(red_ref, a_hbm, b_hbm, v_hbm, d_hbm, up_ref, na_ref, nb_ref, a_ref, b_ref, v_ref, d_ref, load_sem, z_ref, y_ref, x_ref, spread):
    loads = fetch((a_hbm, b_hbm, v_hbm, d_hbm), (a_ref, b_ref, v_ref, d_ref), load_sem)
    rows, width = a_ref.shape
    cols = v_ref.shape[0]
    small = red_ref[320:352, :]
    va = jnp.concatenate([red_ref[256:256 + cols, :], red_ref[256 + cols:320, :]], axis=1)
    db = jnp.concatenate([red_ref[608:648, :], red_ref[648:688, :]], axis=1)
    proj_t, proj_r = db[:cols, :], db[cols:cols + 8, :]
    solved = eliminate(small[:cols, :], 64, [identity_at(0), proj_t[:, :LANES], proj_t[:, LANES:]], spread)
    low = solved[0][:, :cols]
    low_t, low = halves(low.T), halves(low)
    half = jnp.concatenate(solved[1:], axis=1)
    half_t, half = halves(half.T), halves(half)
    vv = small[:cols, :cols]
    gram_r = red_ref[696:704, :cols]
    diag_a = jnp.concatenate([small[k:k + 1, 32:64] for k in range(4)], axis=1)
    gram_a = unpack_pair(red_ref, 0, diag_a)
    gram_b = unpack_pair(red_ref, 352, red_ref[688:689, :])
    scale_a = 1.0 / jnp.maximum(largest(diagonal(gram_a)), largest(diagonal(vv)))
    scale_b = 1.0 / largest(diagonal(gram_b))
    gram_a = halves(gram_a * scale_a)
    va = va * scale_a
    vv = halves(vv * scale_a)
    av, va = halves(va.T), halves(va)

    s = halves((gram_b - dot(half_t, half)) * scale_b)
    w = dot(low_t, half)
    ws = halves(w * scale_b)
    wst = halves(dot(half_t, low) * scale_b)
    inv_v = halves(dot(low_t, low))
    k1 = dot(gram_a, s) + dot(av, ws)
    k1t, k1 = halves(k1.T), halves(k1)
    k2 = dot(va, s) + dot(vv, ws)
    k2t = halves(dot(s, av) + dot(wst, vv))
    j1 = halves(dot(s, k1))
    c = dot(inv_v, k2)
    cs = halves(c * scale_b)

    def rows_of(pair, start, stop):
        return tuple(part[start:stop, :] for part in pair)

    def lanes_of(pair, start):
        return tuple(part[:, start:start + LANES] for part in pair)

    z_ref[:LANES, :] = dot(rows_of(k1t, 0, LANES), j1) + dot(rows_of(k2t, 0, LANES), cs)
    z_ref[LANES:, LANES:] = dot(rows_of(k1t, LANES, width), lanes_of(j1, LANES)) + dot(
        rows_of(k2t, LANES, width), lanes_of(cs, LANES)
    )
    row = lax.broadcasted_iota(jnp.int32, (width, width), 0)
    column = lax.broadcasted_iota(jnp.int32, (width, width), 1)
    y_ref[...] = jnp.where(row == column, 1.0, 0.0)
    lane = lax.broadcasted_iota(jnp.int32, (BLOCK, LANES), 1)
    root = jnp.sqrt(scale_b)
    fronts = []

    for lo in range(0, width, BLOCK):
        hi = lo + BLOCK
        base = lo // LANES * LANES
        own = slice(base, base + LANES)
        offset = lo - base
        block = z_ref[lo:hi, own]
        inside = (lane >= offset) & (lane < offset + BLOCK)
        carried = [jnp.where(inside, identity_at(offset), block)]
        rest = [z_ref[lo:hi, start:start + LANES] for start in range(base + LANES, width, LANES)]
        if hi % LANES == 0:
            carried += rest
        carried = eliminate(block, offset, carried, spread)
        inv = halves(jnp.where(inside, carried[0], 0.0))
        if hi % LANES:
            narrow = halves(pltpu.roll(jnp.where(inside, carried[0], 0.0), (LANES - offset) % LANES, 1)[:, :BLOCK])
            carried += [dot(narrow, part) for part in rest]
        right = {start: halves(part) for start, part in zip(range(base, width, LANES), carried) if start + LANES > hi}
        left = {start: halves(part.T) for start, part in zip(range(base, width, LANES), carried) if start + LANES > hi}
        if hi < width:
            first = hi // LANES * LANES
            near = rows_of(left[first], hi - first, hi - first + BLOCK)
            for start in right:
                tile = slice(start, start + LANES)
                z_ref[hi:hi + BLOCK, tile] = z_ref[hi:hi + BLOCK, tile] - dot(near, right[start])
        solved = dot(inv, y_ref[own, :base + LANES])
        x_ref[lo:hi, :base + LANES] = solved
        if base + LANES < width:
            x_ref[lo:hi, base + LANES:] = jnp.zeros((BLOCK, width - base - LANES), jnp.float32)
        solved = halves(solved)
        for start in right:
            top = max(hi, start)
            part = rows_of(left[start], top - start, LANES)
            y_ref[top:start + LANES, :base + LANES] = y_ref[top:start + LANES, :base + LANES] - dot(part, solved)
            top = max(hi + BLOCK, start)
            if top < start + LANES:
                part = rows_of(left[start], top - start, LANES)
                for other in right:
                    if other >= start:
                        tile = slice(other, other + LANES)
                        z_ref[top:start + LANES, tile] = z_ref[top:start + LANES, tile] - dot(part, right[other])

        if lo == 0:
            for copy in loads:
                copy.wait()
            coeffs = -dot(gram_r, inv_v)
            lead = -proj_r - dot(coeffs, proj_t)
            a = halves(a_ref[...])
            up = dot(lead, a, NT) + dot(coeffs, v_ref[...])
            up_ref[...] = up[:1, :]
            fronts.append(halves((dot(a, j1) + dot(v_ref[...].T, cs)) / root))
        if lo == BLOCK:
            d = halves(d_ref[...].T)
            fronts.append(halves((dot(b_ref[...] - dot(d, w), k1) + dot(d, c)) * root))
        if hi % LANES == 0:
            back = halves(x_ref[own, :])
            na_ref[:, own] = dot(fronts[0], back, NT)
            nb_ref[:, own] = dot(fronts[1], back, NT)


def finish(red, a, b, v, d):
    vmem = pl.BlockSpec(memory_space=pltpu.VMEM)
    rows, width = a.shape
    return pl.pallas_call(
        chain_kernel,
        out_shape=(
            jax.ShapeDtypeStruct((1, rows), jnp.float32),
            jax.ShapeDtypeStruct((rows, width), jnp.float32),
            jax.ShapeDtypeStruct((rows, width), jnp.float32),
        ),
        in_specs=[vmem] + [pl.BlockSpec(memory_space=pltpu.HBM)] * 4,
        out_specs=(vmem,) * 3,
        scratch_shapes=[
            *(pltpu.VMEM(value.shape, jnp.float32) for value in (a, b, v, d)),
            pltpu.SemaphoreType.DMA((4,)),
            pltpu.VMEM((width, width), jnp.float32), pltpu.VMEM((width, width), jnp.float32),
            pltpu.VMEM((width, width), jnp.float32), pltpu.VMEM((BLOCK, BLOCK, LANES), jnp.float32)],
        compiler_params=pltpu.CompilerParams(vmem_limit_bytes=32 << 20),
    )(red, a, b, v, d)


def solution(mesh):
    nx = mesh.shape["sub"]
    sizes = (mesh.shape["rows"] // (2 * nx), nx, nx)

    def on_device(a, b, v, d, r):
        hbm = lambda value: pltpu.with_memory_space_constraint(value, pltpu.HBM)
        a, b, vt, dt, rt = hbm(a), hbm(b), hbm(v.T), hbm(d.T), hbm(r.reshape(1, -1))
        red = reduce_all(sizes, a, b, vt, dt, rt)
        up, new_a, new_b = finish(red, a, b, vt, dt)
        return up.reshape(-1), new_a, new_b

    spread = P(("rows", "sub"))
    wide = P(("rows", "sub"), None)
    return jax.shard_map(
        on_device, mesh=mesh, in_specs=(wide,) * 4 + (spread,), out_specs=(spread, wide, wide), check_vma=False
    )
```

```python
import functools

import jax
import jax.numpy as jnp
from jax import lax
from jax.experimental import pallas as pl
from jax.experimental.pallas import tpu as pltpu
from jax.sharding import PartitionSpec as P

MESH = pl.DeviceIdType.MESH
LANES = 128
PACK = 704
BLOCK = 32
NEXT = 4

NN = (((1,), (0,)), ((), ()))
NT = (((1,), (1,)), ((), ()))
TN = (((0,), (0,)), ((), ()))


def halves(value):
    high = value.astype(jnp.bfloat16)
    return high, (value - high.astype(jnp.float32)).astype(jnp.bfloat16)


def dot(left, right, dims=NN):
    left = left if isinstance(left, tuple) else halves(left)
    right = right if isinstance(right, tuple) else halves(right)

    def one(l, r):
        return lax.dot_general(l, r, dims, preferred_element_type=jnp.float32)

    return one(left[0], right[0]) + (one(left[0], right[1]) + one(left[1], right[0]))


def gram_pair(value, out_ref, base):
    turned = value.T
    whole, first = halves(value), halves(turned[:LANES, :])
    return pack_pair(
        dot(first, tuple(part[:, :LANES] for part in whole)), dot(turned[LANES:, :], whole), out_ref, base
    )


def pack_pair(first, below, out_ref, base):
    row = lax.broadcasted_iota(jnp.int32, (LANES, LANES), 0)
    lane = lax.broadcasted_iota(jnp.int32, (LANES, LANES), 1)
    last = below[:, LANES:]
    out_ref[base:base + LANES, :] = jnp.where(row >= lane, first, last)
    out_ref[base + LANES:base + 2 * LANES, :] = below[:, :LANES]
    return jnp.sum(jnp.where(row == lane, last, 0.0), axis=0, keepdims=True)


def unpack_pair(red_ref, base, diag):
    row = lax.broadcasted_iota(jnp.int32, (LANES, LANES), 0)
    lane = lax.broadcasted_iota(jnp.int32, (LANES, LANES), 1)
    both = red_ref[base:base + LANES, :]
    turned = both.T
    low = red_ref[base + LANES:base + 2 * LANES, :]
    first = jnp.where(row >= lane, both, turned)
    last = jnp.where(row < lane, both, jnp.where(row > lane, turned, diag))
    return jnp.concatenate(
        [jnp.concatenate([first, low.T], axis=1), jnp.concatenate([low, last], axis=1)], axis=0
    )


def fetch(sources, targets, sems):
    copies = [pltpu.make_async_copy(src, dst, sems.at[k]) for k, (src, dst) in enumerate(zip(sources, targets))]
    for copy in copies:
        copy.start()
    return copies


def reduce_kernel(sizes, a_hbm, b_hbm, v_hbm, d_hbm, r_hbm, out_ref, a_ref, b_ref, v_ref, d_ref, r_ref, load_sem,
                  local, pair, half, near, more, mine, far, total, full,
                  hello, pair_sem, near_sem, more_sem, far_sem, back_sem, rest_sem, cross_sem,
                  pair_out, near_out, more_out, far_out, back_out, rest_out, cross_out):
    nz, ny, nx = sizes
    rows = PACK // 2
    plane = ny * nx
    cell = 2 * plane
    steps = nz // 2
    place = lax.axis_index("rows")
    x = lax.axis_index("sub")
    core = lax.rem(place, 2)
    y = lax.rem(place // 2, ny)
    z = place // (2 * ny)
    side, step = lax.rem(z, 2), z // 2
    me = side * plane + y * nx + x
    near_ids = []
    for dz in range(2):
        for dy in range(ny):
            for dx in range(nx):
                if dz or dy or dx:
                    qz, qy, qx = lax.rem(side + dz, 2), lax.rem(y + dy, ny), lax.rem(x + dx, nx)
                    hops = dz + min(dy, ny - dy) + min(dx, nx - dx)
                    dev = (((2 * step + qz) * ny + qy) * 2 + core, qx)
                    near_ids.append((hops, len(near_ids), qz * plane + qy * nx + qx, dev))
    near_ids = sorted(near_ids, key=lambda item: (-item[0], item[1]))
    rings = [[(q, dev) for hops, _, q, dev in near_ids if hops == ring] for ring in range(1, near_ids[0][0] + 1)]
    near_ids = [(hops - 1, q, dev) for hops, _, q, dev in near_ids]
    far_ids = []
    for dz in sorted(range(1, steps), key=lambda d: -min(d, steps - d)):
        qz = lax.rem(step + dz, steps)
        far_ids.append((qz, ((2 * (2 * ny) * qz + 2 * ny * side) + 2 * y + core, x)))
    partner = (place + 1 - 2 * core, x)
    beside = []
    for dz in (1, steps - 1):
        qz = lax.rem(step + dz, steps)
        beside.append(((2 * (2 * ny) * qz + 2 * ny * side) + 2 * y + core, x))
    doubles = [(0, qy, qx) for qy in range(ny) for qx in range(nx) if (qx + qy) % 2 == 0]
    doubles += [(1, qy, qx) for qy in range(ny) for qx in range(nx) if (qx + qy) % 4 == 1]
    even = side == 0
    double = (even & (lax.rem(x + y, 2) == 0)) | ((side == 1) & (lax.rem(x + y, 4) == 1))
    mine_second = jnp.where(even, y * (nx // 2) + x // 2, plane // 2 + y)

    loads = fetch((b_hbm, d_hbm, r_hbm, a_hbm, v_hbm), (b_ref, d_ref, r_ref, a_ref, v_ref), load_sem)
    barrier = pltpu.get_barrier_semaphore()
    for dev in beside:
        pl.semaphore_signal(barrier, inc=1, device_id=dev, device_id_type=MESH)
    for _, _, dev in near_ids:
        pl.semaphore_signal(barrier, inc=1, device_id=dev, device_id_type=MESH)
    pl.semaphore_signal(barrier, inc=1, device_id=partner, device_id_type=MESH)

    cols = v_ref.shape[0]

    def half_a():
        for k in (3, 4):
            loads[k].wait()
        diag = gram_pair(a_ref[...], local, 0)
        v, d = halves(v_ref[...]), halves(d_ref[...])
        va = dot(v, a_ref[...])
        local[256:256 + cols, :] = va[:, :LANES]
        local[256 + cols:320, :] = va[:, LANES:]
        local[320:352, :] = jnp.zeros((32, LANES), jnp.float32)
        local[320:320 + cols, 0:cols] = dot(v, v, NT)
        local[320:320 + cols, 64:64 + cols] = dot(d, d, NT)
        for k in range(4):
            local[320 + k:321 + k, 32:64] = diag[:, 32 * k:32 * k + 32]

    def half_b():
        for k in (0, 2):
            loads[k].wait()
        diag = gram_pair(b_ref[...], local, rows)
        d = d_ref[...]
        last = jnp.broadcast_to(r_ref[...], (8, d.shape[1]))
        db = dot(jnp.concatenate([d, last], axis=0), b_ref[...])
        local[608:648, :] = db[:, :LANES]
        local[648:688, :] = db[:, LANES:]
        local[688:704, :] = jnp.zeros((16, LANES), jnp.float32)
        local[688:689, :] = diag
        local[696:704, 0:cols] = dot(last, d, NT)

    def send(src, dst, out_sem, in_sem, dev):
        pltpu.make_async_remote_copy(
            src_ref=src, dst_ref=dst, send_sem=out_sem, recv_sem=in_sem, device_id=dev, device_id_type=MESH
        ).start()

    def arrived(ref, sem):
        pltpu.make_async_copy(ref, ref, sem).wait()

    def at(start, size=8):
        return pl.ds(pl.multiple_of(start, 8), size)

    def wait_tiles(count, sem):
        arrived(full.at[pl.ds(0, 8 * count)], sem)

    def each_double(action):
        for k, (qz, qy, qx) in enumerate(doubles):

            @pl.when(me != qz * plane + qy * nx + qx)
            def _():
                action(k, (((2 * step + qz) * ny + qy) * 2 + core, qx))

    def tell(level):
        for dev in beside:
            pl.semaphore_signal(hello.at[level], inc=1, device_id=dev, device_id_type=MESH)

    def told(level):
        pl.semaphore_wait(hello.at[level], 2)

    others, lines = cell - 1, steps - 1
    single = jnp.logical_not(double)

    @pl.when(core == 0)
    def _():
        loads[1].wait()
        half_b()
        pl.semaphore_wait(barrier, len(beside) + len(near_ids) + 1)
        send(local.at[rows:PACK], pair, pair_out, pair_sem, partner)
        tell(0)
        half_a()

    @pl.when(core == 1)
    def _():
        loads[1].wait()
        half_a()
        pl.semaphore_wait(barrier, len(beside) + len(near_ids) + 1)
        send(local.at[0:rows], pair, pair_out, pair_sem, partner)
        tell(0)
        half_b()

    arrived(pair, pair_sem)
    half[...] = local[at(core * rows, rows), :] + pair[...]

    for _, q, dev in near_ids:
        send(half.at[at(8 * q)], near.at[me], near_out, near_sem, dev)
    each_double(lambda k, dev: send(half.at[pl.ds(8 * (cell + k), 8)], more.at[me], more_out, more_sem, dev))
    for level in range(steps // 2 - 1):
        told(level)
        if level < steps // 2 - 2:
            tell(level + 1)
    arrived(pair, pair_out)
    near[me] = half[at(8 * me), :]
    wait_tiles(others, near_sem)
    mine[0:8, :] = jnp.sum(near[...], axis=0)

    @pl.when(single)
    def _():
        for q, dev in far_ids:
            send(mine.at[0:8], far.at[step, 0:8], far_out, far_sem, dev)
        far[step, 0:8] = mine[0:8, :]
        wait_tiles(others, near_out)
        wait_tiles(len(doubles), more_out)
        wait_tiles(lines, far_sem)
        total[0:8, :] = jnp.sum(far[:, 0:8, :], axis=0)

    @pl.when(double)
    def _():
        more[me] = half[at(8 * (cell + mine_second)), :]
        wait_tiles(others, more_sem)
        mine[8:16, :] = jnp.sum(more[...], axis=0)
        for q, dev in far_ids:
            send(mine, far.at[step], far_out, far_sem, dev)
        far[step] = mine[...]
        wait_tiles(others, near_out)
        wait_tiles(len(doubles) - 1, more_out)
        wait_tiles(2 * lines, far_sem)
        total[...] = jnp.sum(far[...], axis=0)

    base = core * rows
    for ring, q, dev in near_ids:
        send(total.at[0:8], full.at[at(base + 8 * me)], back_out, back_sem.at[ring], dev)
    send(total.at[0:8], full.at[at(base + 8 * me)], cross_out, cross_sem, partner)
    full[at(base + 8 * me), :] = total[0:8, :]

    @pl.when(double)
    def _():
        spot = base + 8 * (cell + mine_second)
        for _, q, dev in near_ids:
            send(total.at[8:16], full.at[at(spot)], rest_out, rest_sem, dev)
        send(total.at[8:16], full.at[at(spot)], cross_out, cross_sem, partner)
        full[at(spot), :] = total[8:16, :]
        wait_tiles(2 * lines, far_out)

    @pl.when(single)
    def _():
        wait_tiles(lines, far_out)

    for ring, members in enumerate(rings):
        wait_tiles(len(members), back_sem.at[ring])
        for q, dev in members:
            tile = full.at[at(base + 8 * q)]
            send(tile, tile, cross_out, cross_sem, partner)

    @pl.when(single)
    def _():
        wait_tiles(len(doubles), rest_sem)

    @pl.when(double)
    def _():
        wait_tiles(len(doubles) - 1, rest_sem)

    def forward(k, dev):
        tile = full.at[at(base + 8 * (cell + k))]
        send(tile, tile, cross_out, cross_sem, partner)

    each_double(forward)
    wait_tiles(others, back_out)

    @pl.when(double)
    def _():
        wait_tiles(others, rest_out)

    arrived(full.at[at((1 - core) * rows, rows)], cross_sem)
    arrived(full.at[at(base, rows)], cross_out)
    out_ref[...] = full[...]


def reduce_all(sizes, a, b, v, d, r):
    nz, ny, nx = sizes
    cell, steps = 2 * ny * nx, nz // 2
    rows = PACK // 2
    twice = rows // 8 - cell
    vmem = pl.BlockSpec(memory_space=pltpu.VMEM)
    dma = pltpu.SemaphoreType.DMA
    return pl.pallas_call(
        functools.partial(reduce_kernel, sizes),
        out_shape=jax.ShapeDtypeStruct((PACK, LANES), jnp.float32),
        in_specs=[pl.BlockSpec(memory_space=pltpu.HBM)] * 5,
        out_specs=vmem,
        scratch_shapes=[
            *(pltpu.VMEM(value.shape, jnp.float32) for value in (a, b, v, d, r)),
            dma((5,)),
            pltpu.VMEM((PACK, LANES), jnp.float32),
            pltpu.VMEM((rows, LANES), jnp.float32),
            pltpu.VMEM((rows, LANES), jnp.float32),
            pltpu.VMEM((cell, 8, LANES), jnp.float32),
            pltpu.VMEM((cell, 8, LANES), jnp.float32),
            pltpu.VMEM((16, LANES), jnp.float32),
            pltpu.VMEM((steps, 16, LANES), jnp.float32),
            pltpu.VMEM((16, LANES), jnp.float32),
            pltpu.VMEM((PACK, LANES), jnp.float32),
            pltpu.SemaphoreType.REGULAR((steps // 2 - 1,)),
            dma(()), dma(()), dma(()), dma(()), dma((8,)), dma(()), dma(()),
            *(dma(()) for _ in range(7)),
        ],
        compiler_params=pltpu.CompilerParams(collective_id=0, has_side_effects=True, vmem_limit_bytes=32 << 20),
    )(a, b, v, d, r)


def eliminate(tile, offset, carried, spread):
    groups = BLOCK // 8
    sub = lax.broadcasted_iota(jnp.int32, (8, LANES), 0)
    columns = [
        {
            i: jnp.broadcast_to(tile[8 * i:8 * i + 8, offset + j:offset + j + 1], (8, LANES))
            for i in range(j // 8, groups)
        }
        for j in range(BLOCK)
    ]
    carried = [[part[8 * i:8 * i + 8, :] for i in range(groups)] for part in carried]
    for j in range(BLOCK):
        g, r = j // 8, j % 8
        scale = lax.rsqrt(columns[j][g][r:r + 1, :])
        column = {i: columns[j][i] * scale for i in range(g, groups)}
        for i in range(g, groups):
            spread[j, 8 * i:8 * i + 8, :] = column[i]
        for b in range(j + 1, BLOCK):
            if b < j + NEXT:
                factor = column[b // 8][b % 8:b % 8 + 1, :]
            else:
                factor = spread[j, b:b + 1, :]
            for i in range(b // 8, groups):
                columns[b][i] = columns[b][i] - column[i] * factor
        below = jnp.where(sub > r, column[g], 0.0)
        for out in carried:
            pivot = out[g][r:r + 1, :] * scale
            out[g] = jnp.where(sub == r, pivot, out[g] - below * pivot)
            for i in range(g + 1, groups):
                out[i] = out[i] - column[i] * pivot
    return [jnp.concatenate(out, axis=0) for out in carried]


def identity_at(offset):
    row = lax.broadcasted_iota(jnp.int32, (BLOCK, LANES), 0)
    lane = lax.broadcasted_iota(jnp.int32, (BLOCK, LANES), 1)
    return jnp.where(lane == row + offset, 1.0, 0.0)


def largest(values):
    return jnp.max(jnp.max(values, axis=1, keepdims=True), axis=0, keepdims=True)


def diagonal(matrix):
    row = lax.broadcasted_iota(jnp.int32, matrix.shape, 0)
    lane = lax.broadcasted_iota(jnp.int32, matrix.shape, 1)
    return jnp.where(row == lane, matrix, 0.0)


def chain_kernel(red_ref, a_hbm, b_hbm, v_hbm, d_hbm, up_ref, na_ref, nb_ref, a_ref, b_ref, v_ref, d_ref, load_sem, z_ref, y_ref, x_ref, spread):
    loads = fetch((a_hbm, b_hbm, v_hbm, d_hbm), (a_ref, b_ref, v_ref, d_ref), load_sem)
    rows, width = a_ref.shape
    cols = v_ref.shape[0]
    small = red_ref[320:352, :]
    va = jnp.concatenate([red_ref[256:256 + cols, :], red_ref[256 + cols:320, :]], axis=1)
    db = jnp.concatenate([red_ref[608:648, :], red_ref[648:688, :]], axis=1)
    proj_t, proj_r = db[:cols, :], db[cols:cols + 8, :]
    solved = eliminate(small[:cols, :], 64, [identity_at(0), proj_t[:, :LANES], proj_t[:, LANES:]], spread)
    low = solved[0][:, :cols]
    low_t, low = halves(low.T), halves(low)
    half = jnp.concatenate(solved[1:], axis=1)
    half_t, half = halves(half.T), halves(half)
    vv = small[:cols, :cols]
    gram_r = red_ref[696:704, :cols]
    diag_a = jnp.concatenate([small[k:k + 1, 32:64] for k in range(4)], axis=1)
    gram_a = unpack_pair(red_ref, 0, diag_a)
    gram_b = unpack_pair(red_ref, 352, red_ref[688:689, :])
    scale_a = 1.0 / jnp.maximum(largest(diagonal(gram_a)), largest(diagonal(vv)))
    scale_b = 1.0 / largest(diagonal(gram_b))
    gram_a = halves(gram_a * scale_a)
    va = va * scale_a
    vv = halves(vv * scale_a)
    av, va = halves(va.T), halves(va)

    s = halves((gram_b - dot(half_t, half)) * scale_b)
    w = dot(low_t, half)
    ws = halves(w * scale_b)
    wst = halves(dot(half_t, low) * scale_b)
    inv_v = halves(dot(low_t, low))
    k1 = dot(gram_a, s) + dot(av, ws)
    k1t, k1 = halves(k1.T), halves(k1)
    k2 = dot(va, s) + dot(vv, ws)
    k2t = halves(dot(s, av) + dot(wst, vv))
    j1 = halves(dot(s, k1))
    c = dot(inv_v, k2)
    cs = halves(c * scale_b)

    def rows_of(pair, start, stop):
        return tuple(part[start:stop, :] for part in pair)

    def lanes_of(pair, start):
        return tuple(part[:, start:start + LANES] for part in pair)

    z_ref[:LANES, :] = dot(rows_of(k1t, 0, LANES), j1) + dot(rows_of(k2t, 0, LANES), cs)
    z_ref[LANES:, LANES:] = dot(rows_of(k1t, LANES, width), lanes_of(j1, LANES)) + dot(
        rows_of(k2t, LANES, width), lanes_of(cs, LANES)
    )
    row = lax.broadcasted_iota(jnp.int32, (width, width), 0)
    column = lax.broadcasted_iota(jnp.int32, (width, width), 1)
    y_ref[...] = jnp.where(row == column, 1.0, 0.0)
    lane = lax.broadcasted_iota(jnp.int32, (BLOCK, LANES), 1)
    root = jnp.sqrt(scale_b)
    fronts = []

    for lo in range(0, width, BLOCK):
        hi = lo + BLOCK
        base = lo // LANES * LANES
        own = slice(base, base + LANES)
        offset = lo - base
        block = z_ref[lo:hi, own]
        inside = (lane >= offset) & (lane < offset + BLOCK)
        carried = [jnp.where(inside, identity_at(offset), block)]
        rest = [z_ref[lo:hi, start:start + LANES] for start in range(base + LANES, width, LANES)]
        if hi % LANES == 0:
            carried += rest
        carried = eliminate(block, offset, carried, spread)
        inv = halves(jnp.where(inside, carried[0], 0.0))
        if hi % LANES:
            narrow = halves(pltpu.roll(jnp.where(inside, carried[0], 0.0), (LANES - offset) % LANES, 1)[:, :BLOCK])
            carried += [dot(narrow, part) for part in rest]
        right = {start: halves(part) for start, part in zip(range(base, width, LANES), carried) if start + LANES > hi}
        left = {start: halves(part.T) for start, part in zip(range(base, width, LANES), carried) if start + LANES > hi}
        if hi < width:
            first = hi // LANES * LANES
            near = rows_of(left[first], hi - first, hi - first + BLOCK)
            for start in right:
                tile = slice(start, start + LANES)
                z_ref[hi:hi + BLOCK, tile] = z_ref[hi:hi + BLOCK, tile] - dot(near, right[start])
        solved = dot(inv, y_ref[own, :base + LANES])
        x_ref[lo:hi, :base + LANES] = solved
        if base + LANES < width:
            x_ref[lo:hi, base + LANES:] = jnp.zeros((BLOCK, width - base - LANES), jnp.float32)
        solved = halves(solved)
        for start in right:
            top = max(hi, start)
            part = rows_of(left[start], top - start, LANES)
            y_ref[top:start + LANES, :base + LANES] = y_ref[top:start + LANES, :base + LANES] - dot(part, solved)
            top = max(hi + BLOCK, start)
            if top < start + LANES:
                part = rows_of(left[start], top - start, LANES)
                for other in right:
                    if other >= start:
                        tile = slice(other, other + LANES)
                        z_ref[top:start + LANES, tile] = z_ref[top:start + LANES, tile] - dot(part, right[other])

        if lo == 0:
            for copy in loads:
                copy.wait()
            coeffs = -dot(gram_r, inv_v)
            lead = -proj_r - dot(coeffs, proj_t)
            a = halves(a_ref[...])
            up = dot(lead, a, NT) + dot(coeffs, v_ref[...])
            up_ref[...] = up[:1, :]
            fronts.append(halves((dot(a, j1) + dot(v_ref[...].T, cs)) / root))
        if lo == BLOCK:
            d = halves(d_ref[...].T)
            fronts.append(halves((dot(b_ref[...] - dot(d, w), k1) + dot(d, c)) * root))
        if hi % LANES == 0:
            back = halves(x_ref[own, :])
            na_ref[:, own] = dot(fronts[0], back, NT)
            nb_ref[:, own] = dot(fronts[1], back, NT)


def finish(red, a, b, v, d):
    vmem = pl.BlockSpec(memory_space=pltpu.VMEM)
    rows, width = a.shape
    return pl.pallas_call(
        chain_kernel,
        out_shape=(
            jax.ShapeDtypeStruct((1, rows), jnp.float32),
            jax.ShapeDtypeStruct((rows, width), jnp.float32),
            jax.ShapeDtypeStruct((rows, width), jnp.float32),
        ),
        in_specs=[vmem] + [pl.BlockSpec(memory_space=pltpu.HBM)] * 4,
        out_specs=(vmem,) * 3,
        scratch_shapes=[
            *(pltpu.VMEM(value.shape, jnp.float32) for value in (a, b, v, d)),
            pltpu.SemaphoreType.DMA((4,)),
            pltpu.VMEM((width, width), jnp.float32), pltpu.VMEM((width, width), jnp.float32),
            pltpu.VMEM((width, width), jnp.float32), pltpu.VMEM((BLOCK, BLOCK, LANES), jnp.float32)],
        compiler_params=pltpu.CompilerParams(vmem_limit_bytes=32 << 20),
    )(red, a, b, v, d)


def solution(mesh):
    nx = mesh.shape["sub"]
    sizes = (mesh.shape["rows"] // (2 * nx), nx, nx)

    def on_device(a, b, v, d, r):
        hbm = lambda value: pltpu.with_memory_space_constraint(value, pltpu.HBM)
        a, b, vt, dt, rt = hbm(a), hbm(b), hbm(v.T), hbm(d.T), hbm(r.reshape(1, -1))
        red = reduce_all(sizes, a, b, vt, dt, rt)
        up, new_a, new_b = finish(red, a, b, vt, dt)
        return up.reshape(-1), new_a, new_b

    spread = P(("rows", "sub"))
    wide = P(("rows", "sub"), None)
    return jax.shard_map(
        on_device, mesh=mesh, in_specs=(wide,) * 4 + (spread,), out_specs=(spread, wide, wide), check_vma=False
    )
```

```python
import functools

import jax
import jax.numpy as jnp
from jax import lax
from jax.experimental import pallas as pl
from jax.experimental.pallas import tpu as pltpu
from jax.sharding import PartitionSpec as P

MESH = pl.DeviceIdType.MESH
LANES = 128
PACK = 704
BLOCK = 32
NEXT = 2

NN = (((1,), (0,)), ((), ()))
NT = (((1,), (1,)), ((), ()))
TN = (((0,), (0,)), ((), ()))


def halves(value):
    high = value.astype(jnp.bfloat16)
    return high, (value - high.astype(jnp.float32)).astype(jnp.bfloat16)


def dot(left, right, dims=NN):
    left = left if isinstance(left, tuple) else halves(left)
    right = right if isinstance(right, tuple) else halves(right)

    def one(l, r):
        return lax.dot_general(l, r, dims, preferred_element_type=jnp.float32)

    return one(left[0], right[0]) + (one(left[0], right[1]) + one(left[1], right[0]))


def gram_pair(value, out_ref, base):
    turned = value.T
    whole, first = halves(value), halves(turned[:LANES, :])
    return pack_pair(
        dot(first, tuple(part[:, :LANES] for part in whole)), dot(turned[LANES:, :], whole), out_ref, base
    )


def pack_pair(first, below, out_ref, base):
    row = lax.broadcasted_iota(jnp.int32, (LANES, LANES), 0)
    lane = lax.broadcasted_iota(jnp.int32, (LANES, LANES), 1)
    last = below[:, LANES:]
    out_ref[base:base + LANES, :] = jnp.where(row >= lane, first, last)
    out_ref[base + LANES:base + 2 * LANES, :] = below[:, :LANES]
    return jnp.sum(jnp.where(row == lane, last, 0.0), axis=0, keepdims=True)


def unpack_pair(red_ref, base, diag):
    row = lax.broadcasted_iota(jnp.int32, (LANES, LANES), 0)
    lane = lax.broadcasted_iota(jnp.int32, (LANES, LANES), 1)
    both = red_ref[base:base + LANES, :]
    turned = both.T
    low = red_ref[base + LANES:base + 2 * LANES, :]
    first = jnp.where(row >= lane, both, turned)
    last = jnp.where(row < lane, both, jnp.where(row > lane, turned, diag))
    return jnp.concatenate(
        [jnp.concatenate([first, low.T], axis=1), jnp.concatenate([low, last], axis=1)], axis=0
    )


def fetch(sources, targets, sems):
    copies = [pltpu.make_async_copy(src, dst, sems.at[k]) for k, (src, dst) in enumerate(zip(sources, targets))]
    for copy in copies:
        copy.start()
    return copies


def reduce_kernel(sizes, a_hbm, b_hbm, v_hbm, d_hbm, r_hbm, out_ref, a_ref, b_ref, v_ref, d_ref, r_ref, load_sem,
                  local, pair, half, near, more, mine, far, total, full,
                  hello, pair_sem, near_sem, more_sem, far_sem, back_sem, rest_sem, cross_sem,
                  pair_out, near_out, more_out, far_out, back_out, rest_out, cross_out):
    nz, ny, nx = sizes
    rows = PACK // 2
    plane = ny * nx
    cell = 2 * plane
    steps = nz // 2
    place = lax.axis_index("rows")
    x = lax.axis_index("sub")
    core = lax.rem(place, 2)
    y = lax.rem(place // 2, ny)
    z = place // (2 * ny)
    side, step = lax.rem(z, 2), z // 2
    me = side * plane + y * nx + x
    near_ids = []
    for dz in range(2):
        for dy in range(ny):
            for dx in range(nx):
                if dz or dy or dx:
                    qz, qy, qx = lax.rem(side + dz, 2), lax.rem(y + dy, ny), lax.rem(x + dx, nx)
                    hops = dz + min(dy, ny - dy) + min(dx, nx - dx)
                    dev = (((2 * step + qz) * ny + qy) * 2 + core, qx)
                    near_ids.append((hops, len(near_ids), qz * plane + qy * nx + qx, dev))
    near_ids = sorted(near_ids, key=lambda item: (-item[0], item[1]))
    rings = [[(q, dev) for hops, _, q, dev in near_ids if hops == ring] for ring in range(1, near_ids[0][0] + 1)]
    near_ids = [(hops - 1, q, dev) for hops, _, q, dev in near_ids]
    far_ids = []
    for dz in sorted(range(1, steps), key=lambda d: -min(d, steps - d)):
        qz = lax.rem(step + dz, steps)
        far_ids.append((qz, ((2 * (2 * ny) * qz + 2 * ny * side) + 2 * y + core, x)))
    partner = (place + 1 - 2 * core, x)
    beside = []
    for dz in (1, steps - 1):
        qz = lax.rem(step + dz, steps)
        beside.append(((2 * (2 * ny) * qz + 2 * ny * side) + 2 * y + core, x))
    doubles = [(0, qy, qx) for qy in range(ny) for qx in range(nx) if (qx + qy) % 2 == 0]
    doubles += [(1, qy, qx) for qy in range(ny) for qx in range(nx) if (qx + qy) % 4 == 1]
    even = side == 0
    double = (even & (lax.rem(x + y, 2) == 0)) | ((side == 1) & (lax.rem(x + y, 4) == 1))
    mine_second = jnp.where(even, y * (nx // 2) + x // 2, plane // 2 + y)

    loads = fetch((b_hbm, d_hbm, r_hbm, a_hbm, v_hbm), (b_ref, d_ref, r_ref, a_ref, v_ref), load_sem)
    barrier = pltpu.get_barrier_semaphore()
    for dev in beside:
        pl.semaphore_signal(barrier, inc=1, device_id=dev, device_id_type=MESH)
    for _, _, dev in near_ids:
        pl.semaphore_signal(barrier, inc=1, device_id=dev, device_id_type=MESH)
    pl.semaphore_signal(barrier, inc=1, device_id=partner, device_id_type=MESH)

    cols = v_ref.shape[0]

    def half_a():
        for k in (3, 4):
            loads[k].wait()
        diag = gram_pair(a_ref[...], local, 0)
        v, d = halves(v_ref[...]), halves(d_ref[...])
        va = dot(v, a_ref[...])
        local[256:256 + cols, :] = va[:, :LANES]
        local[256 + cols:320, :] = va[:, LANES:]
        local[320:352, :] = jnp.zeros((32, LANES), jnp.float32)
        local[320:320 + cols, 0:cols] = dot(v, v, NT)
        local[320:320 + cols, 64:64 + cols] = dot(d, d, NT)
        for k in range(4):
            local[320 + k:321 + k, 32:64] = diag[:, 32 * k:32 * k + 32]

    def half_b():
        for k in (0, 2):
            loads[k].wait()
        diag = gram_pair(b_ref[...], local, rows)
        d = d_ref[...]
        last = jnp.broadcast_to(r_ref[...], (8, d.shape[1]))
        db = dot(jnp.concatenate([d, last], axis=0), b_ref[...])
        local[608:648, :] = db[:, :LANES]
        local[648:688, :] = db[:, LANES:]
        local[688:704, :] = jnp.zeros((16, LANES), jnp.float32)
        local[688:689, :] = diag
        local[696:704, 0:cols] = dot(last, d, NT)

    def send(src, dst, out_sem, in_sem, dev):
        pltpu.make_async_remote_copy(
            src_ref=src, dst_ref=dst, send_sem=out_sem, recv_sem=in_sem, device_id=dev, device_id_type=MESH
        ).start()

    def arrived(ref, sem):
        pltpu.make_async_copy(ref, ref, sem).wait()

    def at(start, size=8):
        return pl.ds(pl.multiple_of(start, 8), size)

    def wait_tiles(count, sem):
        arrived(full.at[pl.ds(0, 8 * count)], sem)

    def each_double(action):
        for k, (qz, qy, qx) in enumerate(doubles):

            @pl.when(me != qz * plane + qy * nx + qx)
            def _():
                action(k, (((2 * step + qz) * ny + qy) * 2 + core, qx))

    def tell(level):
        for dev in beside:
            pl.semaphore_signal(hello.at[level], inc=1, device_id=dev, device_id_type=MESH)

    def told(level):
        pl.semaphore_wait(hello.at[level], 2)

    others, lines = cell - 1, steps - 1
    single = jnp.logical_not(double)

    @pl.when(core == 0)
    def _():
        loads[1].wait()
        half_b()
        pl.semaphore_wait(barrier, len(beside) + len(near_ids) + 1)
        send(local.at[rows:PACK], pair, pair_out, pair_sem, partner)
        tell(0)
        half_a()

    @pl.when(core == 1)
    def _():
        loads[1].wait()
        half_a()
        pl.semaphore_wait(barrier, len(beside) + len(near_ids) + 1)
        send(local.at[0:rows], pair, pair_out, pair_sem, partner)
        tell(0)
        half_b()

    arrived(pair, pair_sem)
    half[...] = local[at(core * rows, rows), :] + pair[...]

    for _, q, dev in near_ids:
        send(half.at[at(8 * q)], near.at[me], near_out, near_sem, dev)
    each_double(lambda k, dev: send(half.at[pl.ds(8 * (cell + k), 8)], more.at[me], more_out, more_sem, dev))
    for level in range(steps // 2 - 1):
        told(level)
        if level < steps // 2 - 2:
            tell(level + 1)
    arrived(pair, pair_out)
    near[me] = half[at(8 * me), :]
    wait_tiles(others, near_sem)
    mine[0:8, :] = jnp.sum(near[...], axis=0)

    @pl.when(single)
    def _():
        for q, dev in far_ids:
            send(mine.at[0:8], far.at[step, 0:8], far_out, far_sem, dev)
        far[step, 0:8] = mine[0:8, :]
        wait_tiles(others, near_out)
        wait_tiles(len(doubles), more_out)
        wait_tiles(lines, far_sem)
        total[0:8, :] = jnp.sum(far[:, 0:8, :], axis=0)

    @pl.when(double)
    def _():
        more[me] = half[at(8 * (cell + mine_second)), :]
        wait_tiles(others, more_sem)
        mine[8:16, :] = jnp.sum(more[...], axis=0)
        for q, dev in far_ids:
            send(mine, far.at[step], far_out, far_sem, dev)
        far[step] = mine[...]
        wait_tiles(others, near_out)
        wait_tiles(len(doubles) - 1, more_out)
        wait_tiles(2 * lines, far_sem)
        total[...] = jnp.sum(far[...], axis=0)

    base = core * rows
    for ring, q, dev in near_ids:
        send(total.at[0:8], full.at[at(base + 8 * me)], back_out, back_sem.at[ring], dev)
    send(total.at[0:8], full.at[at(base + 8 * me)], cross_out, cross_sem, partner)
    full[at(base + 8 * me), :] = total[0:8, :]

    @pl.when(double)
    def _():
        spot = base + 8 * (cell + mine_second)
        for _, q, dev in near_ids:
            send(total.at[8:16], full.at[at(spot)], rest_out, rest_sem, dev)
        send(total.at[8:16], full.at[at(spot)], cross_out, cross_sem, partner)
        full[at(spot), :] = total[8:16, :]
        wait_tiles(2 * lines, far_out)

    @pl.when(single)
    def _():
        wait_tiles(lines, far_out)

    for ring, members in enumerate(rings):
        wait_tiles(len(members), back_sem.at[ring])
        for q, dev in members:
            tile = full.at[at(base + 8 * q)]
            send(tile, tile, cross_out, cross_sem, partner)

    @pl.when(single)
    def _():
        wait_tiles(len(doubles), rest_sem)

    @pl.when(double)
    def _():
        wait_tiles(len(doubles) - 1, rest_sem)

    def forward(k, dev):
        tile = full.at[at(base + 8 * (cell + k))]
        send(tile, tile, cross_out, cross_sem, partner)

    each_double(forward)
    wait_tiles(others, back_out)

    @pl.when(double)
    def _():
        wait_tiles(others, rest_out)

    arrived(full.at[at((1 - core) * rows, rows)], cross_sem)
    arrived(full.at[at(base, rows)], cross_out)
    out_ref[...] = full[...]


def reduce_all(sizes, a, b, v, d, r):
    nz, ny, nx = sizes
    cell, steps = 2 * ny * nx, nz // 2
    rows = PACK // 2
    twice = rows // 8 - cell
    vmem = pl.BlockSpec(memory_space=pltpu.VMEM)
    dma = pltpu.SemaphoreType.DMA
    return pl.pallas_call(
        functools.partial(reduce_kernel, sizes),
        out_shape=jax.ShapeDtypeStruct((PACK, LANES), jnp.float32),
        in_specs=[pl.BlockSpec(memory_space=pltpu.HBM)] * 5,
        out_specs=vmem,
        scratch_shapes=[
            *(pltpu.VMEM(value.shape, jnp.float32) for value in (a, b, v, d, r)),
            dma((5,)),
            pltpu.VMEM((PACK, LANES), jnp.float32),
            pltpu.VMEM((rows, LANES), jnp.float32),
            pltpu.VMEM((rows, LANES), jnp.float32),
            pltpu.VMEM((cell, 8, LANES), jnp.float32),
            pltpu.VMEM((cell, 8, LANES), jnp.float32),
            pltpu.VMEM((16, LANES), jnp.float32),
            pltpu.VMEM((steps, 16, LANES), jnp.float32),
            pltpu.VMEM((16, LANES), jnp.float32),
            pltpu.VMEM((PACK, LANES), jnp.float32),
            pltpu.SemaphoreType.REGULAR((steps // 2 - 1,)),
            dma(()), dma(()), dma(()), dma(()), dma((8,)), dma(()), dma(()),
            *(dma(()) for _ in range(7)),
        ],
        compiler_params=pltpu.CompilerParams(collective_id=0, has_side_effects=True, vmem_limit_bytes=32 << 20),
    )(a, b, v, d, r)


def eliminate(tile, offset, carried, spread):
    groups = BLOCK // 8
    sub = lax.broadcasted_iota(jnp.int32, (8, LANES), 0)
    columns = [
        {
            i: jnp.broadcast_to(tile[8 * i:8 * i + 8, offset + j:offset + j + 1], (8, LANES))
            for i in range(j // 8, groups)
        }
        for j in range(BLOCK)
    ]
    carried = [[part[8 * i:8 * i + 8, :] for i in range(groups)] for part in carried]
    for j in range(BLOCK):
        g, r = j // 8, j % 8
        scale = lax.rsqrt(jnp.broadcast_to(columns[j][g][r:r + 1, :], (8, LANES)))
        column = {i: columns[j][i] * scale for i in range(g, groups)}
        for i in range(g, groups):
            spread[j, 8 * i:8 * i + 8, :] = column[i]
        for b in range(j + 1, BLOCK):
            if b < j + NEXT:
                factor = jnp.broadcast_to(columns[j][b // 8][b % 8:b % 8 + 1, :], (8, LANES)) * scale
            else:
                factor = spread[j, b:b + 1, :]
            for i in range(b // 8, groups):
                columns[b][i] = columns[b][i] - column[i] * factor
        below = jnp.where(sub > r, column[g], 0.0)
        for out in carried:
            pivot = jnp.broadcast_to(out[g][r:r + 1, :], (8, LANES)) * scale
            out[g] = jnp.where(sub == r, pivot, out[g] - below * pivot)
            for i in range(g + 1, groups):
                out[i] = out[i] - column[i] * pivot
    return [jnp.concatenate(out, axis=0) for out in carried]


def identity_at(offset):
    row = lax.broadcasted_iota(jnp.int32, (BLOCK, LANES), 0)
    lane = lax.broadcasted_iota(jnp.int32, (BLOCK, LANES), 1)
    return jnp.where(lane == row + offset, 1.0, 0.0)


def largest(values):
    return jnp.max(jnp.max(values, axis=1, keepdims=True), axis=0, keepdims=True)


def diagonal(matrix):
    row = lax.broadcasted_iota(jnp.int32, matrix.shape, 0)
    lane = lax.broadcasted_iota(jnp.int32, matrix.shape, 1)
    return jnp.where(row == lane, matrix, 0.0)


def chain_kernel(red_ref, a_hbm, b_hbm, v_hbm, d_hbm, up_ref, na_ref, nb_ref, a_ref, b_ref, v_ref, d_ref, load_sem, z_ref, y_ref, x_ref, spread):
    loads = fetch((a_hbm, b_hbm, v_hbm, d_hbm), (a_ref, b_ref, v_ref, d_ref), load_sem)
    rows, width = a_ref.shape
    cols = v_ref.shape[0]
    small = red_ref[320:352, :]
    va = jnp.concatenate([red_ref[256:256 + cols, :], red_ref[256 + cols:320, :]], axis=1)
    db = jnp.concatenate([red_ref[608:648, :], red_ref[648:688, :]], axis=1)
    proj_t, proj_r = db[:cols, :], db[cols:cols + 8, :]
    solved = eliminate(small[:cols, :], 64, [identity_at(0), proj_t[:, :LANES], proj_t[:, LANES:]], spread)
    low = solved[0][:, :cols]
    low_t, low = halves(low.T), halves(low)
    half = jnp.concatenate(solved[1:], axis=1)
    half_t, half = halves(half.T), halves(half)
    vv = small[:cols, :cols]
    gram_r = red_ref[696:704, :cols]
    diag_a = jnp.concatenate([small[k:k + 1, 32:64] for k in range(4)], axis=1)
    gram_a = unpack_pair(red_ref, 0, diag_a)
    gram_b = unpack_pair(red_ref, 352, red_ref[688:689, :])
    scale_a = 1.0 / jnp.maximum(largest(diagonal(gram_a)), largest(diagonal(vv)))
    scale_b = 1.0 / largest(diagonal(gram_b))
    gram_a = halves(gram_a * scale_a)
    va = va * scale_a
    vv = halves(vv * scale_a)
    av, va = halves(va.T), halves(va)

    s = halves((gram_b - dot(half_t, half)) * scale_b)
    w = dot(low_t, half)
    ws = halves(w * scale_b)
    wst = halves(dot(half_t, low) * scale_b)
    inv_v = halves(dot(low_t, low))
    k1 = dot(gram_a, s) + dot(av, ws)
    k1t, k1 = halves(k1.T), halves(k1)
    k2 = dot(va, s) + dot(vv, ws)
    k2t = halves(dot(s, av) + dot(wst, vv))
    j1 = halves(dot(s, k1))
    c = dot(inv_v, k2)
    cs = halves(c * scale_b)

    def rows_of(pair, start, stop):
        return tuple(part[start:stop, :] for part in pair)

    def lanes_of(pair, start):
        return tuple(part[:, start:start + LANES] for part in pair)

    z_ref[:LANES, :] = dot(rows_of(k1t, 0, LANES), j1) + dot(rows_of(k2t, 0, LANES), cs)
    z_ref[LANES:, LANES:] = dot(rows_of(k1t, LANES, width), lanes_of(j1, LANES)) + dot(
        rows_of(k2t, LANES, width), lanes_of(cs, LANES)
    )
    row = lax.broadcasted_iota(jnp.int32, (width, width), 0)
    column = lax.broadcasted_iota(jnp.int32, (width, width), 1)
    y_ref[...] = jnp.where(row == column, 1.0, 0.0)
    lane = lax.broadcasted_iota(jnp.int32, (BLOCK, LANES), 1)
    root = jnp.sqrt(scale_b)
    fronts = []

    for lo in range(0, width, BLOCK):
        hi = lo + BLOCK
        base = lo // LANES * LANES
        own = slice(base, base + LANES)
        offset = lo - base
        block = z_ref[lo:hi, own]
        inside = (lane >= offset) & (lane < offset + BLOCK)
        carried = [jnp.where(inside, identity_at(offset), block)]
        rest = [z_ref[lo:hi, start:start + LANES] for start in range(base + LANES, width, LANES)]
        if hi % LANES == 0:
            carried += rest
        carried = eliminate(block, offset, carried, spread)
        inv = halves(jnp.where(inside, carried[0], 0.0))
        if hi % LANES:
            narrow = halves(pltpu.roll(jnp.where(inside, carried[0], 0.0), (LANES - offset) % LANES, 1)[:, :BLOCK])
            carried += [dot(narrow, part) for part in rest]
        right = {start: halves(part) for start, part in zip(range(base, width, LANES), carried) if start + LANES > hi}
        left = {start: halves(part.T) for start, part in zip(range(base, width, LANES), carried) if start + LANES > hi}
        if hi < width:
            first = hi // LANES * LANES
            near = rows_of(left[first], hi - first, hi - first + BLOCK)
            for start in right:
                tile = slice(start, start + LANES)
                z_ref[hi:hi + BLOCK, tile] = z_ref[hi:hi + BLOCK, tile] - dot(near, right[start])
        solved = dot(inv, y_ref[own, :base + LANES])
        x_ref[lo:hi, :base + LANES] = solved
        if base + LANES < width:
            x_ref[lo:hi, base + LANES:] = jnp.zeros((BLOCK, width - base - LANES), jnp.float32)
        solved = halves(solved)
        for start in right:
            top = max(hi, start)
            part = rows_of(left[start], top - start, LANES)
            y_ref[top:start + LANES, :base + LANES] = y_ref[top:start + LANES, :base + LANES] - dot(part, solved)
            top = max(hi + BLOCK, start)
            if top < start + LANES:
                part = rows_of(left[start], top - start, LANES)
                for other in right:
                    if other >= start:
                        tile = slice(other, other + LANES)
                        z_ref[top:start + LANES, tile] = z_ref[top:start + LANES, tile] - dot(part, right[other])

        if lo == 0:
            for copy in loads:
                copy.wait()
            coeffs = -dot(gram_r, inv_v)
            lead = -proj_r - dot(coeffs, proj_t)
            a = halves(a_ref[...])
            up = dot(lead, a, NT) + dot(coeffs, v_ref[...])
            up_ref[...] = up[:1, :]
            fronts.append(halves((dot(a, j1) + dot(v_ref[...].T, cs)) / root))
        if lo == BLOCK:
            d = halves(d_ref[...].T)
            fronts.append(halves((dot(b_ref[...] - dot(d, w), k1) + dot(d, c)) * root))
        if hi % LANES == 0:
            back = halves(x_ref[own, :])
            na_ref[:, own] = dot(fronts[0], back, NT)
            nb_ref[:, own] = dot(fronts[1], back, NT)


def finish(red, a, b, v, d):
    vmem = pl.BlockSpec(memory_space=pltpu.VMEM)
    rows, width = a.shape
    return pl.pallas_call(
        chain_kernel,
        out_shape=(
            jax.ShapeDtypeStruct((1, rows), jnp.float32),
            jax.ShapeDtypeStruct((rows, width), jnp.float32),
            jax.ShapeDtypeStruct((rows, width), jnp.float32),
        ),
        in_specs=[vmem] + [pl.BlockSpec(memory_space=pltpu.HBM)] * 4,
        out_specs=(vmem,) * 3,
        scratch_shapes=[
            *(pltpu.VMEM(value.shape, jnp.float32) for value in (a, b, v, d)),
            pltpu.SemaphoreType.DMA((4,)),
            pltpu.VMEM((width, width), jnp.float32), pltpu.VMEM((width, width), jnp.float32),
            pltpu.VMEM((width, width), jnp.float32), pltpu.VMEM((BLOCK, BLOCK, LANES), jnp.float32)],
        compiler_params=pltpu.CompilerParams(vmem_limit_bytes=32 << 20),
    )(red, a, b, v, d)


def solution(mesh):
    nx = mesh.shape["sub"]
    sizes = (mesh.shape["rows"] // (2 * nx), nx, nx)

    def on_device(a, b, v, d, r):
        hbm = lambda value: pltpu.with_memory_space_constraint(value, pltpu.HBM)
        a, b, vt, dt, rt = hbm(a), hbm(b), hbm(v.T), hbm(d.T), hbm(r.reshape(1, -1))
        red = reduce_all(sizes, a, b, vt, dt, rt)
        up, new_a, new_b = finish(red, a, b, vt, dt)
        return up.reshape(-1), new_a, new_b

    spread = P(("rows", "sub"))
    wide = P(("rows", "sub"), None)
    return jax.shard_map(
        on_device, mesh=mesh, in_specs=(wide,) * 4 + (spread,), out_specs=(spread, wide, wide), check_vma=False
    )
```
